256 devices in a mesh: rep: 4 (over y_lo, core), seq: 64 (over x, z, y_hi).
Axes of the slice: x: 4, y: 4 (y_hi: 2, y_lo: 2; y = y_hi * 2 + y_lo), z: 8, core: 2. Of those that a mesh axis runs over, the one named last changes fastest.
Arguments:
- inputs: bfloat16 [4, 8192, 4096], P('rep', 'seq'), may hold values from -8 to 8
- queries: bfloat16 [4, 8192, 2048], P('rep', 'seq'), may hold values from -4.5 to 4.5
- key_heads: bfloat16 [4, 8192, 512], P('rep', 'seq'), may hold values from -4.5 to 4.5
- cotangent: bfloat16 [4, 8192, 2048], P('rep', 'seq'), may hold values from -6 to 6
- value_weight: float32 [4, 4096, 512], P('rep', 'seq'), may hold values from -6 to 6
- random_blocks: int32 [64, 2], replicated, may hold values from 0 to 63, as said below
Outputs:
- input_grad: bfloat16 [4, 8192, 4096], P('rep', 'seq')
- query_gradient: bfloat16 [4, 8192, 2048], P('rep', 'seq')
- key_grad: bfloat16 [4, 8192, 512], P('rep', 'seq')
- new_weight: float32 [4, 4096, 512], P('rep', 'seq')
The draws below stay inside these ranges and needn't reach their ends.
Inputs may be any that keep to these rules, and one draw needn't show every extreme that they name: Device k of seq holds block k; let n = 64. For each slot j there is one offset o_j for all blocks, with o_0 + o_1 = n - 1 and both at least 1, such that random_blocks[i, j] = (i - o_j) mod n.
All inputs are finite; a program needn't handle non-finite values.
Results may differ from the reference program's by a relative error of at most 0.012.
Values may be sent and summed in bfloat16 or wider, within the bound.
A program may use at most 128 MiB of HBM per device.

```python
import jax
import jax.numpy as jnp
from jax import lax

D = 4096
HEADS = 16
KV_HEADS = 4
HD = 128
BLOCK_TOKENS = 128
RAND = 2
STEP = 4
REPLICAS = 4
BPD = 1
NB = 64
LENGTH = 8192
KEY_BLOCK_COUNT = 6
QUERY_WIDTH = 2048
KEY_VALUE_WIDTH = 512


def draw_queries(key, part):
    noise_key = jax.random.fold_in(key, 101)
    shape_full = (REPLICAS, NB, BLOCK_TOKENS, HEADS, HD)
    drawn_values = jnp.clip(jax.random.normal(noise_key, shape_full, jnp.float32), -4.5, 4.5)
    return drawn_values.reshape(REPLICAS, NB * BLOCK_TOKENS, HEADS * HD).astype(jnp.bfloat16)


def draw_key_heads(key, part):
    noise_key = jax.random.fold_in(key, 202)
    shape_full = (REPLICAS, NB, BLOCK_TOKENS, KV_HEADS, HD)
    drawn_values = jnp.clip(jax.random.normal(noise_key, shape_full, jnp.float32), -4.5, 4.5)
    return drawn_values.reshape(REPLICAS, NB * BLOCK_TOKENS, KV_HEADS * HD).astype(jnp.bfloat16)


def draw_random_blocks(key, part):
    seq_devices = NB // BPD
    first_key, shift_key = jax.random.split(jax.random.fold_in(key, 303))
    first_offset = jax.random.randint(first_key, (), 1, seq_devices - 1)
    offsets = jnp.stack([first_offset, seq_devices - 1 - first_offset])
    rotations = jax.random.randint(shift_key, (seq_devices, RAND), 0, BPD)
    block_ids = jnp.arange(NB, dtype=jnp.int32)
    device_ids = block_ids // BPD
    sources = (device_ids[:, None] - offsets[None, :]) % seq_devices
    within = (block_ids[:, None] % BPD + rotations[device_ids]) % BPD
    return (sources * BPD + within).astype(jnp.int32)


def raised(drawn, rng, source, target, shards_of, factor):
    owner, partner = [(jnp.arange(drawn.shape[position]) // (drawn.shape[position] // shards_of)).reshape([-1 if axis == position else 1 for axis in range(drawn.ndim)]) for position in (source, target)]
    chosen = jax.random.permutation(rng, shards_of)[partner]
    strong = (owner == chosen) | (owner == (partner + shards_of // 2) % shards_of)
    return jnp.where(strong, factor * drawn, drawn)


def block_scale(own_key, extent, cuts, low, top_value):
    factor_of = 1.0
    for position, shards_of in cuts:
        draws = jax.random.uniform(jax.random.fold_in(jax.random.fold_in(own_key, 6), position), (shards_of,), jnp.float32, low / len(cuts), top_value / len(cuts))
        factor_of = factor_of * jnp.repeat(jnp.exp(draws), extent[position] // shards_of).reshape((-1,) + (1,) * (len(extent) - 1 - position))
    return factor_of


def bell_draw(key, dims, width, bound, pieces=(), kind=jnp.bfloat16):
    drawn = width * jax.random.normal(key, dims, jnp.float32)
    if pieces:
        drawn = drawn * block_scale(key, dims, pieces, -0.22, 0.18)
    return jnp.clip(drawn, -bound, bound).astype(kind)


def gaussian_with(key, dims, width, bound, pieces, heavy, kind=jnp.bfloat16):
    result = width * jax.random.normal(key, dims, jnp.float32)
    if pieces:
        result = result * block_scale(key, dims, pieces, -0.22, 0.18)
    return jnp.clip(raised(result, jax.random.fold_in(key, 3), *heavy), -bound, bound).astype(kind)


def setup_inputs(seed: int = 0) -> dict:
    keys = jax.random.split(jax.random.key(seed), 7)
    inputs = gaussian_with(keys[0], (REPLICAS, LENGTH, D), 1.0, 8.0, ((0, 4), (1, 64)), (1, 2, 64, 4.0))
    queries = draw_queries(jax.random.fold_in(keys[6], 71), 0)
    key_heads = draw_key_heads(jax.random.fold_in(keys[6], 71), 0)
    cotangent = bell_draw(keys[3], (REPLICAS, LENGTH, QUERY_WIDTH), 1.0, 6.0, ((0, 4), (1, 64)))
    value_weight = bell_draw(keys[4], (REPLICAS, D, KEY_VALUE_WIDTH), 1.0, 6.0, ((0, 4), (1, 64)), jnp.float32)
    random_blocks = draw_random_blocks(jax.random.fold_in(keys[6], 71), 0)
    return {"inputs": inputs, "queries": queries, "key_heads": key_heads, "cotangent": cotangent, "value_weight": value_weight, "random_blocks": random_blocks}


learn_rate = 2.0
masked_score = -1e30


def round_trip(source):
    narrow = lax.optimization_barrier(source.astype(jnp.bfloat16))
    return narrow.astype(jnp.float32)


def block_lists(random_blocks):
    block_ids = jnp.arange(NB, dtype=jnp.int32)
    window = jnp.stack([block_ids - 1, block_ids, block_ids + 1, jnp.zeros_like(block_ids)], axis=1)
    listed = jnp.concatenate([window, random_blocks.astype(jnp.int32)], axis=1)
    present = jnp.concatenate([(block_ids > 0)[:, None], jnp.ones((NB, 1), bool), (block_ids < NB - 1)[:, None], jnp.ones((NB, 1 + RAND), bool)], axis=1)
    return jnp.clip(listed, 0, NB - 1).astype(jnp.int32), present


def replica_pass(tokens, query_rows, key_rows, upstream_rows, weight, listed, present):
    proj_scale = D ** -0.5
    score_factor = HD ** -0.5
    heads_group = HEADS // KV_HEADS
    weight_low = weight.astype(jnp.bfloat16)
    values = (jnp.dot(tokens, weight_low, preferred_element_type=jnp.float32) * proj_scale).astype(jnp.bfloat16)
    key_pairs = jnp.concatenate([key_rows, values], axis=1).reshape(NB, BLOCK_TOKENS, 2 * KEY_VALUE_WIDTH)
    query_blocks = query_rows.reshape(NB, BLOCK_TOKENS, KV_HEADS, heads_group, HD)
    upstream_blocks = upstream_rows.reshape(NB, BLOCK_TOKENS, KV_HEADS, heads_group, HD)
    slot_ids = jnp.arange(KEY_BLOCK_COUNT)
    keep_exact = (slot_ids == 1) | (slot_ids == 3)

    def one_block(running, block_args):
        query_block, upstream_block, block_names, block_ok = block_args
        key_set = key_pairs[block_names].reshape(KEY_BLOCK_COUNT * BLOCK_TOKENS, 2, KV_HEADS, HD).astype(jnp.float32)
        key_portion = key_set[:, 0]
        value_portion = key_set[:, 1]
        query_portion = query_block.astype(jnp.float32)
        upstream_portion = upstream_block.astype(jnp.float32)
        key_mask = jnp.repeat(block_ok, BLOCK_TOKENS)
        score_matrix = jnp.einsum("hukq,auq->ukha", query_portion, key_portion) * score_factor
        score_matrix = jnp.where(key_mask, score_matrix, masked_score)
        highest = jnp.max(score_matrix, axis=-1, keepdims=True)
        exp_scores = jnp.exp(score_matrix - highest)
        soft_weights = exp_scores / jnp.sum(exp_scores, axis=-1, keepdims=True)
        softmax_lowered = round_trip(soft_weights)
        attended_output = jnp.einsum("wjek,kwf->ewjf", softmax_lowered, value_portion)
        row_delta = jnp.sum(upstream_portion * attended_output, axis=-1)
        weight_gradient = jnp.einsum("hukq,auq->ukha", upstream_portion, value_portion)
        score_gradient = round_trip(soft_weights * (weight_gradient - jnp.transpose(row_delta, (1, 2, 0))[..., None]) * score_factor)
        query_gradient = jnp.einsum("wjek,kwf->ewjf", score_gradient, key_portion).astype(jnp.bfloat16).reshape(BLOCK_TOKENS, QUERY_WIDTH)
        key_delta_rows = jnp.einsum("yoji,jyoe->iye", score_gradient, query_portion).reshape(KEY_BLOCK_COUNT, BLOCK_TOKENS, KEY_VALUE_WIDTH)
        value_delta_rows = jnp.einsum("yoji,jyoe->iye", softmax_lowered, upstream_portion).reshape(KEY_BLOCK_COUNT, BLOCK_TOKENS, KEY_VALUE_WIDTH)
        changes = jnp.concatenate([key_delta_rows, value_delta_rows], axis=-1)
        changes = jnp.where(keep_exact[:, None, None], changes, round_trip(changes))
        return running.at[block_names].add(changes), query_gradient

    totals, query_grads = lax.scan(one_block, jnp.zeros((NB, BLOCK_TOKENS, 2 * KEY_VALUE_WIDTH), jnp.float32), (query_blocks, upstream_blocks, listed, present))
    key_grad = totals[..., :KEY_VALUE_WIDTH].reshape(NB * BLOCK_TOKENS, KEY_VALUE_WIDTH).astype(jnp.bfloat16)
    value_total = totals[..., KEY_VALUE_WIDTH:].reshape(NB * BLOCK_TOKENS, KEY_VALUE_WIDTH).astype(jnp.bfloat16)
    input_grad = (jnp.dot(value_total, weight_low.T, preferred_element_type=jnp.float32) * proj_scale).astype(jnp.bfloat16)
    weight_change = jnp.dot(tokens.T, value_total, preferred_element_type=jnp.float32) * proj_scale
    updated = weight - learn_rate * weight_change
    return input_grad, query_grads.reshape(NB * BLOCK_TOKENS, QUERY_WIDTH), key_grad, updated


def reference(inputs, queries, key_heads, cotangent, value_weight, random_blocks):
    listed, present = block_lists(random_blocks)
    outcomes = [replica_pass(inputs[replica], queries[replica], key_heads[replica], cotangent[replica], value_weight[replica], listed, present) for replica in range(REPLICAS)]
    rep_sections = REPLICAS.bit_length() - 1
    peer_hop = 2 ** (STEP % rep_sections)
    updated = jnp.stack([outcome[3] for outcome in outcomes])
    new_weight = 0.5 * (updated + jnp.roll(updated, peer_hop, axis=0))
    input_grad = jnp.stack([outcome[0] for outcome in outcomes])
    query_gradient = jnp.stack([outcome[1] for outcome in outcomes])
    key_grad = jnp.stack([outcome[2] for outcome in outcomes])
    return (input_grad, query_gradient, key_grad, new_weight)
```

```python
import functools
import jax
import jax.numpy as jnp
from jax import lax
from jax.experimental import pallas as pl
from jax.experimental.pallas import tpu as pltpu
from jax.sharding import PartitionSpec as P

HEADS = 16
KV_HEADS = 4
HD = 128
BLOCK_TOKENS = 128
STEP = 4
LEARN_RATE = 2.0
MASKED = -1e30
GROUP = HEADS // KV_HEADS
MESH = pl.DeviceIdType.MESH
F32 = jnp.float32
BF16 = jnp.bfloat16


def grid_of(n):
    return {64: (4, 8), 16: (2, 4), 8: (2, 2)}[n]


class Place:
    def __init__(self, n, send_sem, recv_sem):
        self.n = n
        self.nx, self.nz = grid_of(n)
        self.me = lax.axis_index("seq")
        self.x = self.me // (2 * self.nz)
        self.z = lax.rem(self.me // 2, self.nz)
        self.y = lax.rem(self.me, 2)
        self.send_sem, self.recv_sem = send_sem, recv_sem
        self.taken = 0
        self.started = []

    def at(self, x, z, y):
        return x * (2 * self.nz) + z * 2 + y

    def xs(self, d):
        return lax.rem(self.x + d + self.nx, self.nx)

    def zs(self, d):
        return lax.rem(self.z + d + self.nz, self.nz)

    def slot(self, count=1):
        first = self.taken
        self.taken += count
        return first

    def copy(self, src, dst, target, slot, recv_slot=None, axis="seq"):
        return pltpu.make_async_remote_copy(
            src_ref=src,
            dst_ref=dst,
            send_sem=self.send_sem.at[slot],
            recv_sem=self.recv_sem.at[slot if recv_slot is None else recv_slot],
            device_id={axis: target},
            device_id_type=MESH,
        )

    def send(self, src, dst, target, slot, axis="seq"):
        made = self.copy(src, dst, target, slot, axis=axis)
        made.start()
        self.started.append(made)
        return made

    def drain(self):
        for made in self.started:
            made.wait_send()
        self.started = []

    def greet(self, near=True, rep=False, first=False):
        barrier = pltpu.get_barrier_semaphore()
        peers = [{"seq": self.at(self.xs(d), self.z, self.y)} for d in range(1, self.nx)]
        peers += [{"seq": self.at(self.x, self.zs(d), self.y)} for d in range(1, self.nz)]
        peers += [{"seq": self.at(self.x, self.z, 1 - self.y)}]
        if near:
            peers += [{"seq": lax.rem(self.me + d, self.n)} for d in (1, self.n - 1)]
        if rep:
            reps = lax.axis_size("rep")
            here = lax.axis_index("rep")
            peers += [{"rep": lax.rem(here + d, reps)} for d in (rep, reps - rep)]
        for peer in peers:
            pl.semaphore_signal(barrier, inc=1, device_id=peer, device_id_type=MESH)
        if first:
            @pl.when(self.me == 0)
            def _():
                for p in range(1, 2 * self.nx):
                    pl.semaphore_signal(
                        barrier, inc=1, device_id={"seq": self.at(p // 2, 0, p % 2)},
                        device_id_type=MESH,
                    )

            @pl.when((self.z == 0) & (self.me != 0))
            def _():
                pl.semaphore_signal(barrier, inc=1, device_id={"seq": 0}, device_id_type=MESH)

        count = len(peers)
        if first:
            more = jnp.where(self.z == 0, 1, 0)
            count = count + jnp.where(self.me == 0, 2 * self.nx - 1, more)
        pl.semaphore_wait(barrier, count)


class Spread:
    def __init__(self, pl_, src, dst):
        self.p, self.src, self.dst = pl_, src, dst
        p = pl_
        self.rows = src.shape[0] // (2 * p.nx)
        self.piece = p.x * 2 + p.y
        self.a = p.slot(2 * p.nx)
        self.b = p.slot(p.nz)
        self.c = p.slot()
        self.d = p.slot(p.nx)

    def cut(self, ref, index, rows=None):
        rows = rows or self.rows
        return ref.at[pl.ds(pl.multiple_of(index * rows, rows), rows)]

    def one(self, p):
        first = []
        for i in range(1, 2 * p.nx):
            first.append(
                p.copy(
                    self.src.at[pl.ds(i * self.rows, self.rows)],
                    self.dst.at[pl.ds(i * self.rows, self.rows)],
                    p.at(i // 2, 0, i % 2), self.a + i, self.a,
                )
            )

        @pl.when(p.me == 0)
        def _():
            for made in first:
                made.start()
            self.dst[pl.ds(0, self.rows)] = self.src[pl.ds(0, self.rows)]
        self.first = first

    def two(self, p):
        mine = self.cut(self.dst, self.piece)
        second = [
            p.copy(mine, mine, p.at(p.x, d, p.y), self.b + d, self.b) for d in range(1, p.nz)
        ]

        @pl.when((p.z == 0) & (p.me != 0))
        def _():
            self.first[0].wait_recv()

        @pl.when(p.z == 0)
        def _():
            for made in second:
                made.start()
        self.second = second

    def three(self, p):
        mine = self.cut(self.dst, self.piece)

        @pl.when(p.z != 0)
        def _():
            self.second[0].wait_recv()
        self.third = p.send(mine, mine, p.at(p.x, p.z, 1 - p.y), self.c)

    def four(self, p):
        self.third.wait_recv()
        pair = self.cut(self.dst, p.x, 2 * self.rows)
        self.fourth = [
            p.send(pair, pair, p.at(p.xs(d), p.z, p.y), self.d + d) for d in range(1, p.nx)
        ]

    def end(self, p):
        for made in self.fourth:
            made.wait_recv()

        @pl.when(p.me == 0)
        def _():
            for made in self.first:
                made.wait_send()

        @pl.when(p.z == 0)
        def _():
            for made in self.second:
                made.wait_send()


def gather_kernel(n, scale, tok, key, wl, kv, wk, tt, pbuf, rbuf, send_sem, recv_sem):
    p = Place(n, send_sem, recv_sem)
    nx, nz = p.nx, p.nz
    width = tok.shape[1] // nx
    half = nz // 2
    p.greet(first=True)

    right = p.at(p.x, p.zs(1), p.y)
    left = p.at(p.x, p.zs(-1), p.y)
    after = lax.rem(p.me + 1, n)
    before = lax.rem(p.me + n - 1, n)

    def shard(dz, k):
        return p.zs(dz) * 2 + (p.y if k == 0 else 1 - p.y)

    rs = [[p.slot() for _ in range(2)] for _ in range(half)]
    ls = [[p.slot() for _ in range(2)] for _ in range(half)]

    def relay(s, k):
        out = []
        src_r = wl if (s == 0 and k == 0) else wk.at[shard(-s, k)]
        src_l = wl if (s == 0 and k == 0) else wk.at[shard(s, k)]
        if s < half - 1 or k == 0:
            hops_r[s][k] = p.send(src_r, wk.at[shard(-s, k)], right, rs[s][k])
        if s < half - 1 or k == 1:
            hops_l[s][k] = p.send(src_l, wk.at[shard(s, k)], left, ls[s][k])

    hops_r = [[None, None] for _ in range(half)]
    hops_l = [[None, None] for _ in range(half)]

    other = p.send(wl, wk.at[shard(0, 0)], p.at(p.x, p.z, 1 - p.y), p.slot())
    relay(0, 0)
    cols = [p.slot() for _ in range(nx)]
    moved = []
    for d in range(1, nx):
        to = p.xs(d)
        part = tok.at[:, pl.ds(pl.multiple_of(to * width, width), width)]
        moved.append(p.send(part, tt.at[p.x], p.at(to, p.z, p.y), cols[d]))
    key_right = p.send(key, kv.at[0, 0], after, p.slot())
    key_left = p.send(key, kv.at[2, 0], before, p.slot())
    keys0 = Spread(p, key, kv.at[3, 0])
    keys0.one(p)
    kv[1, 0] = key[...]
    wk[shard(0, 0)] = wl[...]
    tt[p.x] = tok[:, pl.ds(pl.multiple_of(p.x * width, width), width)]
    other.wait_recv()
    relay(0, 1)
    stages = [keys0.two, keys0.three, keys0.four]
    for s in range(1, half):
        for k in range(2):
            if hops_r[s - 1][k] is not None:
                hops_r[s - 1][k].wait_recv()
            if hops_l[s - 1][k] is not None:
                hops_l[s - 1][k].wait_recv()
            relay(s, k)
        if stages:
            stages.pop(0)(p)
    while stages:
        stages.pop(0)(p)
    for k in range(2):
        if hops_r[half - 1][k] is not None:
            hops_r[half - 1][k].wait_recv()
        if hops_l[half - 1][k] is not None:
            hops_l[half - 1][k].wait_recv()
    for made in moved:
        made.wait_recv()
    weight = wk[...].reshape(2 * nz * wk.shape[1], wk.shape[2])
    sums = [p.slot() for _ in range(nx)]
    parts = []
    for d in range(1, nx):
        to = p.xs(d)
        part = jnp.dot(tt[to], weight, preferred_element_type=F32) * scale
        pbuf[to] = part.astype(BF16)
        parts.append(p.send(pbuf.at[to], rbuf.at[p.x], p.at(to, p.z, p.y), sums[d]))
    total = jnp.dot(tt[p.x], weight, preferred_element_type=F32) * scale
    for d in range(1, nx):
        parts[d - 1].wait_recv()
        total = total + rbuf[p.xs(-d)].astype(F32)
    kv[1, 1] = total.astype(BF16)
    own = kv.at[1, 1]
    val_right = p.send(own, kv.at[0, 1], after, p.slot())
    val_left = p.send(own, kv.at[2, 1], before, p.slot())
    vals0 = Spread(p, own, kv.at[3, 1])
    vals0.one(p)
    vals0.two(p)
    vals0.three(p)
    vals0.four(p)
    keys0.end(p)
    vals0.end(p)
    for made in (key_right, key_left, val_right, val_left):
        made.wait_recv()
    p.drain()


def attend_kernel(
    n, q, cot, kv, ra, rb, dq, tot, cha, chb,
    kc, vc, qs, cs, sc, gw, low, out_l, out_r, out_g, in_l, in_r,
    g1, r1, g2, r2, g3, r3, g4, send_sem, recv_sem,
):
    p = Place(n, send_sem, recv_sem)
    nx, nz = p.nx, p.nz
    p.greet(first=True)
    score = HD ** -0.5
    for s in range(6):
        src = kv.at[s] if s < 4 else (ra, rb)[s - 4]
        kc[s] = src[0]
        vc[s] = src[1]
    first_ok = jnp.where(p.me == 0, MASKED, 0.0)
    last_ok = jnp.where(p.me == n - 1, MASKED, 0.0)
    nt = (((1,), (1,)), ((), ()))
    tn = (((0,), (0,)), ((), ()))
    nn = (((1,), (0,)), ((), ()))

    def mm(a, b, dims):
        return lax.dot_general(a, b, dims, preferred_element_type=F32)

    def group(g, _):
        cols = pl.ds(pl.multiple_of(g * HD, HD), HD)
        for r in range(GROUP):
            head = pl.ds(pl.multiple_of((g * GROUP + r) * HD, HD), HD)
            qs[pl.ds(r * BLOCK_TOKENS, BLOCK_TOKENS)] = q[:, head]
            cs[pl.ds(r * BLOCK_TOKENS, BLOCK_TOKENS)] = cot[:, head]
        high = None
        for s in range(6):
            t = mm(kc[s, :, cols], qs[...], nt) * score
            if s == 0:
                t = t + first_ok
            if s == 2:
                t = t + last_ok
            sc[s] = t
            m = jnp.max(t, axis=0, keepdims=True)
            high = m if high is None else jnp.maximum(high, m)
        total = None
        for s in range(6):
            e = jnp.exp(sc[s] - high)
            sc[s] = e
            m = jnp.sum(e, axis=0, keepdims=True)
            total = m if total is None else total + m
        inv = 1.0 / total
        delta = None
        for s in range(6):
            w = sc[s] * inv
            sc[s] = w
            wl = w.astype(BF16)
            low[s] = wl
            gv = mm(vc[s, :, cols], cs[...], nt)
            gw[s] = gv
            m = jnp.sum(wl.astype(F32) * gv, axis=0, keepdims=True)
            delta = m if delta is None else delta + m
        back = None
        for s in range(6):
            ds = (sc[s] * (gw[s] - delta) * score).astype(BF16)
            dv = mm(low[s], cs[...], nn)
            dk = mm(ds, qs[...], nn)
            if s == 1:
                tot[0, :, cols] = dk
                tot[1, :, cols] = dv
            else:
                to = {0: out_l, 2: out_r, 3: out_g, 4: cha, 5: chb}[s]
                to[0, :, cols] = dk.astype(BF16)
                to[1, :, cols] = dv.astype(BF16)
            part = mm(kc[s, :, cols], ds, tn)
            back = part if back is None else back + part
        for r in range(GROUP):
            head = pl.ds(pl.multiple_of((g * GROUP + r) * HD, HD), HD)
            piece = back[:, r * BLOCK_TOKENS:(r + 1) * BLOCK_TOKENS]
            dq[:, head] = piece.T.astype(BF16)
        return 0

    lax.fori_loop(0, KV_HEADS, group, 0)

    after = lax.rem(p.me + 1, n)
    before = lax.rem(p.me + n - 1, n)
    to_left = p.send(out_l, in_r, before, p.slot())
    to_right = p.send(out_r, in_l, after, p.slot())
    rows = BLOCK_TOKENS // nx
    cut = rows // 2

    def row(index, size):
        return pl.ds(pl.multiple_of(index * size, size), size)

    base = p.slot(nx)
    ones = [
        p.send(out_g.at[:, row(p.xs(d), rows)], g1.at[p.x], p.at(p.xs(d), p.z, p.y), base + d)
        for d in range(1, nx)
    ]
    acc = out_g[:, row(p.x, rows)].astype(F32)
    for d in range(1, nx):
        ones[d - 1].wait_recv()
        acc = acc + g1[p.xs(-d)].astype(F32)
    r1[...] = acc
    g2[0] = r1[:, row(1 - p.y, cut)].astype(BF16)
    two = p.send(g2.at[0], g2.at[1], p.at(p.x, p.z, 1 - p.y), p.slot())
    two.wait_recv()
    acc = r1[:, row(p.y, cut)] + g2[1].astype(F32)
    r2[...] = acc.astype(BF16)
    zbase = p.slot(nz)
    fbase = p.slot(2 * nx)
    piece = p.x * 2 + p.y

    def up(d, slot):
        return p.copy(r2, g3.at[d], p.at(p.x, 0, p.y), slot)

    def home(d, slot):
        return p.copy(r3, g4.at[d], 0, slot)

    three = up(p.z, zbase + p.z)
    four = home(piece, fbase + piece)

    @pl.when(p.z != 0)
    def _():
        three.start()

    @pl.when(p.z == 0)
    def _():
        for d in range(1, nz):
            up(d, zbase + d).wait_recv()
        tally = acc
        for d in range(1, nz):
            tally = tally + g3[d].astype(F32)
        r3[...] = tally

        @pl.when(p.me != 0)
        def _():
            four.start()

    to_right.wait_recv()
    to_left.wait_recv()
    tot[...] = tot[...] + in_l[...].astype(F32) + in_r[...].astype(F32)

    @pl.when(p.me == 0)
    def _():
        for d in range(1, 2 * nx):
            home(d, fbase + d).wait_recv()
        tot[:, pl.ds(0, cut)] = tot[:, pl.ds(0, cut)] + r3[...]
        for d in range(1, 2 * nx):
            at = pl.ds(d * cut, cut)
            tot[:, at] = tot[:, at] + g4[d]

    @pl.when(p.z != 0)
    def _():
        three.wait_send()

    @pl.when((p.z == 0) & (p.me != 0))
    def _():
        four.wait_send()

    p.drain()


def update_kernel(
    n, hop, scale, vt, tt, wk, weight, ig, nw,
    vt4, igs, dsend, drecv, own, ys, yr, us, ur, send_sem, recv_sem,
):
    p = Place(n, send_sem, recv_sem)
    nx, nz = p.nx, p.nz
    width = tt.shape[2]
    deep = width // nz
    p.greet(near=False, rep=hop)
    base = p.slot(nx)
    sent = [p.send(vt, vt4.at[p.x], p.at(p.xs(d), p.z, p.y), base + d) for d in range(1, nx)]
    vt4[p.x] = vt[...]
    for made in sent:
        made.wait_recv()
    grads = vt4[...].reshape(nx * BLOCK_TOKENS, vt.shape[1])
    tn = (((0,), (0,)), ((), ()))

    def change(block):
        rows = tt[:, :, pl.ds(pl.multiple_of(block * deep, deep), deep)]
        rows = rows.reshape(nx * BLOCK_TOKENS, deep)
        return lax.dot_general(rows, grads, tn, preferred_element_type=F32) * scale

    zbase = p.slot(nz)
    zs = []
    for d in range(1, nz):
        to = p.zs(d)
        part = change(to).astype(BF16)
        dsend[to] = part.reshape(dsend.shape[1:])
        zs.append(p.send(dsend.at[to], drecv.at[p.z], p.at(p.x, to, p.y), zbase + d))
    own[...] = change(p.z).reshape(own.shape)
    ibase = p.slot(nx)
    whole = wk[...].reshape(width, wk.shape[2])
    nt = (((1,), (1,)), ((), ()))

    def back(which):
        return lax.dot_general(vt4[which], whole, nt, preferred_element_type=F32) * scale

    here = pl.ds(pl.multiple_of(p.x * width, width), width)
    backs = []
    for d in range(1, nx):
        to = p.xs(d)
        igs[to] = back(to).astype(BF16)
        backs.append(p.send(igs.at[to], ig.at[:, here], p.at(to, p.z, p.y), ibase + d))
    ig[:, here] = back(p.x).astype(BF16)
    for made in zs:
        made.wait_recv()
    acc = own[...]
    for d in range(1, nz):
        acc = acc + drecv[p.zs(-d)].astype(F32)
    own[...] = acc
    ys[...] = own[1 - p.y].astype(BF16)
    yc = p.send(ys, yr, p.at(p.x, p.z, 1 - p.y), p.slot())
    yc.wait_recv()
    updated = weight[...] - LEARN_RATE * (own[p.y] + yr[...].astype(F32))
    us[...] = updated.astype(BF16)
    reps = lax.axis_size("rep")
    rc = p.send(us, ur, lax.rem(lax.axis_index("rep") + hop, reps), p.slot(), axis="rep")
    rc.wait_recv()
    nw[...] = 0.5 * (updated + ur[...].astype(F32))
    for made in backs:
        made.wait_recv()
    p.drain()


VM = pl.BlockSpec(memory_space=pltpu.VMEM)


def sems(count):
    return [pltpu.SemaphoreType.DMA((count,)), pltpu.SemaphoreType.DMA((count,))]


def params(which, mib=60):
    return pltpu.CompilerParams(
        collective_id=which, has_side_effects=True, vmem_limit_bytes=mib * 2**20
    )


def sds(shape, dtype):
    return jax.ShapeDtypeStruct(shape, dtype)


def swap(a, b, shift, sign, n):
    def branch(c):
        def go(a, b):
            fore = [(i, (i + sign * c) % n) for i in range(n)]
            aft = [(i, (i - sign * (c + 1)) % n) for i in range(n)]
            return lax.ppermute(a, "seq", fore), lax.ppermute(b, "seq", aft)
        return go

    def pick(low, high):
        if high - low == 1:
            return branch(low)
        mid = (low + high) // 2
        one, two = pick(low, mid), pick(mid, high)
        return lambda a, b: lax.cond(shift < mid, one, two, a, b)

    return pick(1, n // 2)(a, b)


def shards(inputs, queries, key_heads, cotangent, value_weight, random_blocks):
    n = lax.axis_size("seq")
    nx, nz = grid_of(n)
    tokens, query, key = inputs[0], queries[0], key_heads[0]
    upstream, weight = cotangent[0], value_weight[0]
    rows, model = tokens.shape
    kvw = key.shape[1]
    qw = query.shape[1]
    deep = weight.shape[0]
    scale = model ** -0.5
    weight_low = weight.astype(BF16)
    offset = lax.rem(n - random_blocks[0, 0], n)
    shift = jnp.minimum(offset, n - 1 - offset)

    kv, wk, tt = pl.pallas_call(
        functools.partial(gather_kernel, n, scale),
        out_shape=(
            sds((4, 2, rows, kvw), BF16),
            sds((2 * nz, deep, kvw), BF16),
            sds((nx, rows, model // nx), BF16),
        ),
        in_specs=[VM] * 3,
        out_specs=(VM,) * 3,
        scratch_shapes=[
            pltpu.VMEM((nx, rows, kvw), BF16),
            pltpu.VMEM((nx, rows, kvw), BF16),
            *sems(96),
        ],
        compiler_params=params(0),
        name="gather",
    )(tokens, key, weight_low)

    pair = kv[1]
    ra, rb = swap(pair, pair, shift, 1, n)

    cut = rows // nx // 2
    dq, tot, cha, chb = pl.pallas_call(
        functools.partial(attend_kernel, n),
        out_shape=(
            sds((rows, qw), BF16),
            sds((2, rows, kvw), F32),
            sds((2, rows, kvw), BF16),
            sds((2, rows, kvw), BF16),
        ),
        in_specs=[VM] * 5,
        out_specs=(VM,) * 4,
        scratch_shapes=[
            pltpu.VMEM((6, rows, kvw), BF16),
            pltpu.VMEM((6, rows, kvw), BF16),
            pltpu.VMEM((GROUP * rows, HD), BF16),
            pltpu.VMEM((GROUP * rows, HD), BF16),
            pltpu.VMEM((6, rows, GROUP * rows), F32),
            pltpu.VMEM((6, rows, GROUP * rows), F32),
            pltpu.VMEM((6, rows, GROUP * rows), BF16),
            *[pltpu.VMEM((2, rows, kvw), BF16)] * 5,
            pltpu.VMEM((nx, 2, 2 * cut, kvw), BF16),
            pltpu.VMEM((2, 2 * cut, kvw), F32),
            pltpu.VMEM((2, 2, cut, kvw), BF16),
            pltpu.VMEM((2, cut, kvw), BF16),
            pltpu.VMEM((nz, 2, cut, kvw), BF16),
            pltpu.VMEM((2, cut, kvw), F32),
            pltpu.VMEM((2 * nx, 2, cut, kvw), F32),
            *sems(32),
        ],
        compiler_params=params(1),
        name="attend",
    )(query, upstream, kv, ra, rb)

    ba, bb = swap(cha, chb, shift, -1, n)
    tot = tot + ba.astype(F32) + bb.astype(F32)
    key_grad = tot[0].astype(BF16)
    value_total = tot[1].astype(BF16)

    reps = lax.axis_size("rep")
    hop = 2 ** (STEP % (reps.bit_length() - 1))
    input_grad, new_weight = pl.pallas_call(
        functools.partial(update_kernel, n, hop, scale),
        out_shape=(sds((rows, model), BF16), sds((deep, kvw), F32)),
        in_specs=[VM] * 4,
        out_specs=(VM,) * 2,
        scratch_shapes=[
            pltpu.VMEM((nx, rows, kvw), BF16),
            pltpu.VMEM((nx, rows, model // nx), BF16),
            pltpu.VMEM((nz, 2, deep, kvw), BF16),
            pltpu.VMEM((nz, 2, deep, kvw), BF16),
            pltpu.VMEM((2, deep, kvw), F32),
            *[pltpu.VMEM((deep, kvw), BF16)] * 4,
            *sems(32),
        ],
        compiler_params=params(2),
        name="update",
    )(value_total, tt, wk, weight)
    return input_grad[None], dq[None], key_grad[None], new_weight[None]


def solution(mesh):
    p3 = P("rep", "seq", None)
    return jax.shard_map(
        shards,
        mesh=mesh,
        in_specs=(p3,) * 5 + (P(),),
        out_specs=(p3,) * 4,
        check_vma=False,
    )
```

```python
import functools
import jax
import jax.numpy as jnp
from jax import lax
from jax.experimental import pallas as pl
from jax.experimental.pallas import tpu as pltpu
from jax.sharding import PartitionSpec as P

HEADS = 16
KV_HEADS = 4
HD = 128
BLOCK_TOKENS = 128
STEP = 4
LEARN_RATE = 2.0
MASKED = -1e30
GROUP = HEADS // KV_HEADS
MESH = pl.DeviceIdType.MESH
F32 = jnp.float32
BF16 = jnp.bfloat16


def grid_of(n):
    return {64: (4, 8), 16: (2, 4), 8: (2, 2)}[n]


class Place:
    def __init__(self, n, send_sem, recv_sem):
        self.n = n
        self.nx, self.nz = grid_of(n)
        self.me = lax.axis_index("seq")
        self.x = self.me // (2 * self.nz)
        self.z = lax.rem(self.me // 2, self.nz)
        self.y = lax.rem(self.me, 2)
        self.send_sem, self.recv_sem = send_sem, recv_sem
        self.taken = 0
        self.started = []

    def at(self, x, z, y):
        return x * (2 * self.nz) + z * 2 + y

    def xs(self, d):
        return lax.rem(self.x + d + self.nx, self.nx)

    def zs(self, d):
        return lax.rem(self.z + d + self.nz, self.nz)

    def slot(self, count=1):
        first = self.taken
        self.taken += count
        return first

    def copy(self, src, dst, target, slot, recv_slot=None, axis="seq"):
        return pltpu.make_async_remote_copy(
            src_ref=src,
            dst_ref=dst,
            send_sem=self.send_sem.at[slot],
            recv_sem=self.recv_sem.at[slot if recv_slot is None else recv_slot],
            device_id={axis: target},
            device_id_type=MESH,
        )

    def send(self, src, dst, target, slot, axis="seq"):
        made = self.copy(src, dst, target, slot, axis=axis)
        made.start()
        self.started.append(made)
        return made

    def drain(self):
        for made in self.started:
            made.wait_send()
        self.started = []

    def greet(self, near=True, rep=False, first=False):
        barrier = pltpu.get_barrier_semaphore()
        peers = [{"seq": self.at(self.xs(d), self.z, self.y)} for d in range(1, self.nx)]
        peers += [{"seq": self.at(self.x, self.zs(d), self.y)} for d in range(1, self.nz)]
        peers += [{"seq": self.at(self.x, self.z, 1 - self.y)}]
        if near:
            peers += [{"seq": lax.rem(self.me + d, self.n)} for d in (1, self.n - 1)]
        if rep:
            reps = lax.axis_size("rep")
            here = lax.axis_index("rep")
            peers += [{"rep": lax.rem(here + d, reps)} for d in (rep, reps - rep)]
        for peer in peers:
            pl.semaphore_signal(barrier, inc=1, device_id=peer, device_id_type=MESH)
        if first:
            @pl.when(self.me == 0)
            def _():
                for p in range(1, 2 * self.nx):
                    pl.semaphore_signal(
                        barrier, inc=1, device_id={"seq": self.at(p // 2, 0, p % 2)},
                        device_id_type=MESH,
                    )

            @pl.when((self.z == 0) & (self.me != 0))
            def _():
                pl.semaphore_signal(barrier, inc=1, device_id={"seq": 0}, device_id_type=MESH)

        count = len(peers)
        if first:
            more = jnp.where(self.z == 0, 1, 0)
            count = count + jnp.where(self.me == 0, 2 * self.nx - 1, more)
        pl.semaphore_wait(barrier, count)


class Spread:
    def __init__(self, pl_, src, dst):
        self.p, self.src, self.dst = pl_, src, dst
        p = pl_
        self.rows = src.shape[0] // (2 * p.nx)
        self.piece = p.x * 2 + p.y
        self.a = p.slot(2 * p.nx)
        self.b = p.slot(p.nz)
        self.c = p.slot()
        self.d = p.slot(p.nx)

    def cut(self, ref, index, rows=None):
        rows = rows or self.rows
        return ref.at[pl.ds(pl.multiple_of(index * rows, rows), rows)]

    def one(self, p):
        first = []
        for i in range(1, 2 * p.nx):
            first.append(
                p.copy(
                    self.src.at[pl.ds(i * self.rows, self.rows)],
                    self.dst.at[pl.ds(i * self.rows, self.rows)],
                    p.at(i // 2, 0, i % 2), self.a + i, self.a,
                )
            )

        @pl.when(p.me == 0)
        def _():
            for made in first:
                made.start()
            self.dst[pl.ds(0, self.rows)] = self.src[pl.ds(0, self.rows)]
        self.first = first

    def two(self, p):
        mine = self.cut(self.dst, self.piece)
        second = [
            p.copy(mine, mine, p.at(p.x, d, p.y), self.b + d, self.b) for d in range(1, p.nz)
        ]

        @pl.when((p.z == 0) & (p.me != 0))
        def _():
            self.first[0].wait_recv()

        @pl.when(p.z == 0)
        def _():
            for made in second:
                made.start()
        self.second = second

    def three(self, p):
        mine = self.cut(self.dst, self.piece)

        @pl.when(p.z != 0)
        def _():
            self.second[0].wait_recv()
        self.third = p.send(mine, mine, p.at(p.x, p.z, 1 - p.y), self.c)

    def four(self, p):
        self.third.wait_recv()
        pair = self.cut(self.dst, p.x, 2 * self.rows)
        self.fourth = [
            p.send(pair, pair, p.at(p.xs(d), p.z, p.y), self.d + d) for d in range(1, p.nx)
        ]

    def end(self, p):
        for made in self.fourth:
            made.wait_recv()

        @pl.when(p.me == 0)
        def _():
            for made in self.first:
                made.wait_send()

        @pl.when(p.z == 0)
        def _():
            for made in self.second:
                made.wait_send()


def gather_kernel(n, scale, tok, key, wl, kv, wk, tt, pbuf, rbuf, send_sem, recv_sem):
    p = Place(n, send_sem, recv_sem)
    nx, nz = p.nx, p.nz
    width = tok.shape[1] // nx
    half = nz // 2
    p.greet(first=True)

    right = p.at(p.x, p.zs(1), p.y)
    left = p.at(p.x, p.zs(-1), p.y)
    after = lax.rem(p.me + 1, n)
    before = lax.rem(p.me + n - 1, n)

    def shard(dz, k):
        return p.zs(dz) * 2 + (p.y if k == 0 else 1 - p.y)

    rs = [[p.slot() for _ in range(2)] for _ in range(half)]
    ls = [[p.slot() for _ in range(2)] for _ in range(half)]

    def relay(s, k):
        out = []
        src_r = wl if (s == 0 and k == 0) else wk.at[shard(-s, k)]
        src_l = wl if (s == 0 and k == 0) else wk.at[shard(s, k)]
        if s < half - 1 or k == 0:
            hops_r[s][k] = p.send(src_r, wk.at[shard(-s, k)], right, rs[s][k])
        if s < half - 1 or k == 1:
            hops_l[s][k] = p.send(src_l, wk.at[shard(s, k)], left, ls[s][k])

    hops_r = [[None, None] for _ in range(half)]
    hops_l = [[None, None] for _ in range(half)]

    other = p.send(wl, wk.at[shard(0, 0)], p.at(p.x, p.z, 1 - p.y), p.slot())
    relay(0, 0)
    cols = [p.slot() for _ in range(nx)]
    moved = []
    for d in range(1, nx):
        to = p.xs(d)
        part = tok.at[:, pl.ds(pl.multiple_of(to * width, width), width)]
        moved.append(p.send(part, tt.at[p.x], p.at(to, p.z, p.y), cols[d]))
    key_right = p.send(key, kv.at[0, 0], after, p.slot())
    key_left = p.send(key, kv.at[2, 0], before, p.slot())
    keys0 = Spread(p, key, kv.at[3, 0])
    keys0.one(p)
    kv[1, 0] = key[...]
    wk[shard(0, 0)] = wl[...]
    tt[p.x] = tok[:, pl.ds(pl.multiple_of(p.x * width, width), width)]
    other.wait_recv()
    relay(0, 1)
    stages = [keys0.two, keys0.three, keys0.four]
    for s in range(1, half):
        for k in range(2):
            if hops_r[s - 1][k] is not None:
                hops_r[s - 1][k].wait_recv()
            if hops_l[s - 1][k] is not None:
                hops_l[s - 1][k].wait_recv()
            relay(s, k)
        if stages:
            stages.pop(0)(p)
    while stages:
        stages.pop(0)(p)
    for k in range(2):
        if hops_r[half - 1][k] is not None:
            hops_r[half - 1][k].wait_recv()
        if hops_l[half - 1][k] is not None:
            hops_l[half - 1][k].wait_recv()
    for made in moved:
        made.wait_recv()
    weight = wk[...].reshape(2 * nz * wk.shape[1], wk.shape[2])
    sums = [p.slot() for _ in range(nx)]
    parts = []
    for d in range(1, nx):
        to = p.xs(d)
        part = jnp.dot(tt[to], weight, preferred_element_type=F32) * scale
        pbuf[to] = part.astype(BF16)
        parts.append(p.send(pbuf.at[to], rbuf.at[p.x], p.at(to, p.z, p.y), sums[d]))
    total = jnp.dot(tt[p.x], weight, preferred_element_type=F32) * scale
    for d in range(1, nx):
        parts[d - 1].wait_recv()
        total = total + rbuf[p.xs(-d)].astype(F32)
    kv[1, 1] = total.astype(BF16)
    own = kv.at[1, 1]
    val_right = p.send(own, kv.at[0, 1], after, p.slot())
    val_left = p.send(own, kv.at[2, 1], before, p.slot())
    vals0 = Spread(p, own, kv.at[3, 1])
    vals0.one(p)
    vals0.two(p)
    vals0.three(p)
    vals0.four(p)
    keys0.end(p)
    vals0.end(p)
    for made in (key_right, key_left, val_right, val_left):
        made.wait_recv()
    p.drain()


def attend_kernel(
    n, q, cot, kv, ra, rb, dq, tot, cha, chb,
    kc, vc, qs, cs, sc, gw, low, out_l, out_r, out_g, in_l, in_r,
    g1, r1, g2, r2, g3, r3, g4, send_sem, recv_sem,
):
    p = Place(n, send_sem, recv_sem)
    nx, nz = p.nx, p.nz
    p.greet(first=True)
    score = HD ** -0.5
    for s in range(6):
        src = kv.at[s] if s < 4 else (ra, rb)[s - 4]
        kc[s] = src[0]
        vc[s] = src[1]
    first_ok = jnp.where(p.me == 0, MASKED, 0.0)
    last_ok = jnp.where(p.me == n - 1, MASKED, 0.0)
    nt = (((1,), (1,)), ((), ()))
    tn = (((0,), (0,)), ((), ()))
    nn = (((1,), (0,)), ((), ()))

    def mm(a, b, dims):
        return lax.dot_general(a, b, dims, preferred_element_type=F32)

    def group(g, _):
        cols = pl.ds(pl.multiple_of(g * HD, HD), HD)
        for r in range(GROUP):
            head = pl.ds(pl.multiple_of((g * GROUP + r) * HD, HD), HD)
            qs[pl.ds(r * BLOCK_TOKENS, BLOCK_TOKENS)] = q[:, head]
            cs[pl.ds(r * BLOCK_TOKENS, BLOCK_TOKENS)] = cot[:, head]
        high = None
        for s in range(6):
            t = mm(kc[s, :, cols], qs[...], nt) * score
            if s == 0:
                t = t + first_ok
            if s == 2:
                t = t + last_ok
            sc[s] = t
            m = jnp.max(t, axis=0, keepdims=True)
            high = m if high is None else jnp.maximum(high, m)
        total = None
        for s in range(6):
            e = jnp.exp(sc[s] - high)
            sc[s] = e
            m = jnp.sum(e, axis=0, keepdims=True)
            total = m if total is None else total + m
        inv = 1.0 / total
        delta = None
        for s in range(6):
            w = sc[s] * inv
            sc[s] = w
            wl = w.astype(BF16)
            low[s] = wl
            gv = mm(vc[s, :, cols], cs[...], nt)
            gw[s] = gv
            m = jnp.sum(wl.astype(F32) * gv, axis=0, keepdims=True)
            delta = m if delta is None else delta + m
        back = None
        for s in range(6):
            ds = (sc[s] * (gw[s] - delta) * score).astype(BF16)
            dv = mm(low[s], cs[...], nn)
            dk = mm(ds, qs[...], nn)
            if s == 1:
                tot[0, :, cols] = dk
                tot[1, :, cols] = dv
            else:
                to = {0: out_l, 2: out_r, 3: out_g, 4: cha, 5: chb}[s]
                to[0, :, cols] = dk.astype(BF16)
                to[1, :, cols] = dv.astype(BF16)
            part = mm(kc[s, :, cols], ds, tn)
            back = part if back is None else back + part
        for r in range(GROUP):
            head = pl.ds(pl.multiple_of((g * GROUP + r) * HD, HD), HD)
            piece = back[:, r * BLOCK_TOKENS:(r + 1) * BLOCK_TOKENS]
            dq[:, head] = piece.T.astype(BF16)
        return 0

    lax.fori_loop(0, KV_HEADS, group, 0)

    after = lax.rem(p.me + 1, n)
    before = lax.rem(p.me + n - 1, n)
    to_left = p.send(out_l, in_r, before, p.slot())
    to_right = p.send(out_r, in_l, after, p.slot())
    rows = BLOCK_TOKENS // nx
    cut = rows // 2

    def row(index, size):
        return pl.ds(pl.multiple_of(index * size, size), size)

    base = p.slot(nx)
    ones = [
        p.send(out_g.at[:, row(p.xs(d), rows)], g1.at[p.x], p.at(p.xs(d), p.z, p.y), base + d)
        for d in range(1, nx)
    ]
    acc = out_g[:, row(p.x, rows)].astype(F32)
    for d in range(1, nx):
        ones[d - 1].wait_recv()
        acc = acc + g1[p.xs(-d)].astype(F32)
    r1[...] = acc
    g2[0] = r1[:, row(1 - p.y, cut)].astype(BF16)
    two = p.send(g2.at[0], g2.at[1], p.at(p.x, p.z, 1 - p.y), p.slot())
    two.wait_recv()
    acc = r1[:, row(p.y, cut)] + g2[1].astype(F32)
    r2[...] = acc.astype(BF16)
    zbase = p.slot(nz)
    fbase = p.slot(2 * nx)
    piece = p.x * 2 + p.y

    def up(d, slot):
        return p.copy(r2, g3.at[d], p.at(p.x, 0, p.y), slot)

    def home(d, slot):
        return p.copy(r3, g4.at[d], 0, slot)

    three = up(p.z, zbase + p.z)
    four = home(piece, fbase + piece)

    @pl.when(p.z != 0)
    def _():
        three.start()

    @pl.when(p.z == 0)
    def _():
        for d in range(1, nz):
            up(d, zbase + d).wait_recv()
        tally = acc
        for d in range(1, nz):
            tally = tally + g3[d].astype(F32)
        r3[...] = tally

        @pl.when(p.me != 0)
        def _():
            four.start()

    to_right.wait_recv()
    to_left.wait_recv()
    tot[...] = tot[...] + in_l[...].astype(F32) + in_r[...].astype(F32)

    @pl.when(p.me == 0)
    def _():
        for d in range(1, 2 * nx):
            home(d, fbase + d).wait_recv()
        tot[:, pl.ds(0, cut)] = tot[:, pl.ds(0, cut)] + r3[...]
        for d in range(1, 2 * nx):
            at = pl.ds(d * cut, cut)
            tot[:, at] = tot[:, at] + g4[d]

    @pl.when(p.z != 0)
    def _():
        three.wait_send()

    @pl.when((p.z == 0) & (p.me != 0))
    def _():
        four.wait_send()

    p.drain()


def update_kernel(
    n, hop, scale, vt, tt, wk, weight, ig, nw,
    vt4, igs, dsend, drecv, own, ys, yr, us, ur, send_sem, recv_sem,
):
    p = Place(n, send_sem, recv_sem)
    nx, nz = p.nx, p.nz
    width = tt.shape[2]
    deep = width // nz
    p.greet(near=False, rep=hop)
    base = p.slot(nx)
    sent = [p.send(vt, vt4.at[p.x], p.at(p.xs(d), p.z, p.y), base + d) for d in range(1, nx)]
    vt4[p.x] = vt[...]
    for made in sent:
        made.wait_recv()
    grads = vt4[...].reshape(nx * BLOCK_TOKENS, vt.shape[1])
    tn = (((0,), (0,)), ((), ()))

    def change(block):
        rows = tt[:, :, pl.ds(pl.multiple_of(block * deep, deep), deep)]
        rows = rows.reshape(nx * BLOCK_TOKENS, deep)
        return lax.dot_general(rows, grads, tn, preferred_element_type=F32) * scale

    zbase = p.slot(nz)
    zs = []
    for d in range(1, nz):
        to = p.zs(d)
        part = change(to).astype(BF16)
        dsend[to] = part.reshape(dsend.shape[1:])
        zs.append(p.send(dsend.at[to], drecv.at[p.z], p.at(p.x, to, p.y), zbase + d))
    own[...] = change(p.z).reshape(own.shape)
    ibase = p.slot(nx)
    whole = wk[...].reshape(width, wk.shape[2])
    nt = (((1,), (1,)), ((), ()))

    def back(which):
        return lax.dot_general(vt4[which], whole, nt, preferred_element_type=F32) * scale

    here = pl.ds(pl.multiple_of(p.x * width, width), width)
    backs = []
    for d in range(1, nx):
        to = p.xs(d)
        igs[to] = back(to).astype(BF16)
        backs.append(p.send(igs.at[to], ig.at[:, here], p.at(to, p.z, p.y), ibase + d))
    ig[:, here] = back(p.x).astype(BF16)
    for made in zs:
        made.wait_recv()
    acc = own[...]
    for d in range(1, nz):
        acc = acc + drecv[p.zs(-d)].astype(F32)
    own[...] = acc
    ys[...] = own[1 - p.y].astype(BF16)
    yc = p.send(ys, yr, p.at(p.x, p.z, 1 - p.y), p.slot())
    yc.wait_recv()
    updated = weight[...] - LEARN_RATE * (own[p.y] + yr[...].astype(F32))
    us[...] = updated.astype(BF16)
    reps = lax.axis_size("rep")
    rc = p.send(us, ur, lax.rem(lax.axis_index("rep") + hop, reps), p.slot(), axis="rep")
    rc.wait_recv()
    nw[...] = 0.5 * (updated + ur[...].astype(F32))
    for made in backs:
        made.wait_recv()
    p.drain()


VM = pl.BlockSpec(memory_space=pltpu.VMEM)


def sems(count):
    return [pltpu.SemaphoreType.DMA((count,)), pltpu.SemaphoreType.DMA((count,))]


def params(which, mib=60):
    return pltpu.CompilerParams(
        collective_id=which, has_side_effects=True, vmem_limit_bytes=mib * 2**20
    )


def sds(shape, dtype):
    return jax.ShapeDtypeStruct(shape, dtype)


def swap_kernel(n, c, sign, a, b, oa, ob, send_sem, recv_sem):
    me = lax.axis_index("seq")
    fore = lax.rem(me + sign * c + n, n)
    aft = lax.rem(me - sign * (c + 1) + n, n)
    from_fore = lax.rem(me - sign * c + n, n)
    from_aft = lax.rem(me + sign * (c + 1) + n, n)
    barrier = pltpu.get_barrier_semaphore()
    for peer in (fore, aft, from_fore, from_aft):
        pl.semaphore_signal(barrier, inc=1, device_id={"seq": peer}, device_id_type=MESH)
    pl.semaphore_wait(barrier, 4)
    made = [
        pltpu.make_async_remote_copy(
            src_ref=src, dst_ref=dst, send_sem=send_sem.at[i], recv_sem=recv_sem.at[i],
            device_id={"seq": to}, device_id_type=MESH,
        )
        for i, (src, dst, to) in enumerate(((a, oa, fore), (b, ob, aft)))
    ]
    for copy in made:
        copy.start()
    for copy in made:
        copy.wait()


def swap(a, b, shift, sign, n, first_id):
    anywhere = pl.BlockSpec(memory_space=pl.ANY)

    def branch(c):
        return pl.pallas_call(
            functools.partial(swap_kernel, n, c, sign),
            out_shape=(sds(a.shape, a.dtype),) * 2,
            in_specs=[anywhere] * 2,
            out_specs=(anywhere,) * 2,
            scratch_shapes=sems(2),
            compiler_params=pltpu.CompilerParams(
                collective_id=first_id + c, has_side_effects=True
            ),
            name=f"swap_{c}",
        )

    return lax.switch(shift - 1, [branch(c) for c in range(1, n // 2)], a, b)


def shards(inputs, queries, key_heads, cotangent, value_weight, random_blocks):
    n = lax.axis_size("seq")
    nx, nz = grid_of(n)
    tokens, query, key = inputs[0], queries[0], key_heads[0]
    upstream, weight = cotangent[0], value_weight[0]
    rows, model = tokens.shape
    kvw = key.shape[1]
    qw = query.shape[1]
    deep = weight.shape[0]
    scale = model ** -0.5
    weight_low = weight.astype(BF16)
    offset = lax.rem(n - random_blocks[0, 0], n)
    shift = jnp.minimum(offset, n - 1 - offset)

    kv, wk, tt = pl.pallas_call(
        functools.partial(gather_kernel, n, scale),
        out_shape=(
            sds((4, 2, rows, kvw), BF16),
            sds((2 * nz, deep, kvw), BF16),
            sds((nx, rows, model // nx), BF16),
        ),
        in_specs=[VM] * 3,
        out_specs=(VM,) * 3,
        scratch_shapes=[
            pltpu.VMEM((nx, rows, kvw), BF16),
            pltpu.VMEM((nx, rows, kvw), BF16),
            *sems(96),
        ],
        compiler_params=params(0),
        name="gather",
    )(tokens, key, weight_low)

    pair = kv[1]
    ra, rb = swap(pair, pair, shift, 1, n, 2)

    cut = rows // nx // 2
    dq, tot, cha, chb = pl.pallas_call(
        functools.partial(attend_kernel, n),
        out_shape=(
            sds((rows, qw), BF16),
            sds((2, rows, kvw), F32),
            sds((2, rows, kvw), BF16),
            sds((2, rows, kvw), BF16),
        ),
        in_specs=[VM] * 5,
        out_specs=(VM,) * 4,
        scratch_shapes=[
            pltpu.VMEM((6, rows, kvw), BF16),
            pltpu.VMEM((6, rows, kvw), BF16),
            pltpu.VMEM((GROUP * rows, HD), BF16),
            pltpu.VMEM((GROUP * rows, HD), BF16),
            pltpu.VMEM((6, rows, GROUP * rows), F32),
            pltpu.VMEM((6, rows, GROUP * rows), F32),
            pltpu.VMEM((6, rows, GROUP * rows), BF16),
            *[pltpu.VMEM((2, rows, kvw), BF16)] * 5,
            pltpu.VMEM((nx, 2, 2 * cut, kvw), BF16),
            pltpu.VMEM((2, 2 * cut, kvw), F32),
            pltpu.VMEM((2, 2, cut, kvw), BF16),
            pltpu.VMEM((2, cut, kvw), BF16),
            pltpu.VMEM((nz, 2, cut, kvw), BF16),
            pltpu.VMEM((2, cut, kvw), F32),
            pltpu.VMEM((2 * nx, 2, cut, kvw), F32),
            *sems(32),
        ],
        compiler_params=params(1),
        name="attend",
    )(query, upstream, kv, ra, rb)

    ba, bb = swap(cha, chb, shift, -1, n, 2 + n // 2)
    tot = tot + ba.astype(F32) + bb.astype(F32)
    key_grad = tot[0].astype(BF16)
    value_total = tot[1].astype(BF16)

    reps = lax.axis_size("rep")
    hop = 2 ** (STEP % (reps.bit_length() - 1))
    input_grad, new_weight = pl.pallas_call(
        functools.partial(update_kernel, n, hop, scale),
        out_shape=(sds((rows, model), BF16), sds((deep, kvw), F32)),
        in_specs=[VM] * 4,
        out_specs=(VM,) * 2,
        scratch_shapes=[
            pltpu.VMEM((nx, rows, kvw), BF16),
            pltpu.VMEM((nx, rows, model // nx), BF16),
            pltpu.VMEM((nz, 2, deep, kvw), BF16),
            pltpu.VMEM((nz, 2, deep, kvw), BF16),
            pltpu.VMEM((2, deep, kvw), F32),
            *[pltpu.VMEM((deep, kvw), BF16)] * 4,
            *sems(32),
        ],
        compiler_params=params(2),
        name="update",
    )(value_total, tt, wk, weight)
    return input_grad[None], dq[None], key_grad[None], new_weight[None]


def solution(mesh):
    p3 = P("rep", "seq", None)
    return jax.shard_map(
        shards,
        mesh=mesh,
        in_specs=(p3,) * 5 + (P(),),
        out_specs=(p3,) * 4,
        check_vma=False,
    )
```

```python
import functools
import jax
import jax.numpy as jnp
from jax import lax
from jax.experimental import pallas as pl
from jax.experimental.pallas import tpu as pltpu
from jax.sharding import PartitionSpec as P

HEADS = 16
KV_HEADS = 4
HD = 128
BLOCK_TOKENS = 128
STEP = 4
LEARN_RATE = 2.0
MASKED = -1e30
GROUP = HEADS // KV_HEADS
MESH = pl.DeviceIdType.MESH
F32 = jnp.float32
BF16 = jnp.bfloat16


def grid_of(n):
    return {64: (4, 8), 16: (2, 4), 8: (2, 2)}[n]


class Place:
    def __init__(self, n, send_sem, recv_sem):
        self.n = n
        self.nx, self.nz = grid_of(n)
        self.me = lax.axis_index("seq")
        self.x = self.me // (2 * self.nz)
        self.z = lax.rem(self.me // 2, self.nz)
        self.y = lax.rem(self.me, 2)
        self.send_sem, self.recv_sem = send_sem, recv_sem
        self.taken = 0
        self.started = []

    def at(self, x, z, y):
        return x * (2 * self.nz) + z * 2 + y

    def xs(self, d):
        return lax.rem(self.x + d + self.nx, self.nx)

    def zs(self, d):
        return lax.rem(self.z + d + self.nz, self.nz)

    def slot(self, count=1):
        first = self.taken
        self.taken += count
        return first

    def copy(self, src, dst, target, slot, recv_slot=None, axis="seq"):
        return pltpu.make_async_remote_copy(
            src_ref=src,
            dst_ref=dst,
            send_sem=self.send_sem.at[slot],
            recv_sem=self.recv_sem.at[slot if recv_slot is None else recv_slot],
            device_id={axis: target},
            device_id_type=MESH,
        )

    def send(self, src, dst, target, slot, axis="seq"):
        made = self.copy(src, dst, target, slot, axis=axis)
        made.start()
        self.started.append(made)
        return made

    def drain(self):
        for made in self.started:
            made.wait_send()
        self.started = []

    def greet(self, near=True, rep=False, first=False):
        barrier = pltpu.get_barrier_semaphore()
        peers = [{"seq": self.at(self.xs(d), self.z, self.y)} for d in range(1, self.nx)]
        peers += [{"seq": self.at(self.x, self.zs(d), self.y)} for d in range(1, self.nz)]
        peers += [{"seq": self.at(self.x, self.z, 1 - self.y)}]
        if near:
            peers += [{"seq": lax.rem(self.me + d, self.n)} for d in (1, self.n - 1)]
        if rep:
            reps = lax.axis_size("rep")
            here = lax.axis_index("rep")
            peers += [{"rep": lax.rem(here + d, reps)} for d in (rep, reps - rep)]
        for peer in peers:
            pl.semaphore_signal(barrier, inc=1, device_id=peer, device_id_type=MESH)
        if first:
            @pl.when(self.me == 0)
            def _():
                for p in range(1, 2 * self.nx):
                    pl.semaphore_signal(
                        barrier, inc=1, device_id={"seq": self.at(p // 2, 0, p % 2)},
                        device_id_type=MESH,
                    )

            @pl.when((self.z == 0) & (self.me != 0))
            def _():
                pl.semaphore_signal(barrier, inc=1, device_id={"seq": 0}, device_id_type=MESH)

        count = len(peers)
        if first:
            more = jnp.where(self.z == 0, 1, 0)
            count = count + jnp.where(self.me == 0, 2 * self.nx - 1, more)
        pl.semaphore_wait(barrier, count)


class Spread:
    def __init__(self, pl_, src, dst):
        self.p, self.src, self.dst = pl_, src, dst
        p = pl_
        self.rows = src.shape[0] // (2 * p.nx)
        self.piece = p.x * 2 + p.y
        self.a = p.slot(2 * p.nx)
        self.b = p.slot(p.nz)
        self.c = p.slot()
        self.d = p.slot(p.nx)

    def cut(self, ref, index, rows=None):
        rows = rows or self.rows
        return ref.at[pl.ds(pl.multiple_of(index * rows, rows), rows)]

    def one(self, p):
        first = []
        for i in range(1, 2 * p.nx):
            first.append(
                p.copy(
                    self.src.at[pl.ds(i * self.rows, self.rows)],
                    self.dst.at[pl.ds(i * self.rows, self.rows)],
                    p.at(i // 2, 0, i % 2), self.a + i, self.a,
                )
            )

        @pl.when(p.me == 0)
        def _():
            for made in first:
                made.start()
            self.dst[pl.ds(0, self.rows)] = self.src[pl.ds(0, self.rows)]
        self.first = first

    def two(self, p):
        mine = self.cut(self.dst, self.piece)
        second = [
            p.copy(mine, mine, p.at(p.x, d, p.y), self.b + d, self.b) for d in range(1, p.nz)
        ]

        @pl.when((p.z == 0) & (p.me != 0))
        def _():
            self.first[0].wait_recv()

        @pl.when(p.z == 0)
        def _():
            for made in second:
                made.start()
        self.second = second

    def three(self, p):
        mine = self.cut(self.dst, self.piece)

        @pl.when(p.z != 0)
        def _():
            self.second[0].wait_recv()
        self.third = p.send(mine, mine, p.at(p.x, p.z, 1 - p.y), self.c)

    def four(self, p):
        self.third.wait_recv()
        pair = self.cut(self.dst, p.x, 2 * self.rows)
        self.fourth = [
            p.send(pair, pair, p.at(p.xs(d), p.z, p.y), self.d + d) for d in range(1, p.nx)
        ]

    def end(self, p):
        for made in self.fourth:
            made.wait_recv()

        @pl.when(p.me == 0)
        def _():
            for made in self.first:
                made.wait_send()

        @pl.when(p.z == 0)
        def _():
            for made in self.second:
                made.wait_send()


class Collect:
    def __init__(self, p, given, c):
        self.p, self.given = p, given
        self.g1, self.r1, self.g2, self.r2, self.g3, self.r3, self.g4 = c
        self.rows = given.shape[0] // p.nx
        self.cut = self.rows // 2
        self.a, self.b = p.slot(p.nx), p.slot()
        self.c, self.d = p.slot(p.nz), p.slot(2 * p.nx)

    def one(self, p):
        def part(index):
            return pl.ds(pl.multiple_of(index * self.rows, self.rows), self.rows)

        self.first = [
            p.send(
                self.given.at[part(p.xs(d))], self.g1.at[p.x],
                p.at(p.xs(d), p.z, p.y), self.a + d,
            )
            for d in range(1, p.nx)
        ]
        self.r1[...] = self.given[part(p.x)].astype(F32)

    def two(self, p):
        acc = self.r1[...]
        for d in range(1, p.nx):
            self.first[d - 1].wait_recv()
            acc = acc + self.g1[p.xs(-d)].astype(F32)
        self.r1[...] = acc
        self.g2[0] = self.half(1 - p.y).astype(BF16)
        self.second = p.send(self.g2.at[0], self.g2.at[1], p.at(p.x, p.z, 1 - p.y), self.b)

    def half(self, y):
        return self.r1[pl.ds(pl.multiple_of(y * self.cut, self.cut), self.cut)]

    def up(self, d):
        return self.p.copy(self.r2, self.g3.at[d], self.p.at(self.p.x, 0, self.p.y), self.c + d)

    def home(self, d):
        return self.p.copy(self.r3, self.g4.at[d], 0, self.d + d)

    def three(self, p):
        self.second.wait_recv()
        self.r3[...] = self.half(p.y) + self.g2[1].astype(F32)
        self.r2[...] = self.r3[...].astype(BF16)
        self.third = self.up(p.z)

        @pl.when(p.z != 0)
        def _():
            self.third.start()

    def four(self, p):
        self.fourth = self.home(p.x * 2 + p.y)

        @pl.when(p.z == 0)
        def _():
            for d in range(1, p.nz):
                self.up(d).wait_recv()
            tally = self.r3[...]
            for d in range(1, p.nz):
                tally = tally + self.g3[d].astype(F32)
            self.r3[...] = tally

            @pl.when(p.me != 0)
            def _():
                self.fourth.start()

    def end(self, p, total):
        @pl.when(p.me == 0)
        def _():
            for d in range(1, 2 * p.nx):
                self.home(d).wait_recv()
            at = pl.ds(0, self.cut)
            total[at] = total[at] + self.r3[...]
            for d in range(1, 2 * p.nx):
                at = pl.ds(d * self.cut, self.cut)
                total[at] = total[at] + self.g4[d]

        @pl.when(p.z != 0)
        def _():
            self.third.wait_send()

        @pl.when((p.z == 0) & (p.me != 0))
        def _():
            self.fourth.wait_send()


def collect_scratch(nx, nz, rows, kvw):
    cut = rows // nx // 2
    return [
        pltpu.VMEM((nx, 2 * cut, kvw), BF16),
        pltpu.VMEM((2 * cut, kvw), F32),
        pltpu.VMEM((2, cut, kvw), BF16),
        pltpu.VMEM((cut, kvw), BF16),
        pltpu.VMEM((nz, cut, kvw), BF16),
        pltpu.VMEM((cut, kvw), F32),
        pltpu.VMEM((2 * nx, cut, kvw), F32),
    ]


NT = (((1,), (1,)), ((), ()))
TN = (((0,), (0,)), ((), ()))
NN = (((1,), (0,)), ((), ()))


def mm(a, b, dims):
    return lax.dot_general(a, b, dims, preferred_element_type=F32)


def lanes(g):
    return pl.ds(pl.multiple_of(g * HD, HD), HD)


def gather_kernel(
    n, scale, tok, key, wl, q, cot, ka, kb,
    val, wk, tt, low, ks, qs, cs, vtot, dva, dvb,
    pbuf, rbuf, sc, out_l, out_r, out_g, in_l, in_r,
    c1, c2, c3, c4, c5, c6, c7, send_sem, recv_sem,
):
    p = Place(n, send_sem, recv_sem)
    nx, nz = p.nx, p.nz
    width = tok.shape[1] // nx
    half = nz // 2
    p.greet(first=True)

    right = p.at(p.x, p.zs(1), p.y)
    left = p.at(p.x, p.zs(-1), p.y)
    after = lax.rem(p.me + 1, n)
    before = lax.rem(p.me + n - 1, n)

    def shard(dz, k):
        return p.zs(dz) * 2 + (p.y if k == 0 else 1 - p.y)

    rs = [[p.slot() for _ in range(2)] for _ in range(half)]
    ls = [[p.slot() for _ in range(2)] for _ in range(half)]
    hops_r = [[None, None] for _ in range(half)]
    hops_l = [[None, None] for _ in range(half)]

    def relay(s, k):
        src_r = wl if (s == 0 and k == 0) else wk.at[shard(-s, k)]
        src_l = wl if (s == 0 and k == 0) else wk.at[shard(s, k)]
        if s < half - 1 or k == 0:
            hops_r[s][k] = p.send(src_r, wk.at[shard(-s, k)], right, rs[s][k])
        if s < half - 1 or k == 1:
            hops_l[s][k] = p.send(src_l, wk.at[shard(s, k)], left, ls[s][k])

    def arrived(s):
        for k in range(2):
            for hops in (hops_r, hops_l):
                if hops[s][k] is not None:
                    hops[s][k].wait_recv()
            if s + 1 < half:
                relay(s + 1, k)

    keys0 = Spread(p, key, ks.at[3])
    keys0.one(p)
    other = p.send(wl, wk.at[shard(0, 0)], p.at(p.x, p.z, 1 - p.y), p.slot())
    relay(0, 0)
    key_right = p.send(key, ks.at[0], after, p.slot())
    key_left = p.send(key, ks.at[2], before, p.slot())
    cols = [p.slot() for _ in range(nx)]
    moved = []
    for d in range(1, nx):
        to = p.xs(d)
        part = tok.at[:, pl.ds(pl.multiple_of(to * width, width), width)]
        moved.append(p.send(part, tt.at[p.x], p.at(to, p.z, p.y), cols[d]))
    wk[shard(0, 0)] = wl[...]
    tt[p.x] = tok[:, pl.ds(pl.multiple_of(p.x * width, width), width)]
    ks[1] = key[...]
    ks[4] = ka[...]
    ks[5] = kb[...]
    for g in range(KV_HEADS):
        for r in range(GROUP):
            at = pl.ds((g * GROUP + r) * HD, HD)
            to = pl.ds(r * BLOCK_TOKENS, BLOCK_TOKENS)
            qs[g, to] = q[:, at]
            cs[g, to] = cot[:, at]
    score = HD ** -0.5
    first_ok = jnp.where(p.me == 0, MASKED, 0.0)
    last_ok = jnp.where(p.me == n - 1, MASKED, 0.0)

    def scores(s):
        def body(g, _):
            t = mm(ks[s, :, lanes(g)], qs[g], NT) * score
            if s == 0:
                t = t + first_ok
            if s == 2:
                t = t + last_ok
            sc[g, s] = t
            return 0
        lax.fori_loop(0, KV_HEADS, body, 0)

    def soften(g):
        high = None
        for s in range(6):
            m = jnp.max(sc[g, s], axis=0, keepdims=True)
            high = m if high is None else jnp.maximum(high, m)
        total = None
        for s in range(6):
            e = jnp.exp(sc[g, s] - high)
            sc[g, s] = e
            m = jnp.sum(e, axis=0, keepdims=True)
            total = m if total is None else total + m
        inv = 1.0 / total
        for s in range(6):
            w = (sc[g, s] * inv).astype(BF16)
            low[g, s] = w
            dv = mm(w, cs[g], NN)
            if s == 1:
                vtot[:, lanes(g)] = dv
            else:
                to = {0: out_l, 2: out_r, 3: out_g, 4: dva, 5: dvb}[s]
                to[:, lanes(g)] = dv.astype(BF16)

    scores(1)
    other.wait_recv()
    relay(0, 1)
    keys0.two(p)
    scores(4)
    scores(5)
    if half > 1:
        arrived(0)
    keys0.three(p)
    key_right.wait_recv()
    scores(0)
    keys0.four(p)
    key_left.wait_recv()
    scores(2)
    if half > 2:
        arrived(1)
    keys0.end(p)
    scores(3)
    for s in range(2, half - 1):
        arrived(s)

    def groups(first, last):
        lax.fori_loop(first, last, lambda g, _: (soften(g), 0)[1], 0)

    groups(0, KV_HEADS)
    to_left = p.send(out_l, in_r, before, p.slot())
    to_right = p.send(out_r, in_l, after, p.slot())
    sums0 = Collect(p, out_g, (c1, c2, c3, c4, c5, c6, c7))
    sums0.one(p)
    arrived(half - 1)
    for made in moved:
        made.wait_recv()
    weight = wk[...].reshape(2 * nz * wk.shape[1], wk.shape[2])
    sums = [p.slot() for _ in range(nx)]
    parts = []
    for d in range(1, nx):
        to = p.xs(d)
        part = jnp.dot(tt[to], weight, preferred_element_type=F32) * scale
        pbuf[to] = part.astype(BF16)
        parts.append(p.send(pbuf.at[to], rbuf.at[p.x], p.at(to, p.z, p.y), sums[d]))
    pown = jnp.dot(tt[p.x], weight, preferred_element_type=F32) * scale
    sums0.two(p)
    to_left.wait_recv()
    to_right.wait_recv()
    vtot[...] = vtot[...] + in_l[...].astype(F32) + in_r[...].astype(F32)
    sums0.three(p)
    for d in range(1, nx):
        parts[d - 1].wait_recv()
        pown = pown + rbuf[p.xs(-d)].astype(F32)
    val[...] = pown.astype(BF16)
    sums0.four(p)
    sums0.end(p, vtot)
    p.drain()


def update_kernel(
    n, hop, scale, qs, cs, low, ks, val, va, vb, vtot, da, db, tt, wk, weight,
    dq, ig, nw, ktot, dka, dkb,
    vt, vs, gw, delta, vt4, igs, dsend, drecv, own, ys, yr, us, ur,
    out_l, out_r, out_g, in_l, in_r, c1, c2, c3, c4, c5, c6, c7, send_sem, recv_sem,
):
    p = Place(n, send_sem, recv_sem)
    nx, nz = p.nx, p.nz
    width = tt.shape[2]
    deep = width // nz
    after = lax.rem(p.me + 1, n)
    before = lax.rem(p.me + n - 1, n)
    vt[...] = (vtot[...] + da[...].astype(F32) + db[...].astype(F32)).astype(BF16)
    p.greet(rep=hop, first=True)
    base = p.slot(nx)
    sent = [p.send(vt, vt4.at[p.x], p.at(p.xs(d), p.z, p.y), base + d) for d in range(1, nx)]
    vals0 = Spread(p, val, vs.at[3])
    vals0.one(p)
    val_right = p.send(val, vs.at[0], after, p.slot())
    val_left = p.send(val, vs.at[2], before, p.slot())
    vt4[p.x] = vt[...]
    vs[1] = val[...]
    vs[4] = va[...]
    vs[5] = vb[...]
    delta[...] = jnp.zeros(delta.shape, F32)

    def grade(s):
        def body(g, _):
            t = mm(vs[s, :, lanes(g)], cs[g], NT)
            gw[g, s] = t
            delta[g] = delta[g] + jnp.sum(low[g, s].astype(F32) * t, axis=0, keepdims=True)
            return 0
        lax.fori_loop(0, KV_HEADS, body, 0)

    grade(1)
    vals0.two(p)
    grade(4)
    vals0.three(p)
    for made in sent:
        made.wait_recv()
    grads = vt4[...].reshape(nx * BLOCK_TOKENS, vt.shape[1])

    def change(block):
        rows = tt[:, :, pl.ds(pl.multiple_of(block * deep, deep), deep)]
        rows = rows.reshape(nx * BLOCK_TOKENS, deep)
        return mm(rows, grads, TN) * scale

    zbase = p.slot(nz)
    zs = []
    for d in sorted(range(1, nz), key=lambda d: -min(d, nz - d)):
        to = p.zs(d)
        part = change(to).astype(BF16)
        dsend[to] = part.reshape(dsend.shape[1:])
        zs.append(p.send(dsend.at[to], drecv.at[p.z], p.at(p.x, to, p.y), zbase + d))
    own[...] = change(p.z).reshape(own.shape)
    vals0.four(p)
    ibase = p.slot(nx)
    whole = wk[...].reshape(width, wk.shape[2])
    here = pl.ds(pl.multiple_of(p.x * width, width), width)
    backs = []
    for d in range(1, nx):
        to = p.xs(d)
        igs[to] = (mm(vt4[to], whole, NT) * scale).astype(BF16)
        backs.append(p.send(igs.at[to], ig.at[:, here], p.at(to, p.z, p.y), ibase + d))
    ig[:, here] = (mm(vt4[p.x], whole, NT) * scale).astype(BF16)
    grade(5)
    val_right.wait_recv()
    grade(0)
    val_left.wait_recv()
    grade(2)
    vals0.end(p)
    grade(3)
    score = HD ** -0.5

    def group(g, _):
        back = None
        for s in range(6):
            ds = (low[g, s].astype(F32) * (gw[g, s] - delta[g]) * score).astype(BF16)
            dk = mm(ds, qs[g], NN)
            if s == 1:
                ktot[:, lanes(g)] = dk
            else:
                to = {0: out_l, 2: out_r, 3: out_g, 4: dka, 5: dkb}[s]
                to[:, lanes(g)] = dk.astype(BF16)
            part = mm(ks[s, :, lanes(g)], ds, TN)
            back = part if back is None else back + part
        for r in range(GROUP):
            piece = back[:, r * BLOCK_TOKENS:(r + 1) * BLOCK_TOKENS]
            dq[:, lanes(g * GROUP + r)] = piece.T.astype(BF16)
        return 0

    lax.fori_loop(0, KV_HEADS, group, 0)
    to_left = p.send(out_l, in_r, before, p.slot())
    to_right = p.send(out_r, in_l, after, p.slot())
    sums0 = Collect(p, out_g, (c1, c2, c3, c4, c5, c6, c7))
    sums0.one(p)
    for made in zs:
        made.wait_recv()
    acc = own[...]
    for d in range(1, nz):
        acc = acc + drecv[p.zs(-d)].astype(F32)
    own[...] = acc
    ys[...] = own[1 - p.y].astype(BF16)
    yc = p.send(ys, yr, p.at(p.x, p.z, 1 - p.y), p.slot())
    sums0.two(p)
    yc.wait_recv()
    updated = weight[...] - LEARN_RATE * (own[p.y] + yr[...].astype(F32))
    nw[...] = updated
    us[...] = updated.astype(BF16)
    reps = lax.axis_size("rep")
    rc = p.send(us, ur, lax.rem(lax.axis_index("rep") + hop, reps), p.slot(), axis="rep")
    sums0.three(p)
    to_left.wait_recv()
    to_right.wait_recv()
    ktot[...] = ktot[...] + in_l[...].astype(F32) + in_r[...].astype(F32)
    sums0.four(p)
    rc.wait_recv()
    nw[...] = 0.5 * (nw[...] + ur[...].astype(F32))
    sums0.end(p, ktot)
    for made in backs:
        made.wait_recv()
    p.drain()


VM = pl.BlockSpec(memory_space=pltpu.VMEM)


def sems(count):
    return [pltpu.SemaphoreType.DMA((count,)), pltpu.SemaphoreType.DMA((count,))]


def params(which, mib=60):
    return pltpu.CompilerParams(
        collective_id=which, has_side_effects=True, vmem_limit_bytes=mib * 2**20
    )


def sds(shape, dtype):
    return jax.ShapeDtypeStruct(shape, dtype)


def swap_kernel(n, c, signs, *refs):
    count = len(signs)
    given, taken = refs[: 2 * count], refs[2 * count: 4 * count]
    send_sem, recv_sem = refs[4 * count:]
    me = lax.axis_index("seq")
    peers = [lax.rem(me + d + n, n) for d in (c, -c, c + 1, -c - 1)]
    barrier = pltpu.get_barrier_semaphore()
    for peer in peers:
        pl.semaphore_signal(barrier, inc=1, device_id={"seq": peer}, device_id_type=MESH)
    pl.semaphore_wait(barrier, 4)
    made = []
    for i in range(2 * count):
        sign = signs[i // 2]
        to = peers[0 if sign > 0 else 1] if i % 2 == 0 else peers[3 if sign > 0 else 2]
        made.append(
            pltpu.make_async_remote_copy(
                src_ref=given[i], dst_ref=taken[i],
                send_sem=send_sem.at[i], recv_sem=recv_sem.at[i],
                device_id={"seq": to}, device_id_type=MESH,
            )
        )
        made[-1].start()
    for copy in made:
        copy.wait()


def swap(arrays, signs, shift, n, first_id):
    anywhere = pl.BlockSpec(memory_space=pl.ANY)

    def branch(c):
        return pl.pallas_call(
            functools.partial(swap_kernel, n, c, signs),
            out_shape=tuple(sds(a.shape, a.dtype) for a in arrays),
            in_specs=[anywhere] * len(arrays),
            out_specs=(anywhere,) * len(arrays),
            scratch_shapes=sems(len(arrays)),
            compiler_params=pltpu.CompilerParams(
                collective_id=first_id + c, has_side_effects=True
            ),
            name=f"swap_{c}",
        )

    return lax.switch(shift - 1, [branch(c) for c in range(1, n // 2)], *arrays)


def shards(inputs, queries, key_heads, cotangent, value_weight, random_blocks):
    n = lax.axis_size("seq")
    nx, nz = grid_of(n)
    tokens, query, key = inputs[0], queries[0], key_heads[0]
    upstream, weight = cotangent[0], value_weight[0]
    rows, model = tokens.shape
    kvw = key.shape[1]
    qw = query.shape[1]
    deep = weight.shape[0]
    scale = model ** -0.5
    weight_low = weight.astype(BF16)
    offset = lax.rem(n - random_blocks[0, 0], n)
    shift = jnp.minimum(offset, n - 1 - offset)
    block = sds((rows, kvw), BF16)
    total = sds((rows, kvw), F32)
    scratch = [pltpu.VMEM((rows, kvw), BF16)] * 5 + collect_scratch(nx, nz, rows, kvw)
    stack = sds((KV_HEADS, GROUP * rows, HD), BF16)

    ka, kb = swap((key, key), (1,), shift, n, 1)

    val, wk, tt, low, ks, qs, cs, vtot, dva, dvb = pl.pallas_call(
        functools.partial(gather_kernel, n, scale),
        out_shape=(
            block,
            sds((2 * nz, deep, kvw), BF16),
            sds((nx, rows, model // nx), BF16),
            sds((KV_HEADS, 6, rows, GROUP * rows), BF16),
            sds((6, rows, kvw), BF16),
            stack, stack, total, block, block,
        ),
        in_specs=[VM] * 7,
        out_specs=(VM,) * 10,
        scratch_shapes=[
            pltpu.VMEM((nx, rows, kvw), BF16),
            pltpu.VMEM((nx, rows, kvw), BF16),
            pltpu.VMEM((KV_HEADS, 6, rows, GROUP * rows), F32),
            *scratch,
            *sems(112),
        ],
        compiler_params=params(0),
        name="gather",
    )(tokens, key, weight_low, query, upstream, ka, kb)

    va, vb, da, db = swap((val, val, dva, dvb), (1, -1), shift, n, n // 2)

    reps = lax.axis_size("rep")
    hop = 2 ** (STEP % (reps.bit_length() - 1))
    dq, input_grad, new_weight, ktot, dka, dkb = pl.pallas_call(
        functools.partial(update_kernel, n, hop, scale),
        out_shape=(
            sds((rows, qw), BF16), sds((rows, model), BF16), sds((deep, kvw), F32),
            total, block, block,
        ),
        in_specs=[VM] * 13,
        out_specs=(VM,) * 6,
        scratch_shapes=[
            pltpu.VMEM((rows, kvw), BF16),
            pltpu.VMEM((6, rows, kvw), BF16),
            pltpu.VMEM((KV_HEADS, 6, rows, GROUP * rows), F32),
            pltpu.VMEM((KV_HEADS, 1, GROUP * rows), F32),
            pltpu.VMEM((nx, rows, kvw), BF16),
            pltpu.VMEM((nx, rows, model // nx), BF16),
            pltpu.VMEM((nz, 2, deep, kvw), BF16),
            pltpu.VMEM((nz, 2, deep, kvw), BF16),
            pltpu.VMEM((2, deep, kvw), F32),
            *[pltpu.VMEM((deep, kvw), BF16)] * 4,
            *scratch,
            *sems(80),
        ],
        compiler_params=params(1),
        name="update",
    )(qs, cs, low, ks, val, va, vb, vtot, da, db, tt, wk, weight)

    ba, bb = swap((dka, dkb), (-1,), shift, n, n - 1)
    key_grad = (ktot + ba.astype(F32) + bb.astype(F32)).astype(BF16)
    return input_grad[None], dq[None], key_grad[None], new_weight[None]


def solution(mesh):
    p3 = P("rep", "seq", None)
    return jax.shard_map(
        shards,
        mesh=mesh,
        in_specs=(p3,) * 5 + (P(),),
        out_specs=(p3,) * 4,
        check_vma=False,
    )
```

```python
import functools
import jax
import jax.numpy as jnp
from jax import lax
from jax.experimental import pallas as pl
from jax.experimental.pallas import tpu as pltpu
from jax.sharding import PartitionSpec as P

HEADS = 16
KV_HEADS = 4
HD = 128
BLOCK_TOKENS = 128
STEP = 4
LEARN_RATE = 2.0
MASKED = -1e30
GROUP = HEADS // KV_HEADS
MESH = pl.DeviceIdType.MESH
F32 = jnp.float32
BF16 = jnp.bfloat16


def grid_of(n):
    return {64: (4, 8), 16: (2, 4), 8: (2, 2)}[n]


class Place:
    def __init__(self, n, send_sem, recv_sem):
        self.n = n
        self.nx, self.nz = grid_of(n)
        self.me = lax.axis_index("seq")
        self.x = self.me // (2 * self.nz)
        self.z = lax.rem(self.me // 2, self.nz)
        self.y = lax.rem(self.me, 2)
        self.send_sem, self.recv_sem = send_sem, recv_sem
        self.taken = 0
        self.started = []

    def at(self, x, z, y):
        return x * (2 * self.nz) + z * 2 + y

    def xs(self, d):
        return lax.rem(self.x + d + self.nx, self.nx)

    def zs(self, d):
        return lax.rem(self.z + d + self.nz, self.nz)

    def plane(self, sign=1):
        out = []
        for i in range(1, 2 * self.nx):
            y = self.y if i % 2 == 0 else 1 - self.y
            out.append((i, self.xs(sign * (i // 2)), y))
        return out

    def slot(self, count=1):
        first = self.taken
        self.taken += count
        return first

    def copy(self, src, dst, target, slot, recv_slot=None, axis="seq"):
        return pltpu.make_async_remote_copy(
            src_ref=src,
            dst_ref=dst,
            send_sem=self.send_sem.at[slot],
            recv_sem=self.recv_sem.at[slot if recv_slot is None else recv_slot],
            device_id={axis: target},
            device_id_type=MESH,
        )

    def send(self, src, dst, target, slot, axis="seq"):
        made = self.copy(src, dst, target, slot, axis=axis)
        made.start()
        self.started.append(made)
        return made

    def drain(self):
        for made in self.started:
            made.wait_send()
        self.started = []

    def greet(self, near=True, rep=False, first=False):
        barrier = pltpu.get_barrier_semaphore()
        peers = [{"seq": self.at(x, self.z, y)} for _, x, y in self.plane()]
        peers += [{"seq": self.at(self.x, self.zs(d), self.y)} for d in range(1, self.nz)]
        if near:
            peers += [{"seq": lax.rem(self.me + d, self.n)} for d in (1, self.n - 1)]
        if rep:
            reps = lax.axis_size("rep")
            here = lax.axis_index("rep")
            peers += [{"rep": lax.rem(here + d, reps)} for d in (rep, reps - rep)]
        for peer in peers:
            pl.semaphore_signal(barrier, inc=1, device_id=peer, device_id_type=MESH)
        if first:
            @pl.when(self.me == 0)
            def _():
                for p in range(1, 2 * self.nx):
                    pl.semaphore_signal(
                        barrier, inc=1, device_id={"seq": self.at(p // 2, 0, p % 2)},
                        device_id_type=MESH,
                    )

            @pl.when((self.z == 0) & (self.me != 0))
            def _():
                pl.semaphore_signal(barrier, inc=1, device_id={"seq": 0}, device_id_type=MESH)

        count = len(peers)
        if first:
            more = jnp.where(self.z == 0, 1, 0)
            count = count + jnp.where(self.me == 0, 2 * self.nx - 1, more)
        pl.semaphore_wait(barrier, count)


class Spread:
    def __init__(self, pl_, src, dst):
        self.p, self.src, self.dst = pl_, src, dst
        p = pl_
        self.rows = src.shape[0] // (2 * p.nx)
        self.piece = p.x * 2 + p.y
        self.a = p.slot(2 * p.nx)
        self.b = p.slot(p.nz)
        self.c = p.slot(2 * p.nx)

    def cut(self, ref, index, rows=None):
        rows = rows or self.rows
        return ref.at[pl.ds(pl.multiple_of(index * rows, rows), rows)]

    def one(self, p):
        first = []
        for i in range(1, 2 * p.nx):
            first.append(
                p.copy(
                    self.src.at[pl.ds(i * self.rows, self.rows)],
                    self.dst.at[pl.ds(i * self.rows, self.rows)],
                    p.at(i // 2, 0, i % 2), self.a + i, self.a,
                )
            )

        @pl.when(p.me == 0)
        def _():
            for made in first:
                made.start()
            self.dst[pl.ds(0, self.rows)] = self.src[pl.ds(0, self.rows)]
        self.first = first

    def two(self, p):
        mine = self.cut(self.dst, self.piece)
        second = [
            p.copy(mine, mine, p.at(p.x, d, p.y), self.b + d, self.b) for d in range(1, p.nz)
        ]

        @pl.when((p.z == 0) & (p.me != 0))
        def _():
            self.first[0].wait_recv()

        @pl.when(p.z == 0)
        def _():
            for made in second:
                made.start()
        self.second = second

    def three(self, p):
        mine = self.cut(self.dst, self.piece)

        @pl.when(p.z != 0)
        def _():
            self.second[0].wait_recv()
        self.third = [
            p.send(mine, mine, p.at(x, p.z, y), self.c + i) for i, x, y in p.plane()
        ]

    def end(self, p):
        for made in self.third:
            made.wait_recv()

        @pl.when(p.me == 0)
        def _():
            for made in self.first:
                made.wait_send()

        @pl.when(p.z == 0)
        def _():
            for made in self.second:
                made.wait_send()


class Collect:
    def __init__(self, p, given, c):
        self.p, self.given = p, given
        self.g1, self.r2, self.g3, self.r3, self.g4 = c
        self.cut = given.shape[0] // (2 * p.nx)
        self.a = p.slot(2 * p.nx)
        self.c, self.d = p.slot(p.nz), p.slot(2 * p.nx)

    def part(self, x, y):
        return pl.ds(pl.multiple_of((x * 2 + y) * self.cut, self.cut), self.cut)

    def one(self, p):
        self.first = [
            p.send(
                self.given.at[self.part(x, y)], self.g1.at[p.x * 2 + p.y],
                p.at(x, p.z, y), self.a + i,
            )
            for i, x, y in p.plane()
        ]

    def up(self, d):
        return self.p.copy(self.r2, self.g3.at[d], self.p.at(self.p.x, 0, self.p.y), self.c + d)

    def home(self, d):
        return self.p.copy(self.r3, self.g4.at[d], 0, self.d + d)

    def two(self, p):
        acc = self.given[self.part(p.x, p.y)].astype(F32)
        for made, (_, x, y) in zip(self.first, p.plane(-1)):
            made.wait_recv()
            acc = acc + self.g1[x * 2 + y].astype(F32)
        self.r3[...] = acc
        self.r2[...] = acc.astype(BF16)
        self.third = self.up(p.z)

        @pl.when(p.z != 0)
        def _():
            self.third.start()

    def three(self, p):
        self.fourth = self.home(p.x * 2 + p.y)

        @pl.when(p.z == 0)
        def _():
            tally = self.r3[...]
            for d in range(1, p.nz):
                self.up(d).wait_recv()
                tally = tally + self.g3[d].astype(F32)
            self.r3[...] = tally

            @pl.when(p.me != 0)
            def _():
                self.fourth.start()

    def end(self, p, total):
        @pl.when(p.me == 0)
        def _():
            at = pl.ds(0, self.cut)
            total[at] = total[at] + self.r3[...]
            for d in range(1, 2 * p.nx):
                self.home(d).wait_recv()
                at = pl.ds(d * self.cut, self.cut)
                total[at] = total[at] + self.g4[d]

        @pl.when(p.z != 0)
        def _():
            self.third.wait_send()

        @pl.when((p.z == 0) & (p.me != 0))
        def _():
            self.fourth.wait_send()


def collect_scratch(nx, nz, rows, kvw):
    cut = rows // nx // 2
    return [
        pltpu.VMEM((2 * nx, cut, kvw), BF16),
        pltpu.VMEM((cut, kvw), BF16),
        pltpu.VMEM((nz, cut, kvw), BF16),
        pltpu.VMEM((cut, kvw), F32),
        pltpu.VMEM((2 * nx, cut, kvw), F32),
    ]


NT = (((1,), (1,)), ((), ()))
TN = (((0,), (0,)), ((), ()))
NN = (((1,), (0,)), ((), ()))


def mm(a, b, dims):
    return lax.dot_general(a, b, dims, preferred_element_type=F32)


def lanes(g):
    return pl.ds(pl.multiple_of(g * HD, HD), HD)


def gather_kernel(
    n, scale, tok, key, wl, q, cot, ka, kb,
    val, wk, tt, low, ks, qs, cs, vtot, dva, dvb,
    pbuf, rbuf, sc, peak, mass, out_l, out_r, out_g, in_l, in_r,
    c1, c2, c3, c4, c5, send_sem, recv_sem,
):
    p = Place(n, send_sem, recv_sem)
    nx, nz = p.nx, p.nz
    width = tok.shape[1] // nx
    half = nz // 2
    p.greet(first=True)

    right = p.at(p.x, p.zs(1), p.y)
    left = p.at(p.x, p.zs(-1), p.y)
    after = lax.rem(p.me + 1, n)
    before = lax.rem(p.me + n - 1, n)

    def shard(dz, k):
        return p.zs(dz) * 2 + (p.y if k == 0 else 1 - p.y)

    rs = [[p.slot() for _ in range(2)] for _ in range(half)]
    ls = [[p.slot() for _ in range(2)] for _ in range(half)]
    hops_r = [[None, None] for _ in range(half)]
    hops_l = [[None, None] for _ in range(half)]

    def relay(s, k):
        src_r = wl if (s == 0 and k == 0) else wk.at[shard(-s, k)]
        src_l = wl if (s == 0 and k == 0) else wk.at[shard(s, k)]
        if s < half - 1 or k == 0:
            hops_r[s][k] = p.send(src_r, wk.at[shard(-s, k)], right, rs[s][k])
        if s < half - 1 or k == 1:
            hops_l[s][k] = p.send(src_l, wk.at[shard(s, k)], left, ls[s][k])

    def arrived(s):
        for k in range(2):
            for hops in (hops_r, hops_l):
                if hops[s][k] is not None:
                    hops[s][k].wait_recv()
            if s + 1 < half:
                relay(s + 1, k)

    keys0 = Spread(p, key, ks.at[3])
    keys0.one(p)
    other = p.send(wl, wk.at[shard(0, 0)], p.at(p.x, p.z, 1 - p.y), p.slot())
    relay(0, 0)
    key_right = p.send(key, ks.at[0], after, p.slot())
    key_left = p.send(key, ks.at[2], before, p.slot())
    cols = [p.slot() for _ in range(nx)]
    moved = []
    for d in range(1, nx):
        to = p.xs(d)
        part = tok.at[:, pl.ds(pl.multiple_of(to * width, width), width)]
        moved.append(p.send(part, tt.at[p.x], p.at(to, p.z, p.y), cols[d]))
    wk[shard(0, 0)] = wl[...]
    tt[p.x] = tok[:, pl.ds(pl.multiple_of(p.x * width, width), width)]
    ks[1] = key[...]
    ks[4] = ka[...]
    ks[5] = kb[...]
    for g in range(KV_HEADS):
        for r in range(GROUP):
            at = pl.ds((g * GROUP + r) * HD, HD)
            to = pl.ds(r * BLOCK_TOKENS, BLOCK_TOKENS)
            qs[g, to] = q[:, at]
            cs[g, to] = cot[:, at]
    score = HD ** -0.5
    first_ok = jnp.where(p.me == 0, MASKED, 0.0)
    last_ok = jnp.where(p.me == n - 1, MASKED, 0.0)

    def scores(s):
        def body(g, _):
            t = mm(ks[s, :, lanes(g)], qs[g], NT) * score
            if s == 0:
                t = t + first_ok
            if s == 2:
                t = t + last_ok
            sc[g, s] = t
            return 0
        lax.fori_loop(0, KV_HEADS, body, 0)

    def early(g, _):
        high = None
        for s in (1, 4, 5, 0, 2):
            m = jnp.max(sc[g, s], axis=0, keepdims=True)
            high = m if high is None else jnp.maximum(high, m)
        total = None
        for s in (1, 4, 5, 0, 2):
            e = jnp.exp(sc[g, s] - high)
            sc[g, s] = e
            m = jnp.sum(e, axis=0, keepdims=True)
            total = m if total is None else total + m
        peak[g] = high
        mass[g] = total
        return 0

    def block0(g, _):
        t = mm(ks[3, :, lanes(g)], qs[g], NT) * score
        high = jnp.maximum(peak[g], jnp.max(t, axis=0, keepdims=True))
        e = jnp.exp(t - high)
        fade = jnp.exp(peak[g] - high)
        inv = 1.0 / (fade * mass[g] + jnp.sum(e, axis=0, keepdims=True))
        mass[g] = fade * inv
        w = (e * inv).astype(BF16)
        low[g, 3] = w
        out_g[:, lanes(g)] = mm(w, cs[g], NN).astype(BF16)
        return 0

    def soften(g, _):
        fade = mass[g]
        for s in (0, 2, 1, 4, 5):
            w = (sc[g, s] * fade).astype(BF16)
            low[g, s] = w
            dv = mm(w, cs[g], NN)
            if s == 1:
                vtot[:, lanes(g)] = dv
            else:
                to = {0: out_l, 2: out_r, 4: dva, 5: dvb}[s]
                to[:, lanes(g)] = dv.astype(BF16)
        return 0

    def groups(body):
        lax.fori_loop(0, KV_HEADS, body, 0)

    scores(1)
    other.wait_recv()
    relay(0, 1)
    keys0.two(p)
    scores(4)
    scores(5)
    if half > 1:
        arrived(0)
    keys0.three(p)
    key_right.wait_recv()
    scores(0)
    key_left.wait_recv()
    scores(2)
    if half > 2:
        arrived(1)
    groups(early)
    keys0.end(p)
    groups(block0)
    sums0 = Collect(p, out_g, (c1, c2, c3, c4, c5))
    sums0.one(p)
    for s in range(2, half - 1):
        arrived(s)
    groups(soften)
    to_left = p.send(out_l, in_r, before, p.slot())
    to_right = p.send(out_r, in_l, after, p.slot())
    sums0.two(p)
    arrived(half - 1)
    for made in moved:
        made.wait_recv()
    weight = wk[...].reshape(2 * nz * wk.shape[1], wk.shape[2])
    sums = [p.slot() for _ in range(nx)]
    parts = []
    for d in range(1, nx):
        to = p.xs(d)
        part = jnp.dot(tt[to], weight, preferred_element_type=F32) * scale
        pbuf[to] = part.astype(BF16)
        parts.append(p.send(pbuf.at[to], rbuf.at[p.x], p.at(to, p.z, p.y), sums[d]))
    pown = jnp.dot(tt[p.x], weight, preferred_element_type=F32) * scale
    to_left.wait_recv()
    to_right.wait_recv()
    vtot[...] = vtot[...] + in_l[...].astype(F32) + in_r[...].astype(F32)
    sums0.three(p)
    for d in range(1, nx):
        parts[d - 1].wait_recv()
        pown = pown + rbuf[p.xs(-d)].astype(F32)
    val[...] = pown.astype(BF16)
    sums0.end(p, vtot)
    p.drain()


def update_kernel(
    n, hop, scale, qs, cs, low, ks, val, va, vb, vtot, da, db, tt, wk, weight,
    dq, ig, nw, ktot, dka, dkb,
    vt, vs, gw, delta, vt4, igs, dsend, drecv, own, ys, yr, us, ur,
    out_l, out_r, out_g, in_l, in_r, c1, c2, c3, c4, c5, send_sem, recv_sem,
):
    p = Place(n, send_sem, recv_sem)
    nx, nz = p.nx, p.nz
    width = tt.shape[2]
    deep = width // nz
    after = lax.rem(p.me + 1, n)
    before = lax.rem(p.me + n - 1, n)
    vt[...] = (vtot[...] + da[...].astype(F32) + db[...].astype(F32)).astype(BF16)
    p.greet(rep=hop, first=True)
    base = p.slot(nx)
    sent = [p.send(vt, vt4.at[p.x], p.at(p.xs(d), p.z, p.y), base + d) for d in range(1, nx)]
    vals0 = Spread(p, val, vs.at[3])
    vals0.one(p)
    val_right = p.send(val, vs.at[0], after, p.slot())
    val_left = p.send(val, vs.at[2], before, p.slot())
    vt4[p.x] = vt[...]
    vs[1] = val[...]
    vs[4] = va[...]
    vs[5] = vb[...]
    delta[...] = jnp.zeros(delta.shape, F32)

    def grade(s):
        def body(g, _):
            t = mm(vs[s, :, lanes(g)], cs[g], NT)
            gw[g, s] = t
            delta[g] = delta[g] + jnp.sum(low[g, s].astype(F32) * t, axis=0, keepdims=True)
            return 0
        lax.fori_loop(0, KV_HEADS, body, 0)

    half = nz // 2
    right = p.at(p.x, p.zs(1), p.y)
    left = p.at(p.x, p.zs(-1), p.y)
    rslot, lslot = p.slot(2 * half), p.slot(2 * half)
    hops = {}

    def contribute(block):
        rows = tt[:, :, pl.ds(pl.multiple_of(block * deep, deep), deep)]
        rows = rows.reshape(nx * BLOCK_TOKENS, deep)
        grads = vt4[...].reshape(nx * BLOCK_TOKENS, vt.shape[1])
        own[block] = (mm(rows, grads, TN) * scale).reshape(own.shape[1:])

    def ring(s):
        for k in range(2):
            for side, (first, to) in enumerate(((rslot, right), (lslot, left))):
                block = p.zs(half - s) if side == 0 else p.zs(s - half)
                if s == 0 and k != side:
                    continue
                acc = own[block, k]
                if (side, s - 1, k) in hops:
                    hops[side, s - 1, k].wait_recv()
                    acc = acc + drecv[side, s - 1, k].astype(F32)
                dsend[side, s, k] = acc.astype(BF16)
                hops[side, s, k] = p.send(
                    dsend.at[side, s, k], drecv.at[side, s, k], to, first + 2 * s + k
                )

    ibase = p.slot(nx)
    here = pl.ds(pl.multiple_of(p.x * width, width), width)
    backs = []

    def back_of(to):
        whole = wk[...].reshape(width, wk.shape[2])
        return (mm(vt4[to], whole, NT) * scale).astype(BF16)

    def send_back(d):
        to = p.xs(d)
        igs[to] = back_of(to)
        backs.append(p.send(igs.at[to], ig.at[:, here], p.at(to, p.z, p.y), ibase + d))

    grade(1)
    vals0.two(p)
    grade(4)
    grade(5)
    vals0.three(p)
    for made in sent:
        made.wait_recv()
    contribute(p.zs(half))
    ring(0)
    for d in range(half - 1, 0, -1):
        contribute(p.zs(d))
        contribute(p.zs(-d))
    val_right.wait_recv()
    grade(0)
    val_left.wait_recv()
    grade(2)
    if half > 1:
        ring(1)
    for d in range(1, nx):
        send_back(d)
    contribute(p.z)
    vals0.end(p)
    grade(3)
    if half > 2:
        ring(2)
    score = HD ** -0.5

    def group(g, _):
        back = None
        for s in range(6):
            ds = (low[g, s].astype(F32) * (gw[g, s] - delta[g]) * score).astype(BF16)
            dk = mm(ds, qs[g], NN)
            if s == 1:
                ktot[:, lanes(g)] = dk
            else:
                to = {0: out_l, 2: out_r, 3: out_g, 4: dka, 5: dkb}[s]
                to[:, lanes(g)] = dk.astype(BF16)
            part = mm(ks[s, :, lanes(g)], ds, TN)
            back = part if back is None else back + part
        for r in range(GROUP):
            piece = back[:, r * BLOCK_TOKENS:(r + 1) * BLOCK_TOKENS]
            dq[:, lanes(g * GROUP + r)] = piece.T.astype(BF16)
        return 0

    lax.fori_loop(0, 2, group, 0)
    for s in range(3, half):
        ring(s)
    lax.fori_loop(2, KV_HEADS, group, 0)
    to_left = p.send(out_l, in_r, before, p.slot())
    to_right = p.send(out_r, in_l, after, p.slot())
    sums0 = Collect(p, out_g, (c1, c2, c3, c4, c5))
    sums0.one(p)
    for k in range(2):
        for side in range(2):
            if (side, half - 1, k) in hops:
                hops[side, half - 1, k].wait_recv()
                own[p.z, k] = own[p.z, k] + drecv[side, half - 1, k].astype(F32)
    ys[...] = own[p.z, 1 - p.y].astype(BF16)
    yc = p.send(ys, yr, p.at(p.x, p.z, 1 - p.y), p.slot())
    ig[:, here] = back_of(p.x)
    sums0.two(p)
    yc.wait_recv()
    updated = weight[...] - LEARN_RATE * (own[p.z, p.y] + yr[...].astype(F32))
    nw[...] = updated
    us[...] = updated.astype(BF16)
    reps = lax.axis_size("rep")
    rc = p.send(us, ur, lax.rem(lax.axis_index("rep") + hop, reps), p.slot(), axis="rep")
    to_left.wait_recv()
    to_right.wait_recv()
    ktot[...] = ktot[...] + in_l[...].astype(F32) + in_r[...].astype(F32)
    sums0.three(p)
    rc.wait_recv()
    nw[...] = 0.5 * (nw[...] + ur[...].astype(F32))
    sums0.end(p, ktot)
    for made in backs:
        made.wait_recv()
    p.drain()


VM = pl.BlockSpec(memory_space=pltpu.VMEM)


def sems(count):
    return [pltpu.SemaphoreType.DMA((count,)), pltpu.SemaphoreType.DMA((count,))]


def params(which, mib=60):
    return pltpu.CompilerParams(
        collective_id=which, has_side_effects=True, vmem_limit_bytes=mib * 2**20
    )


def sds(shape, dtype):
    return jax.ShapeDtypeStruct(shape, dtype)


def swap_kernel(n, c, signs, *refs):
    count = len(signs)
    given, taken = refs[: 2 * count], refs[2 * count: 4 * count]
    send_sem, recv_sem = refs[4 * count:]
    me = lax.axis_index("seq")
    peers = [lax.rem(me + d + n, n) for d in (c, -c, c + 1, -c - 1)]
    barrier = pltpu.get_barrier_semaphore()
    for peer in peers:
        pl.semaphore_signal(barrier, inc=1, device_id={"seq": peer}, device_id_type=MESH)
    pl.semaphore_wait(barrier, 4)
    made = []
    for i in range(2 * count):
        sign = signs[i // 2]
        to = peers[0 if sign > 0 else 1] if i % 2 == 0 else peers[3 if sign > 0 else 2]
        made.append(
            pltpu.make_async_remote_copy(
                src_ref=given[i], dst_ref=taken[i],
                send_sem=send_sem.at[i], recv_sem=recv_sem.at[i],
                device_id={"seq": to}, device_id_type=MESH,
            )
        )
        made[-1].start()
    for copy in made:
        copy.wait()


def swap(arrays, signs, shift, n, first_id):
    anywhere = pl.BlockSpec(memory_space=pl.ANY)

    def branch(c):
        return pl.pallas_call(
            functools.partial(swap_kernel, n, c, signs),
            out_shape=tuple(sds(a.shape, a.dtype) for a in arrays),
            in_specs=[anywhere] * len(arrays),
            out_specs=(anywhere,) * len(arrays),
            scratch_shapes=sems(len(arrays)),
            compiler_params=pltpu.CompilerParams(
                collective_id=first_id + c, has_side_effects=True
            ),
            name=f"swap_{c}",
        )

    return lax.switch(shift - 1, [branch(c) for c in range(1, n // 2)], *arrays)


def shards(inputs, queries, key_heads, cotangent, value_weight, random_blocks):
    n = lax.axis_size("seq")
    nx, nz = grid_of(n)
    tokens, query, key = inputs[0], queries[0], key_heads[0]
    upstream, weight = cotangent[0], value_weight[0]
    rows, model = tokens.shape
    kvw = key.shape[1]
    qw = query.shape[1]
    deep = weight.shape[0]
    scale = model ** -0.5
    weight_low = weight.astype(BF16)
    offset = lax.rem(n - random_blocks[0, 0], n)
    shift = jnp.minimum(offset, n - 1 - offset)
    block = sds((rows, kvw), BF16)
    total = sds((rows, kvw), F32)
    scratch = [pltpu.VMEM((rows, kvw), BF16)] * 5 + collect_scratch(nx, nz, rows, kvw)
    stack = sds((KV_HEADS, GROUP * rows, HD), BF16)

    ka, kb = swap((key, key), (1,), shift, n, 1)

    val, wk, tt, low, ks, qs, cs, vtot, dva, dvb = pl.pallas_call(
        functools.partial(gather_kernel, n, scale),
        out_shape=(
            block,
            sds((2 * nz, deep, kvw), BF16),
            sds((nx, rows, model // nx), BF16),
            sds((KV_HEADS, 6, rows, GROUP * rows), BF16),
            sds((6, rows, kvw), BF16),
            stack, stack, total, block, block,
        ),
        in_specs=[VM] * 7,
        out_specs=(VM,) * 10,
        scratch_shapes=[
            pltpu.VMEM((nx, rows, kvw), BF16),
            pltpu.VMEM((nx, rows, kvw), BF16),
            pltpu.VMEM((KV_HEADS, 6, rows, GROUP * rows), F32),
            pltpu.VMEM((KV_HEADS, 1, GROUP * rows), F32),
            pltpu.VMEM((KV_HEADS, 1, GROUP * rows), F32),
            *scratch,
            *sems(112),
        ],
        compiler_params=params(0),
        name="gather",
    )(tokens, key, weight_low, query, upstream, ka, kb)

    va, vb, da, db = swap((val, val, dva, dvb), (1, -1), shift, n, n // 2)

    reps = lax.axis_size("rep")
    hop = 2 ** (STEP % (reps.bit_length() - 1))
    dq, input_grad, new_weight, ktot, dka, dkb = pl.pallas_call(
        functools.partial(update_kernel, n, hop, scale),
        out_shape=(
            sds((rows, qw), BF16), sds((rows, model), BF16), sds((deep, kvw), F32),
            total, block, block,
        ),
        in_specs=[VM] * 13,
        out_specs=(VM,) * 6,
        scratch_shapes=[
            pltpu.VMEM((rows, kvw), BF16),
            pltpu.VMEM((6, rows, kvw), BF16),
            pltpu.VMEM((KV_HEADS, 6, rows, GROUP * rows), F32),
            pltpu.VMEM((KV_HEADS, 1, GROUP * rows), F32),
            pltpu.VMEM((nx, rows, kvw), BF16),
            pltpu.VMEM((nx, rows, model // nx), BF16),
            pltpu.VMEM((2, nz // 2, 2, deep, kvw), BF16),
            pltpu.VMEM((2, nz // 2, 2, deep, kvw), BF16),
            pltpu.VMEM((nz, 2, deep, kvw), F32),
            *[pltpu.VMEM((deep, kvw), BF16)] * 4,
            *scratch,
            *sems(80),
        ],
        compiler_params=params(1),
        name="update",
    )(qs, cs, low, ks, val, va, vb, vtot, da, db, tt, wk, weight)

    ba, bb = swap((dka, dkb), (-1,), shift, n, n - 1)
    key_grad = (ktot + ba.astype(F32) + bb.astype(F32)).astype(BF16)
    return input_grad[None], dq[None], key_grad[None], new_weight[None]


def solution(mesh):
    p3 = P("rep", "seq", None)
    return jax.shard_map(
        shards,
        mesh=mesh,
        in_specs=(p3,) * 5 + (P(),),
        out_specs=(p3,) * 4,
        check_vma=False,
    )
```

```python
import functools
import jax
import jax.numpy as jnp
from jax import lax
from jax.experimental import pallas as pl
from jax.experimental.pallas import tpu as pltpu
from jax.sharding import PartitionSpec as P

HEADS = 16
KV_HEADS = 4
HD = 128
BLOCK_TOKENS = 128
STEP = 4
LEARN_RATE = 2.0
MASKED = -1e30
GROUP = HEADS // KV_HEADS
MESH = pl.DeviceIdType.MESH
F32 = jnp.float32
BF16 = jnp.bfloat16


def grid_of(n):
    return {64: (4, 8), 16: (2, 4), 8: (2, 2)}[n]


class Place:
    def __init__(self, n, send_sem, recv_sem):
        self.n = n
        self.nx, self.nz = grid_of(n)
        self.me = lax.axis_index("seq")
        self.x = self.me // (2 * self.nz)
        self.z = lax.rem(self.me // 2, self.nz)
        self.y = lax.rem(self.me, 2)
        self.send_sem, self.recv_sem = send_sem, recv_sem
        self.taken = 0
        self.started = []

    def at(self, x, z, y):
        return x * (2 * self.nz) + z * 2 + y

    def xs(self, d):
        return lax.rem(self.x + d + self.nx, self.nx)

    def zs(self, d):
        return lax.rem(self.z + d + self.nz, self.nz)

    def plane(self, sign=1):
        out = []
        for i in range(1, 2 * self.nx):
            y = self.y if i % 2 == 0 else 1 - self.y
            out.append((i, self.xs(sign * (i // 2)), y))
        return out

    def slot(self, count=1):
        first = self.taken
        self.taken += count
        return first

    def copy(self, src, dst, target, slot, recv_slot=None, axis="seq"):
        return pltpu.make_async_remote_copy(
            src_ref=src,
            dst_ref=dst,
            send_sem=self.send_sem.at[slot],
            recv_sem=self.recv_sem.at[slot if recv_slot is None else recv_slot],
            device_id={axis: target},
            device_id_type=MESH,
        )

    def send(self, src, dst, target, slot, axis="seq"):
        made = self.copy(src, dst, target, slot, axis=axis)
        made.start()
        self.started.append(made)
        return made

    def drain(self):
        for made in self.started:
            made.wait_send()
        self.started = []

    def greet(self, near=True, rep=False, first=False, cross=False):
        barrier = pltpu.get_barrier_semaphore()
        peers = [{"seq": self.at(x, self.z, y)} for _, x, y in self.plane()]
        peers += [{"seq": self.at(self.x, self.zs(d), self.y)} for d in range(1, self.nz)]
        if cross:
            peers += [{"seq": self.at(self.x, self.zs(d), 1 - self.y)} for d in (1, -1)]
        if near:
            peers += [{"seq": lax.rem(self.me + d, self.n)} for d in (1, self.n - 1)]
        if rep:
            reps = lax.axis_size("rep")
            here = lax.axis_index("rep")
            peers += [{"rep": lax.rem(here + d, reps)} for d in (rep, reps - rep)]
        for peer in peers:
            pl.semaphore_signal(barrier, inc=1, device_id=peer, device_id_type=MESH)
        if first:
            @pl.when(self.me == 0)
            def _():
                for p in range(1, 2 * self.nx):
                    pl.semaphore_signal(
                        barrier, inc=1, device_id={"seq": self.at(p // 2, 0, p % 2)},
                        device_id_type=MESH,
                    )

            @pl.when((self.z == 0) & (self.me != 0))
            def _():
                pl.semaphore_signal(barrier, inc=1, device_id={"seq": 0}, device_id_type=MESH)

        count = len(peers)
        if first:
            more = jnp.where(self.z == 0, 1, 0)
            count = count + jnp.where(self.me == 0, 2 * self.nx - 1, more)
        pl.semaphore_wait(barrier, count)


class Spread:
    def __init__(self, pl_, src, dst):
        self.p, self.src, self.dst = pl_, src, dst
        p = pl_
        self.rows = src.shape[0] // (2 * p.nx)
        self.piece = p.x * 2 + p.y
        self.a = p.slot(2 * p.nx)
        self.b = p.slot(p.nz)
        self.c = p.slot(2 * p.nx)

    def cut(self, ref, index, rows=None):
        rows = rows or self.rows
        return ref.at[pl.ds(pl.multiple_of(index * rows, rows), rows)]

    def one(self, p):
        first = []
        for i in range(1, 2 * p.nx):
            first.append(
                p.copy(
                    self.src.at[pl.ds(i * self.rows, self.rows)],
                    self.dst.at[pl.ds(i * self.rows, self.rows)],
                    p.at(i // 2, 0, i % 2), self.a + i, self.a,
                )
            )

        @pl.when(p.me == 0)
        def _():
            for made in first:
                made.start()
            self.dst[pl.ds(0, self.rows)] = self.src[pl.ds(0, self.rows)]
        self.first = first

    def two(self, p):
        mine = self.cut(self.dst, self.piece)
        second = [
            p.copy(mine, mine, p.at(p.x, d, p.y), self.b + d, self.b) for d in range(1, p.nz)
        ]

        @pl.when((p.z == 0) & (p.me != 0))
        def _():
            self.first[0].wait_recv()

        @pl.when(p.z == 0)
        def _():
            for made in second:
                made.start()
        self.second = second

    def three(self, p):
        mine = self.cut(self.dst, self.piece)

        @pl.when(p.z != 0)
        def _():
            self.second[0].wait_recv()
        self.third = [
            p.send(mine, mine, p.at(x, p.z, y), self.c + i) for i, x, y in p.plane()
        ]

    def end(self, p):
        for made in self.third:
            made.wait_recv()

        @pl.when(p.me == 0)
        def _():
            for made in self.first:
                made.wait_send()

        @pl.when(p.z == 0)
        def _():
            for made in self.second:
                made.wait_send()


class Collect:
    def __init__(self, p, given, c):
        self.p, self.given = p, given
        self.g1, self.r2, self.g3, self.r3 = c
        self.cut = given.shape[0] // (2 * p.nx)
        self.a = p.slot(2 * p.nx)
        self.c = p.slot(p.nz)

    def part(self, x, y):
        return pl.ds(pl.multiple_of((x * 2 + y) * self.cut, self.cut), self.cut)

    def one(self, p):
        self.first = [
            p.send(
                self.given.at[self.part(x, y)], self.g1.at[p.x * 2 + p.y],
                p.at(x, p.z, y), self.a + i,
            )
            for i, x, y in p.plane()
        ]

    def up(self, d):
        return self.p.copy(self.r2, self.g3.at[d], self.p.at(self.p.x, 0, self.p.y), self.c + d)

    def two(self, p):
        acc = self.given[self.part(p.x, p.y)].astype(F32)
        for made, (_, x, y) in zip(self.first, p.plane(-1)):
            made.wait_recv()
            acc = acc + self.g1[x * 2 + y].astype(F32)
        self.r3[...] = acc
        self.r2[...] = acc.astype(BF16)
        self.third = self.up(p.z)

        @pl.when(p.z != 0)
        def _():
            self.third.start()

    def three(self, p):
        @pl.when(p.z == 0)
        def _():
            tally = self.r3[...]
            for d in range(1, p.nz):
                self.up(d).wait_recv()
                tally = tally + self.g3[d].astype(F32)
            self.r3[...] = tally

        @pl.when(p.z != 0)
        def _():
            self.third.wait_send()


def collect_scratch(nx, nz, rows, kvw):
    cut = rows // nx // 2
    return [
        pltpu.VMEM((2 * nx, cut, kvw), BF16),
        pltpu.VMEM((cut, kvw), BF16),
        pltpu.VMEM((nz, cut, kvw), BF16),
    ]


NT = (((1,), (1,)), ((), ()))
TN = (((0,), (0,)), ((), ()))
NN = (((1,), (0,)), ((), ()))


def mm(a, b, dims):
    return lax.dot_general(a, b, dims, preferred_element_type=F32)


def lanes(g):
    return pl.ds(pl.multiple_of(g * HD, HD), HD)


def gather_kernel(
    n, scale, tok, key, weight_f32, val, wk, tt, kn,
    wl, pbuf, rbuf, send_sem, recv_sem,
):
    p = Place(n, send_sem, recv_sem)
    nx, nz = p.nx, p.nz
    width = tok.shape[1] // nx
    half = nz // 2
    wl[...] = weight_f32[...].astype(BF16)
    p.greet(first=True)

    right = p.at(p.x, p.zs(1), p.y)
    left = p.at(p.x, p.zs(-1), p.y)
    after = lax.rem(p.me + 1, n)
    before = lax.rem(p.me + n - 1, n)

    def shard(dz, k):
        return p.zs(dz) * 2 + (p.y if k == 0 else 1 - p.y)

    rs = [[p.slot() for _ in range(2)] for _ in range(half)]
    ls = [[p.slot() for _ in range(2)] for _ in range(half)]
    hops_r = [[None, None] for _ in range(half)]
    hops_l = [[None, None] for _ in range(half)]

    def relay(s, k):
        src_r = wl if (s == 0 and k == 0) else wk.at[shard(-s, k)]
        src_l = wl if (s == 0 and k == 0) else wk.at[shard(s, k)]
        if s < half - 1 or k == 0:
            hops_r[s][k] = p.send(src_r, wk.at[shard(-s, k)], right, rs[s][k])
        if s < half - 1 or k == 1:
            hops_l[s][k] = p.send(src_l, wk.at[shard(s, k)], left, ls[s][k])

    def arrived(s):
        for k in range(2):
            for hops in (hops_r, hops_l):
                if hops[s][k] is not None:
                    hops[s][k].wait_recv()
            if s + 1 < half:
                relay(s + 1, k)

    keys0 = Spread(p, key, kn.at[2])
    keys0.one(p)
    other = p.send(wl, wk.at[shard(0, 0)], p.at(p.x, p.z, 1 - p.y), p.slot())
    relay(0, 0)
    key_right = p.send(key, kn.at[0], after, p.slot())
    key_left = p.send(key, kn.at[1], before, p.slot())
    cols = [p.slot() for _ in range(nx)]
    moved = []
    for d in range(1, nx):
        to = p.xs(d)
        part = tok.at[:, pl.ds(pl.multiple_of(to * width, width), width)]
        moved.append(p.send(part, tt.at[p.x], p.at(to, p.z, p.y), cols[d]))
    wk[shard(0, 0)] = wl[...]
    tt[p.x] = tok[:, pl.ds(pl.multiple_of(p.x * width, width), width)]
    other.wait_recv()
    relay(0, 1)
    for s in range(half - 1):
        arrived(s)
        if s == max(half - 3, 0):
            keys0.two(p)
    keys0.three(p)
    arrived(half - 1)
    for made in moved:
        made.wait_recv()
    weight = wk[...].reshape(2 * nz * wk.shape[1], wk.shape[2])
    sums = [p.slot() for _ in range(nx)]
    parts = []
    for d in range(1, nx):
        to = p.xs(d)
        part = jnp.dot(tt[to], weight, preferred_element_type=F32) * scale
        pbuf[to] = part.astype(BF16)
        parts.append(p.send(pbuf.at[to], rbuf.at[p.x], p.at(to, p.z, p.y), sums[d]))
    pown = jnp.dot(tt[p.x], weight, preferred_element_type=F32) * scale
    keys0.end(p)
    key_right.wait_recv()
    key_left.wait_recv()
    for d in range(1, nx):
        parts[d - 1].wait_recv()
        pown = pown + rbuf[p.xs(-d)].astype(F32)
    val[...] = pown.astype(BF16)
    p.drain()


def attend_kernel(
    n, q, cot, key, kn, ka, kb, val, va, vb,
    dq, vtot, ktot, dva, dvb, dka, dkb, r3,
    ks, vs, qs, cs, sc, low, gw, delta, dsb,
    vout_l, vout_r, vout_g, vin_l, vin_r, kout_l, kout_r, kout_g, kin_l, kin_r,
    c1, c2, c3, d1, d2, d3, send_sem, recv_sem,
):
    p = Place(n, send_sem, recv_sem)
    nx, nz = p.nx, p.nz
    after = lax.rem(p.me + 1, n)
    before = lax.rem(p.me + n - 1, n)
    p.greet(first=True)
    vals0 = Spread(p, val, vs.at[3])
    vals0.one(p)
    val_right = p.send(val, vs.at[0], after, p.slot())
    val_left = p.send(val, vs.at[2], before, p.slot())
    for s, (kr, vr) in {1: (key, val), 4: (ka, va), 5: (kb, vb)}.items():
        ks[s] = kr[...]
        vs[s] = vr[...]
    ks[0] = kn[0]
    ks[2] = kn[1]
    ks[3] = kn[2]
    for g in range(KV_HEADS):
        for r in range(GROUP):
            at = pl.ds((g * GROUP + r) * HD, HD)
            to = pl.ds(r * BLOCK_TOKENS, BLOCK_TOKENS)
            qs[g, to] = q[:, at]
            cs[g, to] = cot[:, at]
    score = HD ** -0.5
    first_ok = jnp.where(p.me == 0, MASKED, 0.0)
    last_ok = jnp.where(p.me == n - 1, MASKED, 0.0)

    def groups(body, first=0, last=KV_HEADS):
        lax.fori_loop(first, last, body, 0)

    def soften(g, _):
        high = None
        for s in range(6):
            t = mm(ks[s, :, lanes(g)], qs[g], NT) * score
            if s == 0:
                t = t + first_ok
            if s == 2:
                t = t + last_ok
            sc[s] = t
            m = jnp.max(t, axis=0, keepdims=True)
            high = m if high is None else jnp.maximum(high, m)
        total = None
        for s in range(6):
            e = jnp.exp(sc[s] - high)
            sc[s] = e
            m = jnp.sum(e, axis=0, keepdims=True)
            total = m if total is None else total + m
        inv = 1.0 / total
        for s in range(6):
            w = (sc[s] * inv).astype(BF16)
            low[g, s] = w
            if s in (0, 2, 3):
                to = {0: vout_l, 2: vout_r, 3: vout_g}[s]
                to[:, lanes(g)] = mm(w, cs[g], NN).astype(BF16)
        return 0

    def others(g, _):
        vtot[:, lanes(g)] = mm(low[g, 1], cs[g], NN)
        dva[:, lanes(g)] = mm(low[g, 4], cs[g], NN).astype(BF16)
        dvb[:, lanes(g)] = mm(low[g, 5], cs[g], NN).astype(BF16)
        return 0

    delta[...] = jnp.zeros(delta.shape, F32)

    def grade(s):
        def body(g, _):
            t = mm(vs[s, :, lanes(g)], cs[g], NT)
            gw[g, s] = t
            delta[g] = delta[g] + jnp.sum(low[g, s].astype(F32) * t, axis=0, keepdims=True)
            return 0
        groups(body)

    groups(soften, 0, 2)
    vals0.two(p)
    groups(soften, 2)
    sums_v = Collect(p, vout_g, (c1, c2, c3, r3.at[0]))
    sums_v.one(p)
    v_left = p.send(vout_l, vin_r, before, p.slot())
    v_right = p.send(vout_r, vin_l, after, p.slot())
    vals0.three(p)
    grade(1)
    grade(4)
    grade(5)
    val_right.wait_recv()
    grade(0)
    val_left.wait_recv()
    grade(2)
    vals0.end(p)
    grade(3)
    ahead = (3, 0, 2)

    def signal(g, s):
        return (low[g, s].astype(F32) * (gw[g, s] - delta[g]) * score).astype(BF16)

    def group_ahead(slots, g, _):
        for s in slots:
            i = ahead.index(s)
            ds = signal(g, s)
            dsb[g, i] = ds
            to = {0: kout_l, 2: kout_r, 3: kout_g}[s]
            to[:, lanes(g)] = mm(ds, qs[g], NN).astype(BF16)
        return 0

    def group(g, _):
        back = None
        for s in range(6):
            if s in ahead:
                ds = dsb[g, ahead.index(s)]
            else:
                ds = signal(g, s)
                dk = mm(ds, qs[g], NN)
                if s == 1:
                    ktot[:, lanes(g)] = dk
                else:
                    to = {4: dka, 5: dkb}[s]
                    to[:, lanes(g)] = dk.astype(BF16)
            part = mm(ks[s, :, lanes(g)], ds, TN)
            back = part if back is None else back + part
        for r in range(GROUP):
            piece = back[:, r * BLOCK_TOKENS:(r + 1) * BLOCK_TOKENS]
            dq[:, lanes(g * GROUP + r)] = piece.T.astype(BF16)
        return 0

    groups(functools.partial(group_ahead, (3,)))
    sums_k = Collect(p, kout_g, (d1, d2, d3, r3.at[1]))
    sums_k.one(p)
    groups(functools.partial(group_ahead, (0, 2)))
    k_left = p.send(kout_l, kin_r, before, p.slot())
    k_right = p.send(kout_r, kin_l, after, p.slot())
    sums_v.two(p)
    groups(group, 0, 2)
    sums_k.two(p)
    groups(others)
    groups(group, 2)
    for made in (v_left, v_right, k_left, k_right):
        made.wait_recv()
    vtot[...] = vtot[...] + vin_l[...].astype(F32) + vin_r[...].astype(F32)
    ktot[...] = ktot[...] + kin_l[...].astype(F32) + kin_r[...].astype(F32)
    sums_v.three(p)
    sums_k.three(p)
    p.drain()


def update_kernel(
    n, hop, scale, vtot, da, db, home, homes, tt, wk, weight, ig, nw,
    vsum, vt, vt4, igs, dsend, drecv, fin, own, ys, yr, us, ur, send_sem, recv_sem,
):
    p = Place(n, send_sem, recv_sem)
    nx, nz = p.nx, p.nz
    width = tt.shape[2]
    deep = width // nz
    vsum[...] = vtot[...] + da[...].astype(F32) + db[...].astype(F32)

    @pl.when(p.me == 0)
    def _():
        cut = home.shape[1]
        for d in range(2 * nx):
            at = pl.ds(d * cut, cut)
            vsum[at] = vsum[at] + (home[0] if d == 0 else homes[d, 0])

    vt[...] = vsum[...].astype(BF16)
    p.greet(near=False, rep=hop, cross=True)
    base = p.slot(nx)
    sent = [p.send(vt, vt4.at[p.x], p.at(p.xs(d), p.z, p.y), base + d) for d in range(1, nx)]
    vt4[p.x] = vt[...]
    half = nz // 2
    right = p.at(p.x, p.zs(1), p.y)
    left = p.at(p.x, p.zs(-1), p.y)
    rslot, lslot = p.slot(2 * half), p.slot(2 * half)
    fslot, gslot = p.slot(4), p.slot(4)
    hops = {}

    def contribute(block):
        rows = tt[:, :, pl.ds(pl.multiple_of(block * deep, deep), deep)]
        rows = rows.reshape(nx * BLOCK_TOKENS, deep)
        grads = vt4[...].reshape(nx * BLOCK_TOKENS, vt.shape[1])
        own[block] = (mm(rows, grads, TN) * scale).reshape(own.shape[1:])

    def ring(s):
        for k in range(2):
            for side, (first, to) in enumerate(((rslot, right), (lslot, left))):
                block = p.zs(half - s) if side == 0 else p.zs(s - half)
                if s == 0 and k != side:
                    continue
                acc = own[block, k]
                if (side, s - 1, k) in hops:
                    hops[side, s - 1, k].wait_recv()
                    acc = acc + drecv[side, s - 1, k].astype(F32)
                dsend[side, s, k] = acc.astype(BF16)
                if s == half - 1:
                    done = p.copy(
                        dsend.at[side, s, k], fin.at[side, p.y],
                        p.at(p.x, p.zs(1 - 2 * side), k),
                        fslot + 2 * side + k, gslot + 2 * side + p.y,
                    )
                    done.start()
                    p.started.append(done)
                    continue
                hops[side, s, k] = p.send(
                    dsend.at[side, s, k], drecv.at[side, s, k], to, first + 2 * s + k
                )

    ibase = p.slot(nx)
    here = pl.ds(pl.multiple_of(p.x * width, width), width)
    backs = []

    def back_of(to):
        whole = wk[...].reshape(width, wk.shape[2])
        return (mm(vt4[to], whole, NT) * scale).astype(BF16)

    def send_back(d):
        to = p.xs(d)
        igs[to] = back_of(to)
        backs.append(p.send(igs.at[to], ig.at[:, here], p.at(to, p.z, p.y), ibase + d))

    for made in sent:
        made.wait_recv()
    contribute(p.zs(half))
    ring(0)
    for d in range(half - 1, 0, -1):
        contribute(p.zs(d))
        contribute(p.zs(-d))
    contribute(p.z)
    ys[...] = own[p.z, 1 - p.y].astype(BF16)
    yc = p.send(ys, yr, p.at(p.x, p.z, 1 - p.y), p.slot())
    waiting = list(range(1, nx))
    for s in range(1, half):
        ring(s)
        if waiting:
            send_back(waiting.pop())
    while waiting:
        send_back(waiting.pop())
    ig[:, here] = back_of(p.x)
    yc.wait_recv()
    acc = own[p.z, p.y] + yr[...].astype(F32)
    for side in range(2):
        for y in range(2):
            at = gslot + 2 * side + y
            p.copy(fin.at[side, y], fin.at[side, y], right, at, at).wait_recv()
            acc = acc + fin[side, y].astype(F32)
    updated = weight[...] - LEARN_RATE * acc
    us[...] = updated.astype(BF16)
    reps = lax.axis_size("rep")
    rc = p.send(us, ur, lax.rem(lax.axis_index("rep") + hop, reps), p.slot(), axis="rep")
    rc.wait_recv()
    nw[...] = 0.5 * (updated + ur[...].astype(F32))
    for made in backs:
        made.wait_recv()
    p.drain()


VM = pl.BlockSpec(memory_space=pltpu.VMEM)


def sems(count):
    return [pltpu.SemaphoreType.DMA((count,)), pltpu.SemaphoreType.DMA((count,))]


def params(which, mib=60):
    return pltpu.CompilerParams(
        collective_id=which, has_side_effects=True, vmem_limit_bytes=mib * 2**20
    )


def sds(shape, dtype):
    return jax.ShapeDtypeStruct(shape, dtype)


def swap_kernel(n, c, signs, hop, *refs):
    count = (len(refs) - 4) // 2
    given, home = refs[:count], refs[count]
    taken, homes = refs[count + 1: 2 * count + 1], refs[2 * count + 1]
    send_sem, recv_sem = refs[2 * count + 2:]
    nx, nz = grid_of(n)
    me = lax.axis_index("seq")
    piece = me // (2 * nz) * 2 + lax.rem(me, 2)
    base = lax.rem(me // 2, nz) == 0
    peers = [{"seq": lax.rem(me + d + n, n)} for d in (c, -c, c + 1, -c - 1)]
    targets = []
    for sign in signs:
        targets += [peers[0], peers[3]] if sign > 0 else [peers[1], peers[2]]
    if hop:
        reps = lax.axis_size("rep")
        rep = lax.axis_index("rep")
        peers += [{"rep": lax.rem(rep + d, reps)} for d in (hop, reps - hop)]
        targets.append(peers[4])
    barrier = pltpu.get_barrier_semaphore()
    for peer in peers:
        pl.semaphore_signal(barrier, inc=1, device_id=peer, device_id_type=MESH)

    @pl.when(me == 0)
    def _():
        @pl.loop(1, 2 * nx)
        def _(i):
            to = i // 2 * (2 * nz) + lax.rem(i, 2)
            pl.semaphore_signal(barrier, inc=1, device_id={"seq": to}, device_id_type=MESH)

    @pl.when(base & (me != 0))
    def _():
        pl.semaphore_signal(barrier, inc=1, device_id={"seq": 0}, device_id_type=MESH)

    more = jnp.where(me == 0, 2 * nx - 1, jnp.where(base, 1, 0))
    pl.semaphore_wait(barrier, len(peers) + more)
    made = []
    for i in range(count):
        made.append(
            pltpu.make_async_remote_copy(
                src_ref=given[i], dst_ref=taken[i],
                send_sem=send_sem.at[i], recv_sem=recv_sem.at[i],
                device_id=targets[i], device_id_type=MESH,
            )
        )
        made[-1].start()

    def last(d):
        return pltpu.make_async_remote_copy(
            src_ref=home, dst_ref=homes.at[d],
            send_sem=send_sem.at[count + d], recv_sem=recv_sem.at[count + d],
            device_id={"seq": 0}, device_id_type=MESH,
        )

    @pl.when(base & (me != 0))
    def _():
        last(piece).start()

    for copy in made:
        copy.wait()

    @pl.when(base & (me != 0))
    def _():
        last(piece).wait_send()

    @pl.when(me == 0)
    def _():
        @pl.loop(1, 2 * nx)
        def _(i):
            last(i).wait_recv()


def out_kernel(n, c, signs, *refs):
    count = (len(refs) - 2) // 2
    given, taken = refs[:count], refs[count: 2 * count]
    send_sem, recv_sem = refs[2 * count:]
    me = lax.axis_index("seq")
    peers = [{"seq": lax.rem(me + d + n, n)} for d in (c, -c, c + 1, -c - 1)]
    targets = []
    for sign in signs:
        targets += [peers[0], peers[3]] if sign > 0 else [peers[1], peers[2]]
    barrier = pltpu.get_barrier_semaphore()
    for peer in peers:
        pl.semaphore_signal(barrier, inc=1, device_id=peer, device_id_type=MESH)
    pl.semaphore_wait(barrier, len(peers))
    made = [
        pltpu.make_async_remote_copy(
            src_ref=given[i], dst_ref=taken[i],
            send_sem=send_sem.at[i], recv_sem=recv_sem.at[i],
            device_id=targets[i], device_id_type=MESH,
        )
        for i in range(count)
    ]
    for copy in made:
        copy.start()
    for copy in made:
        copy.wait()


def swap(arrays, signs, shift, n, first_id, hop=0, home=None):
    anywhere = pl.BlockSpec(memory_space=pl.ANY)
    given = list(arrays)
    taken = [sds(a.shape, a.dtype) for a in arrays]
    spare = 0
    if home is not None:
        spare = 2 * grid_of(n)[0]
        given.append(home)
        taken.append(sds((spare, *home.shape), home.dtype))

    def branch(c):
        if home is None:
            body = functools.partial(out_kernel, n, c, signs)
        else:
            body = functools.partial(swap_kernel, n, c, signs, hop)
        return pl.pallas_call(
            body,
            out_shape=tuple(taken),
            in_specs=[anywhere] * len(given),
            out_specs=(anywhere,) * len(taken),
            scratch_shapes=sems(len(arrays) + spare),
            compiler_params=pltpu.CompilerParams(
                collective_id=first_id + c, has_side_effects=True
            ),
            name=f"swap_{c}",
        )

    return lax.switch(shift - 1, [branch(c) for c in range(1, n // 2)], *given)


def shards(inputs, queries, key_heads, cotangent, value_weight, random_blocks):
    n = lax.axis_size("seq")
    nx, nz = grid_of(n)
    tokens, query, key = inputs[0], queries[0], key_heads[0]
    upstream, weight = cotangent[0], value_weight[0]
    rows, model = tokens.shape
    kvw = key.shape[1]
    qw = query.shape[1]
    deep = weight.shape[0]
    scale = model ** -0.5
    offset = lax.rem(n - random_blocks[0, 0], n)
    shift = jnp.minimum(offset, n - 1 - offset)
    block = sds((rows, kvw), BF16)
    total = sds((rows, kvw), F32)
    buffers = [pltpu.VMEM((rows, kvw), BF16)]
    home = sds((2, rows // nx // 2, kvw), F32)

    val, wk, tt, kn = pl.pallas_call(
        functools.partial(gather_kernel, n, scale),
        out_shape=(
            block,
            sds((2 * nz, deep, kvw), BF16),
            sds((nx, rows, model // nx), BF16),
            sds((3, rows, kvw), BF16),
        ),
        in_specs=[VM] * 3,
        out_specs=(VM,) * 4,
        scratch_shapes=[
            pltpu.VMEM((deep, kvw), BF16),
            pltpu.VMEM((nx, rows, kvw), BF16),
            pltpu.VMEM((nx, rows, kvw), BF16),
            *sems(72),
        ],
        compiler_params=params(0),
        name="gather",
    )(tokens, key, weight)

    ka, kb, va, vb = swap((key, key, val, val), (1, 1), shift, n, 3)

    wide = (KV_HEADS, 6, rows, GROUP * rows)
    dq, vtot, ktot, dva, dvb, dka, dkb, r3 = pl.pallas_call(
        functools.partial(attend_kernel, n),
        out_shape=(sds((rows, qw), BF16), total, total, block, block, block, block, home),
        in_specs=[VM] * 9,
        out_specs=(VM,) * 8,
        scratch_shapes=[
            pltpu.VMEM((6, rows, kvw), BF16),
            pltpu.VMEM((6, rows, kvw), BF16),
            pltpu.VMEM((KV_HEADS, GROUP * rows, HD), BF16),
            pltpu.VMEM((KV_HEADS, GROUP * rows, HD), BF16),
            pltpu.VMEM(wide[1:], F32),
            pltpu.VMEM(wide, BF16),
            pltpu.VMEM(wide, F32),
            pltpu.VMEM((KV_HEADS, 1, GROUP * rows), F32),
            pltpu.VMEM((KV_HEADS, 3, rows, GROUP * rows), BF16),
            *buffers * 10,
            *collect_scratch(nx, nz, rows, kvw) * 2,
            *sems(80),
        ],
        compiler_params=params(1),
        name="attend",
    )(query, upstream, key, kn, ka, kb, val, va, vb)

    da, db, ba, bb, homes = swap(
        (dva, dvb, dka, dkb), (-1, -1), shift, n, 3 + n // 2, home=r3
    )
    block0 = jnp.concatenate([r3[None, 1], homes[1:, 1]], axis=0).reshape(rows, kvw)
    block0 = jnp.where(lax.axis_index("seq") == 0, block0, 0.0)
    key_grad = (ktot + ba.astype(F32) + bb.astype(F32) + block0).astype(BF16)

    reps = lax.axis_size("rep")
    hop = 2 ** (STEP % (reps.bit_length() - 1))
    input_grad, new_weight = pl.pallas_call(
        functools.partial(update_kernel, n, hop, scale),
        out_shape=(sds((rows, model), BF16), sds((deep, kvw), F32)),
        in_specs=[VM] * 8,
        out_specs=(VM,) * 2,
        scratch_shapes=[
            pltpu.VMEM((rows, kvw), F32),
            pltpu.VMEM((rows, kvw), BF16),
            pltpu.VMEM((nx, rows, kvw), BF16),
            pltpu.VMEM((nx, rows, model // nx), BF16),
            pltpu.VMEM((2, nz // 2, 2, deep, kvw), BF16),
            pltpu.VMEM((2, nz // 2, 2, deep, kvw), BF16),
            pltpu.VMEM((2, 2, deep, kvw), BF16),
            pltpu.VMEM((nz, 2, deep, kvw), F32),
            *[pltpu.VMEM((deep, kvw), BF16)] * 4,
            *sems(40),
        ],
        compiler_params=params(2),
        name="update",
    )(vtot, da, db, r3, homes, tt, wk, weight)
    return input_grad[None], dq[None], key_grad[None], new_weight[None]


def solution(mesh):
    p3 = P("rep", "seq", None)
    return jax.shard_map(
        shards,
        mesh=mesh,
        in_specs=(p3,) * 5 + (P(),),
        out_specs=(p3,) * 4,
        check_vma=False,
    )
```

```python
import functools
import jax
import jax.numpy as jnp
from jax import lax
from jax.experimental import pallas as pl
from jax.experimental.pallas import tpu as pltpu
from jax.sharding import PartitionSpec as P

HEADS = 16
KV_HEADS = 4
HD = 128
BLOCK_TOKENS = 128
STEP = 4
LEARN_RATE = 2.0
MASKED = -1e30
GROUP = HEADS // KV_HEADS
MESH = pl.DeviceIdType.MESH
F32 = jnp.float32
BF16 = jnp.bfloat16


def grid_of(n):
    return {64: (4, 8), 16: (2, 4), 8: (2, 2)}[n]


class Place:
    def __init__(self, n, send_sem, recv_sem):
        self.n = n
        self.nx, self.nz = grid_of(n)
        self.me = lax.axis_index("seq")
        self.x = self.me // (2 * self.nz)
        self.z = lax.rem(self.me // 2, self.nz)
        self.y = lax.rem(self.me, 2)
        self.send_sem, self.recv_sem = send_sem, recv_sem
        self.taken = 0
        self.started = []

    def at(self, x, z, y):
        return x * (2 * self.nz) + z * 2 + y

    def xs(self, d):
        return lax.rem(self.x + d + self.nx, self.nx)

    def zs(self, d):
        return lax.rem(self.z + d + self.nz, self.nz)

    def plane(self, sign=1):
        out = []
        for i in range(1, 2 * self.nx):
            y = self.y if i % 2 == 0 else 1 - self.y
            out.append((i, self.xs(sign * (i // 2)), y))
        return out

    def slot(self, count=1):
        first = self.taken
        self.taken += count
        return first

    def copy(self, src, dst, target, slot, recv_slot=None, axis="seq"):
        return pltpu.make_async_remote_copy(
            src_ref=src,
            dst_ref=dst,
            send_sem=self.send_sem.at[slot],
            recv_sem=self.recv_sem.at[slot if recv_slot is None else recv_slot],
            device_id={axis: target},
            device_id_type=MESH,
        )

    def send(self, src, dst, target, slot, axis="seq"):
        made = self.copy(src, dst, target, slot, axis=axis)
        made.start()
        self.started.append(made)
        return made

    def drain(self):
        for made in self.started:
            made.wait_send()
        self.started = []

    def greet(self, near=True, rep=False, first=False, cross=False):
        barrier = pltpu.get_barrier_semaphore()
        peers = [{"seq": self.at(x, self.z, y)} for _, x, y in self.plane()]
        peers += [{"seq": self.at(self.x, self.zs(d), self.y)} for d in range(1, self.nz)]
        if cross:
            peers += [{"seq": self.at(self.x, self.zs(d), 1 - self.y)} for d in (1, -1)]
        if near:
            peers += [{"seq": lax.rem(self.me + d, self.n)} for d in (1, self.n - 1)]
        if rep:
            reps = lax.axis_size("rep")
            here = lax.axis_index("rep")
            peers += [{"rep": lax.rem(here + d, reps)} for d in (rep, reps - rep)]
        for peer in peers:
            pl.semaphore_signal(barrier, inc=1, device_id=peer, device_id_type=MESH)
        if first:
            @pl.when(self.me == 0)
            def _():
                for p in range(1, 2 * self.nx):
                    pl.semaphore_signal(
                        barrier, inc=1, device_id={"seq": self.at(p // 2, 0, p % 2)},
                        device_id_type=MESH,
                    )

            @pl.when((self.z == 0) & (self.me != 0))
            def _():
                pl.semaphore_signal(barrier, inc=1, device_id={"seq": 0}, device_id_type=MESH)

        count = len(peers)
        if first:
            more = jnp.where(self.z == 0, 1, 0)
            count = count + jnp.where(self.me == 0, 2 * self.nx - 1, more)
        pl.semaphore_wait(barrier, count)


class Spread:
    def __init__(self, pl_, src, dst):
        self.p, self.src, self.dst = pl_, src, dst
        p = pl_
        self.rows = src.shape[0] // (2 * p.nx)
        self.piece = p.x * 2 + p.y
        self.a = p.slot(2 * p.nx)
        self.b = p.slot(p.nz)
        self.c = p.slot(2 * p.nx)

    def cut(self, ref, index, rows=None):
        rows = rows or self.rows
        return ref.at[pl.ds(pl.multiple_of(index * rows, rows), rows)]

    def one(self, p):
        first = []
        for i in range(1, 2 * p.nx):
            first.append(
                p.copy(
                    self.src.at[pl.ds(i * self.rows, self.rows)],
                    self.dst.at[pl.ds(i * self.rows, self.rows)],
                    p.at(i // 2, 0, i % 2), self.a + i, self.a,
                )
            )

        @pl.when(p.me == 0)
        def _():
            for made in first:
                made.start()
            self.dst[pl.ds(0, self.rows)] = self.src[pl.ds(0, self.rows)]
        self.first = first

    def two(self, p):
        mine = self.cut(self.dst, self.piece)
        second = [
            p.copy(mine, mine, p.at(p.x, d, p.y), self.b + d, self.b) for d in range(1, p.nz)
        ]

        @pl.when((p.z == 0) & (p.me != 0))
        def _():
            self.first[0].wait_recv()

        @pl.when(p.z == 0)
        def _():
            for made in second:
                made.start()
        self.second = second

    def three(self, p):
        mine = self.cut(self.dst, self.piece)

        @pl.when(p.z != 0)
        def _():
            self.second[0].wait_recv()
        self.third = [
            p.send(mine, mine, p.at(x, p.z, y), self.c + i) for i, x, y in p.plane()
        ]

    def end(self, p):
        for made in self.third:
            made.wait_recv()

        @pl.when(p.me == 0)
        def _():
            for made in self.first:
                made.wait_send()

        @pl.when(p.z == 0)
        def _():
            for made in self.second:
                made.wait_send()


class Collect:
    def __init__(self, p, given, c):
        self.p, self.given = p, given
        self.g1, self.r2, self.g3, self.r3 = c
        self.cut = given.shape[0] // (2 * p.nx)
        self.a = p.slot(2 * p.nx)
        self.c = p.slot(p.nz)

    def part(self, x, y):
        return pl.ds(pl.multiple_of((x * 2 + y) * self.cut, self.cut), self.cut)

    def one(self, p):
        self.first = [
            p.send(
                self.given.at[self.part(x, y)], self.g1.at[p.x * 2 + p.y],
                p.at(x, p.z, y), self.a + i,
            )
            for i, x, y in p.plane()
        ]

    def up(self, d):
        return self.p.copy(self.r2, self.g3.at[d], self.p.at(self.p.x, 0, self.p.y), self.c + d)

    def two(self, p):
        acc = self.given[self.part(p.x, p.y)].astype(F32)
        for made, (_, x, y) in zip(self.first, p.plane(-1)):
            made.wait_recv()
            acc = acc + self.g1[x * 2 + y].astype(F32)
        self.r3[...] = acc
        self.r2[...] = acc.astype(BF16)
        self.third = self.up(p.z)

        @pl.when(p.z != 0)
        def _():
            self.third.start()

    def three(self, p):
        @pl.when(p.z == 0)
        def _():
            tally = self.r3[...]
            for d in range(1, p.nz):
                self.up(d).wait_recv()
                tally = tally + self.g3[d].astype(F32)
            self.r3[...] = tally

        @pl.when(p.z != 0)
        def _():
            self.third.wait_send()


def collect_scratch(nx, nz, rows, kvw):
    cut = rows // nx // 2
    return [
        pltpu.VMEM((2 * nx, cut, kvw), BF16),
        pltpu.VMEM((cut, kvw), BF16),
        pltpu.VMEM((nz, cut, kvw), BF16),
    ]


NT = (((1,), (1,)), ((), ()))
TN = (((0,), (0,)), ((), ()))
NN = (((1,), (0,)), ((), ()))


def mm(a, b, dims):
    return lax.dot_general(a, b, dims, preferred_element_type=F32)


def lanes(g):
    return pl.ds(pl.multiple_of(g * HD, HD), HD)


def gather_kernel(
    n, scale, tok, key, weight_f32, val, wk, tt, kn,
    wl, pbuf, rbuf, send_sem, recv_sem,
):
    p = Place(n, send_sem, recv_sem)
    nx, nz = p.nx, p.nz
    width = tok.shape[1] // nx
    half = nz // 2
    wl[...] = weight_f32[...].astype(BF16)
    p.greet(first=True)

    right = p.at(p.x, p.zs(1), p.y)
    left = p.at(p.x, p.zs(-1), p.y)
    after = lax.rem(p.me + 1, n)
    before = lax.rem(p.me + n - 1, n)

    def shard(dz, k):
        return p.zs(dz) * 2 + (p.y if k == 0 else 1 - p.y)

    rs = [[p.slot() for _ in range(2)] for _ in range(half)]
    ls = [[p.slot() for _ in range(2)] for _ in range(half)]
    hops_r = [[None, None] for _ in range(half)]
    hops_l = [[None, None] for _ in range(half)]

    def relay(s, k):
        src_r = wl if (s == 0 and k == 0) else wk.at[shard(-s, k)]
        src_l = wl if (s == 0 and k == 0) else wk.at[shard(s, k)]
        if s < half - 1 or k == 0:
            hops_r[s][k] = p.send(src_r, wk.at[shard(-s, k)], right, rs[s][k])
        if s < half - 1 or k == 1:
            hops_l[s][k] = p.send(src_l, wk.at[shard(s, k)], left, ls[s][k])

    def arrived(s):
        for k in range(2):
            for hops in (hops_r, hops_l):
                if hops[s][k] is not None:
                    hops[s][k].wait_recv()
            if s + 1 < half:
                relay(s + 1, k)

    keys0 = Spread(p, key, kn.at[2])
    keys0.one(p)
    other = p.send(wl, wk.at[shard(0, 0)], p.at(p.x, p.z, 1 - p.y), p.slot())
    relay(0, 0)
    key_right = p.send(key, kn.at[0], after, p.slot())
    key_left = p.send(key, kn.at[1], before, p.slot())
    cols = [p.slot() for _ in range(nx)]
    moved = []
    for d in range(1, nx):
        to = p.xs(d)
        part = tok.at[:, pl.ds(pl.multiple_of(to * width, width), width)]
        moved.append(p.send(part, tt.at[p.x], p.at(to, p.z, p.y), cols[d]))
    wk[shard(0, 0)] = wl[...]
    tt[p.x] = tok[:, pl.ds(pl.multiple_of(p.x * width, width), width)]
    other.wait_recv()
    relay(0, 1)
    for s in range(half - 1):
        arrived(s)
        if s == max(half - 3, 0):
            keys0.two(p)
    keys0.three(p)
    arrived(half - 1)
    for made in moved:
        made.wait_recv()
    weight = wk[...].reshape(2 * nz * wk.shape[1], wk.shape[2])
    sums = [p.slot() for _ in range(nx)]
    parts = []
    for d in range(1, nx):
        to = p.xs(d)
        part = jnp.dot(tt[to], weight, preferred_element_type=F32) * scale
        pbuf[to] = part.astype(BF16)
        parts.append(p.send(pbuf.at[to], rbuf.at[p.x], p.at(to, p.z, p.y), sums[d]))
    pown = jnp.dot(tt[p.x], weight, preferred_element_type=F32) * scale
    keys0.end(p)
    key_right.wait_recv()
    key_left.wait_recv()
    for d in range(1, nx):
        parts[d - 1].wait_recv()
        pown = pown + rbuf[p.xs(-d)].astype(F32)
    val[...] = pown.astype(BF16)
    p.drain()


def attend_kernel(
    n, q, cot, key, kn, ka, kb, val, va, vb,
    dq, vtot, ktot, dva, dvb, dka, dkb, r3,
    ks, vs, qs, cs, sc, low, gw, delta, dsb,
    vout_l, vout_r, vout_g, vin_l, vin_r, kout_l, kout_r, kout_g, kin_l, kin_r,
    c1, c2, c3, d1, d2, d3, send_sem, recv_sem,
):
    p = Place(n, send_sem, recv_sem)
    nx, nz = p.nx, p.nz
    after = lax.rem(p.me + 1, n)
    before = lax.rem(p.me + n - 1, n)
    p.greet(first=True)
    vals0 = Spread(p, val, vs.at[3])
    vals0.one(p)
    val_right = p.send(val, vs.at[0], after, p.slot())
    val_left = p.send(val, vs.at[2], before, p.slot())
    for s, (kr, vr) in {1: (key, val), 4: (ka, va), 5: (kb, vb)}.items():
        ks[s] = kr[...]
        vs[s] = vr[...]
    ks[0] = kn[0]
    ks[2] = kn[1]
    ks[3] = kn[2]
    for g in range(KV_HEADS):
        for r in range(GROUP):
            at = pl.ds((g * GROUP + r) * HD, HD)
            to = pl.ds(r * BLOCK_TOKENS, BLOCK_TOKENS)
            qs[g, to] = q[:, at]
            cs[g, to] = cot[:, at]
    score = HD ** -0.5
    first_ok = jnp.where(p.me == 0, MASKED, 0.0)
    last_ok = jnp.where(p.me == n - 1, MASKED, 0.0)

    def groups(body, first=0, last=KV_HEADS):
        lax.fori_loop(first, last, body, 0)

    def soften(g, _):
        high = None
        for s in range(6):
            t = mm(ks[s, :, lanes(g)], qs[g], NT) * score
            if s == 0:
                t = t + first_ok
            if s == 2:
                t = t + last_ok
            sc[s] = t
            m = jnp.max(t, axis=0, keepdims=True)
            high = m if high is None else jnp.maximum(high, m)
        total = None
        for s in range(6):
            e = jnp.exp(sc[s] - high)
            sc[s] = e
            m = jnp.sum(e, axis=0, keepdims=True)
            total = m if total is None else total + m
        inv = 1.0 / total
        for s in range(6):
            w = (sc[s] * inv).astype(BF16)
            low[g, s] = w
            if s in (0, 2, 3):
                to = {0: vout_l, 2: vout_r, 3: vout_g}[s]
                to[:, lanes(g)] = mm(w, cs[g], NN).astype(BF16)
        return 0

    def others(g, _):
        vtot[:, lanes(g)] = mm(low[g, 1], cs[g], NN)
        dva[:, lanes(g)] = mm(low[g, 4], cs[g], NN).astype(BF16)
        dvb[:, lanes(g)] = mm(low[g, 5], cs[g], NN).astype(BF16)
        return 0

    delta[...] = jnp.zeros(delta.shape, F32)

    def grade(s):
        def body(g, _):
            t = mm(vs[s, :, lanes(g)], cs[g], NT)
            gw[g, s] = t
            delta[g] = delta[g] + jnp.sum(low[g, s].astype(F32) * t, axis=0, keepdims=True)
            return 0
        groups(body)

    groups(soften, 0, 2)
    vals0.two(p)
    groups(soften, 2)
    sums_v = Collect(p, vout_g, (c1, c2, c3, r3.at[0]))
    sums_v.one(p)
    v_left = p.send(vout_l, vin_r, before, p.slot())
    v_right = p.send(vout_r, vin_l, after, p.slot())
    vals0.three(p)
    grade(1)
    grade(4)
    grade(5)
    val_right.wait_recv()
    grade(0)
    val_left.wait_recv()
    grade(2)
    vals0.end(p)
    grade(3)
    ahead = (3, 0, 2)

    def signal(g, s):
        return (low[g, s].astype(F32) * (gw[g, s] - delta[g]) * score).astype(BF16)

    def group_ahead(slots, g, _):
        for s in slots:
            i = ahead.index(s)
            ds = signal(g, s)
            dsb[g, i] = ds
            to = {0: kout_l, 2: kout_r, 3: kout_g}[s]
            to[:, lanes(g)] = mm(ds, qs[g], NN).astype(BF16)
        return 0

    def group(g, _):
        back = None
        for s in range(6):
            if s in ahead:
                ds = dsb[g, ahead.index(s)]
            else:
                ds = signal(g, s)
                dk = mm(ds, qs[g], NN)
                if s == 1:
                    ktot[:, lanes(g)] = dk
                else:
                    to = {4: dka, 5: dkb}[s]
                    to[:, lanes(g)] = dk.astype(BF16)
            part = mm(ks[s, :, lanes(g)], ds, TN)
            back = part if back is None else back + part
        for r in range(GROUP):
            piece = back[:, r * BLOCK_TOKENS:(r + 1) * BLOCK_TOKENS]
            dq[:, lanes(g * GROUP + r)] = piece.T.astype(BF16)
        return 0

    groups(functools.partial(group_ahead, (3,)))
    sums_k = Collect(p, kout_g, (d1, d2, d3, r3.at[1]))
    sums_k.one(p)
    groups(functools.partial(group_ahead, (0, 2)))
    k_left = p.send(kout_l, kin_r, before, p.slot())
    k_right = p.send(kout_r, kin_l, after, p.slot())
    sums_v.two(p)
    groups(group, 0, 2)
    sums_k.two(p)
    groups(others)
    groups(group, 2)
    for made in (v_left, v_right, k_left, k_right):
        made.wait_recv()
    vtot[...] = vtot[...] + vin_l[...].astype(F32) + vin_r[...].astype(F32)
    ktot[...] = ktot[...] + kin_l[...].astype(F32) + kin_r[...].astype(F32)
    sums_v.three(p)
    sums_k.three(p)
    p.drain()


def update_kernel(
    n, hop, scale, vtot, da, db, ktot, ba, bb, home, homes, tt, wk, weight, ig, nw, kg,
    vsum, ksum, vt, vt4, igs, dsend, drecv, fin, own, ys, yr, us, ur, send_sem, recv_sem,
):
    p = Place(n, send_sem, recv_sem)
    nx, nz = p.nx, p.nz
    width = tt.shape[2]
    deep = width // nz
    vsum[...] = vtot[...] + da[...].astype(F32) + db[...].astype(F32)

    @pl.when(p.me == 0)
    def _():
        cut = home.shape[1]
        for d in range(2 * nx):
            at = pl.ds(d * cut, cut)
            vsum[at] = vsum[at] + (home[0] if d == 0 else homes[d, 0])

    vt[...] = vsum[...].astype(BF16)
    p.greet(near=False, rep=hop, cross=True)
    base = p.slot(nx)
    more = p.slot(nx)
    kvw = vt.shape[1]
    cols = [pl.ds(h * (kvw // 2), kvw // 2) for h in range(2)]
    sent = [
        [
            p.send(
                vt.at[:, cols[h]], vt4.at[p.x, :, cols[h]],
                p.at(p.xs(d), p.z, p.y), (base, more)[h] + d,
            )
            for d in range(1, nx)
        ]
        for h in range(2)
    ]
    vt4[p.x] = vt[...]
    ksum[...] = ktot[...] + ba[...].astype(F32) + bb[...].astype(F32)

    @pl.when(p.me == 0)
    def _():
        cut = home.shape[1]
        for d in range(2 * nx):
            at = pl.ds(d * cut, cut)
            ksum[at] = ksum[at] + (home[1] if d == 0 else homes[d, 1])

    kg[...] = ksum[...].astype(BF16)
    half = nz // 2
    right = p.at(p.x, p.zs(1), p.y)
    left = p.at(p.x, p.zs(-1), p.y)
    rslot, lslot = p.slot(4 * half), p.slot(4 * half)
    fslot, gslot = p.slot(8), p.slot(8)
    hops = {}

    def contribute(block, h):
        rows = tt[:, :, pl.ds(pl.multiple_of(block * deep, deep), deep)]
        rows = rows.reshape(nx * BLOCK_TOKENS, deep)
        grads = vt4[:, :, cols[h]].reshape(nx * BLOCK_TOKENS, kvw // 2)
        whole = (mm(rows, grads, TN) * scale).reshape(2, deep // 2, kvw // 2)
        own[block, :, :, cols[h]] = whole

    def ring(s, h):
        for k in range(2):
            for side, (first, to) in enumerate(((rslot, right), (lslot, left))):
                block = p.zs(half - s) if side == 0 else p.zs(s - half)
                if s == 0 and k != side:
                    continue
                acc = own[block, k, :, cols[h]]
                if (side, s - 1, k, h) in hops:
                    hops[side, s - 1, k, h].wait_recv()
                    acc = acc + drecv[side, s - 1, k, :, cols[h]].astype(F32)
                dsend[side, s, k, :, cols[h]] = acc.astype(BF16)
                piece = dsend.at[side, s, k, :, cols[h]]
                if s == half - 1:
                    done = p.copy(
                        piece, fin.at[side, p.y, :, cols[h]],
                        p.at(p.x, p.zs(1 - 2 * side), k),
                        fslot + 4 * h + 2 * side + k, gslot + 4 * h + 2 * side + p.y,
                    )
                    done.start()
                    p.started.append(done)
                    continue
                hops[side, s, k, h] = p.send(
                    piece, drecv.at[side, s, k, :, cols[h]], to, first + 4 * s + 2 * h + k
                )

    ibase = p.slot(nx)
    here = pl.ds(pl.multiple_of(p.x * width, width), width)
    backs = []

    def back_of(to):
        whole = wk[...].reshape(width, wk.shape[2])
        return (mm(vt4[to], whole, NT) * scale).astype(BF16)

    def send_back(d):
        to = p.xs(d)
        igs[to] = back_of(to)
        backs.append(p.send(igs.at[to], ig.at[:, here], p.at(to, p.z, p.y), ibase + d))

    for h in range(2):
        for made in sent[h]:
            made.wait_recv()
        contribute(p.zs(half), h)
        ring(0, h)
        for d in range(half - 1, 0, -1):
            contribute(p.zs(d), h)
            contribute(p.zs(-d), h)
    contribute(p.z, 0)
    contribute(p.z, 1)
    ys[...] = own[p.z, 1 - p.y].astype(BF16)
    yc = p.send(ys, yr, p.at(p.x, p.z, 1 - p.y), p.slot())
    waiting = list(range(1, nx))
    for s in range(1, half):
        for h in range(2):
            ring(s, h)
        if waiting:
            send_back(waiting.pop())
    while waiting:
        send_back(waiting.pop())
    ig[:, here] = back_of(p.x)
    yc.wait_recv()
    acc = own[p.z, p.y] + yr[...].astype(F32)
    for side in range(2):
        for y in range(2):
            for h in range(2):
                at = gslot + 4 * h + 2 * side + y
                part = fin.at[side, y, :, cols[h]]
                p.copy(part, part, right, at, at).wait_recv()
            acc = acc + fin[side, y].astype(F32)
    updated = weight[...] - LEARN_RATE * acc
    us[...] = updated.astype(BF16)
    reps = lax.axis_size("rep")
    rc = p.send(us, ur, lax.rem(lax.axis_index("rep") + hop, reps), p.slot(), axis="rep")
    rc.wait_recv()
    nw[...] = 0.5 * (updated + ur[...].astype(F32))
    for made in backs:
        made.wait_recv()
    p.drain()


VM = pl.BlockSpec(memory_space=pltpu.VMEM)


def sems(count):
    return [pltpu.SemaphoreType.DMA((count,)), pltpu.SemaphoreType.DMA((count,))]


def params(which, mib=60):
    return pltpu.CompilerParams(
        collective_id=which, has_side_effects=True, vmem_limit_bytes=mib * 2**20
    )


def sds(shape, dtype):
    return jax.ShapeDtypeStruct(shape, dtype)


def swap_kernel(n, c, signs, hop, *refs):
    count = (len(refs) - 4) // 2
    given, home = refs[:count], refs[count]
    taken, homes = refs[count + 1: 2 * count + 1], refs[2 * count + 1]
    send_sem, recv_sem = refs[2 * count + 2:]
    nx, nz = grid_of(n)
    me = lax.axis_index("seq")
    piece = me // (2 * nz) * 2 + lax.rem(me, 2)
    base = lax.rem(me // 2, nz) == 0
    peers = [{"seq": lax.rem(me + d + n, n)} for d in (c, -c, c + 1, -c - 1)]
    targets = []
    for sign in signs:
        targets += [peers[0], peers[3]] if sign > 0 else [peers[1], peers[2]]
    if hop:
        reps = lax.axis_size("rep")
        rep = lax.axis_index("rep")
        peers += [{"rep": lax.rem(rep + d, reps)} for d in (hop, reps - hop)]
        targets.append(peers[4])
    barrier = pltpu.get_barrier_semaphore()
    for peer in peers:
        pl.semaphore_signal(barrier, inc=1, device_id=peer, device_id_type=MESH)

    @pl.when(me == 0)
    def _():
        @pl.loop(1, 2 * nx)
        def _(i):
            to = i // 2 * (2 * nz) + lax.rem(i, 2)
            pl.semaphore_signal(barrier, inc=1, device_id={"seq": to}, device_id_type=MESH)

    @pl.when(base & (me != 0))
    def _():
        pl.semaphore_signal(barrier, inc=1, device_id={"seq": 0}, device_id_type=MESH)

    more = jnp.where(me == 0, 2 * nx - 1, jnp.where(base, 1, 0))
    pl.semaphore_wait(barrier, len(peers) + more)
    made = []
    for i in range(count):
        made.append(
            pltpu.make_async_remote_copy(
                src_ref=given[i], dst_ref=taken[i],
                send_sem=send_sem.at[i], recv_sem=recv_sem.at[i],
                device_id=targets[i], device_id_type=MESH,
            )
        )
        made[-1].start()

    def last(d):
        return pltpu.make_async_remote_copy(
            src_ref=home, dst_ref=homes.at[d],
            send_sem=send_sem.at[count + d], recv_sem=recv_sem.at[count + d],
            device_id={"seq": 0}, device_id_type=MESH,
        )

    @pl.when(base & (me != 0))
    def _():
        last(piece).start()

    for copy in made:
        copy.wait()

    @pl.when(base & (me != 0))
    def _():
        last(piece).wait_send()

    @pl.when(me == 0)
    def _():
        @pl.loop(1, 2 * nx)
        def _(i):
            last(i).wait_recv()


def out_kernel(n, c, signs, *refs):
    count = (len(refs) - 2) // 2
    given, taken = refs[:count], refs[count: 2 * count]
    send_sem, recv_sem = refs[2 * count:]
    me = lax.axis_index("seq")
    peers = [{"seq": lax.rem(me + d + n, n)} for d in (c, -c, c + 1, -c - 1)]
    targets = []
    for sign in signs:
        targets += [peers[0], peers[3]] if sign > 0 else [peers[1], peers[2]]
    barrier = pltpu.get_barrier_semaphore()
    for peer in peers:
        pl.semaphore_signal(barrier, inc=1, device_id=peer, device_id_type=MESH)
    pl.semaphore_wait(barrier, len(peers))
    made = [
        pltpu.make_async_remote_copy(
            src_ref=given[i], dst_ref=taken[i],
            send_sem=send_sem.at[i], recv_sem=recv_sem.at[i],
            device_id=targets[i], device_id_type=MESH,
        )
        for i in range(count)
    ]
    for copy in made:
        copy.start()
    for copy in made:
        copy.wait()


def swap(arrays, signs, shift, n, first_id, hop=0, home=None):
    anywhere = pl.BlockSpec(memory_space=pl.ANY)
    given = list(arrays)
    taken = [sds(a.shape, a.dtype) for a in arrays]
    spare = 0
    if home is not None:
        spare = 2 * grid_of(n)[0]
        given.append(home)
        taken.append(sds((spare, *home.shape), home.dtype))

    def branch(c):
        if home is None:
            body = functools.partial(out_kernel, n, c, signs)
        else:
            body = functools.partial(swap_kernel, n, c, signs, hop)
        return pl.pallas_call(
            body,
            out_shape=tuple(taken),
            in_specs=[anywhere] * len(given),
            out_specs=(anywhere,) * len(taken),
            scratch_shapes=sems(len(arrays) + spare),
            compiler_params=pltpu.CompilerParams(
                collective_id=first_id + c, has_side_effects=True
            ),
            name=f"swap_{c}",
        )

    return lax.switch(shift - 1, [branch(c) for c in range(1, n // 2)], *given)


def shards(inputs, queries, key_heads, cotangent, value_weight, random_blocks):
    n = lax.axis_size("seq")
    nx, nz = grid_of(n)
    tokens, query, key = inputs[0], queries[0], key_heads[0]
    upstream, weight = cotangent[0], value_weight[0]
    rows, model = tokens.shape
    kvw = key.shape[1]
    qw = query.shape[1]
    deep = weight.shape[0]
    scale = model ** -0.5
    offset = lax.rem(n - random_blocks[0, 0], n)
    shift = jnp.minimum(offset, n - 1 - offset)
    block = sds((rows, kvw), BF16)
    total = sds((rows, kvw), F32)
    buffers = [pltpu.VMEM((rows, kvw), BF16)]
    home = sds((2, rows // nx // 2, kvw), F32)

    val, wk, tt, kn = pl.pallas_call(
        functools.partial(gather_kernel, n, scale),
        out_shape=(
            block,
            sds((2 * nz, deep, kvw), BF16),
            sds((nx, rows, model // nx), BF16),
            sds((3, rows, kvw), BF16),
        ),
        in_specs=[VM] * 3,
        out_specs=(VM,) * 4,
        scratch_shapes=[
            pltpu.VMEM((deep, kvw), BF16),
            pltpu.VMEM((nx, rows, kvw), BF16),
            pltpu.VMEM((nx, rows, kvw), BF16),
            *sems(72),
        ],
        compiler_params=params(0),
        name="gather",
    )(tokens, key, weight)

    ka, kb, va, vb = swap((key, key, val, val), (1, 1), shift, n, 3)

    wide = (KV_HEADS, 6, rows, GROUP * rows)
    dq, vtot, ktot, dva, dvb, dka, dkb, r3 = pl.pallas_call(
        functools.partial(attend_kernel, n),
        out_shape=(sds((rows, qw), BF16), total, total, block, block, block, block, home),
        in_specs=[VM] * 9,
        out_specs=(VM,) * 8,
        scratch_shapes=[
            pltpu.VMEM((6, rows, kvw), BF16),
            pltpu.VMEM((6, rows, kvw), BF16),
            pltpu.VMEM((KV_HEADS, GROUP * rows, HD), BF16),
            pltpu.VMEM((KV_HEADS, GROUP * rows, HD), BF16),
            pltpu.VMEM(wide[1:], F32),
            pltpu.VMEM(wide, BF16),
            pltpu.VMEM(wide, F32),
            pltpu.VMEM((KV_HEADS, 1, GROUP * rows), F32),
            pltpu.VMEM((KV_HEADS, 3, rows, GROUP * rows), BF16),
            *buffers * 10,
            *collect_scratch(nx, nz, rows, kvw) * 2,
            *sems(80),
        ],
        compiler_params=params(1),
        name="attend",
    )(query, upstream, key, kn, ka, kb, val, va, vb)

    da, db, ba, bb, homes = swap(
        (dva, dvb, dka, dkb), (-1, -1), shift, n, 3 + n // 2, home=r3
    )
    reps = lax.axis_size("rep")
    hop = 2 ** (STEP % (reps.bit_length() - 1))
    input_grad, new_weight, key_grad = pl.pallas_call(
        functools.partial(update_kernel, n, hop, scale),
        out_shape=(sds((rows, model), BF16), sds((deep, kvw), F32), block),
        in_specs=[VM] * 11,
        out_specs=(VM,) * 3,
        scratch_shapes=[
            pltpu.VMEM((rows, kvw), F32),
            pltpu.VMEM((rows, kvw), F32),
            pltpu.VMEM((rows, kvw), BF16),
            pltpu.VMEM((nx, rows, kvw), BF16),
            pltpu.VMEM((nx, rows, model // nx), BF16),
            pltpu.VMEM((2, nz // 2, 2, deep, kvw), BF16),
            pltpu.VMEM((2, nz // 2, 2, deep, kvw), BF16),
            pltpu.VMEM((2, 2, deep, kvw), BF16),
            pltpu.VMEM((nz, 2, deep, kvw), F32),
            *[pltpu.VMEM((deep, kvw), BF16)] * 4,
            *sems(72),
        ],
        compiler_params=params(2),
        name="update",
    )(vtot, da, db, ktot, ba, bb, r3, homes, tt, wk, weight)
    return input_grad[None], dq[None], key_grad[None], new_weight[None]


def solution(mesh):
    p3 = P("rep", "seq", None)
    return jax.shard_map(
        shards,
        mesh=mesh,
        in_specs=(p3,) * 5 + (P(),),
        out_specs=(p3,) * 4,
        check_vma=False,
    )
```

```python
import functools
import jax
import jax.numpy as jnp
from jax import lax
from jax.experimental import pallas as pl
from jax.experimental.pallas import tpu as pltpu
from jax.sharding import PartitionSpec as P

HEADS = 16
KV_HEADS = 4
HD = 128
BLOCK_TOKENS = 128
STEP = 4
LEARN_RATE = 2.0
MASKED = -1e30
GROUP = HEADS // KV_HEADS
MESH = pl.DeviceIdType.MESH
F32 = jnp.float32
BF16 = jnp.bfloat16


def grid_of(n):
    return {64: (4, 8), 16: (2, 4), 8: (2, 2)}[n]


class Place:
    def __init__(self, n, send_sem, recv_sem):
        self.n = n
        self.nx, self.nz = grid_of(n)
        self.me = lax.axis_index("seq")
        self.x = self.me // (2 * self.nz)
        self.z = lax.rem(self.me // 2, self.nz)
        self.y = lax.rem(self.me, 2)
        self.send_sem, self.recv_sem = send_sem, recv_sem
        self.taken = 0
        self.started = []

    def at(self, x, z, y):
        return x * (2 * self.nz) + z * 2 + y

    def xs(self, d):
        return lax.rem(self.x + d + self.nx, self.nx)

    def zs(self, d):
        return lax.rem(self.z + d + self.nz, self.nz)

    def plane(self, sign=1):
        out = []
        for i in range(1, 2 * self.nx):
            y = self.y if i % 2 == 0 else 1 - self.y
            out.append((i, self.xs(sign * (i // 2)), y))
        return out

    def slot(self, count=1):
        first = self.taken
        self.taken += count
        return first

    def copy(self, src, dst, target, slot, recv_slot=None, axis="seq"):
        return pltpu.make_async_remote_copy(
            src_ref=src,
            dst_ref=dst,
            send_sem=self.send_sem.at[slot],
            recv_sem=self.recv_sem.at[slot if recv_slot is None else recv_slot],
            device_id={axis: target},
            device_id_type=MESH,
        )

    def send(self, src, dst, target, slot, axis="seq"):
        made = self.copy(src, dst, target, slot, axis=axis)
        made.start()
        self.started.append(made)
        return made

    def drain(self):
        for made in self.started:
            made.wait_send()
        self.started = []

    def greet(self, near=True, rep=False, first=False, cross=False):
        barrier = pltpu.get_barrier_semaphore()
        peers = [{"seq": self.at(x, self.z, y)} for _, x, y in self.plane()]
        peers += [{"seq": self.at(self.x, self.zs(d), self.y)} for d in range(1, self.nz)]
        if cross:
            peers += [{"seq": self.at(self.x, self.zs(d), 1 - self.y)} for d in (1, -1)]
        if near:
            peers += [{"seq": lax.rem(self.me + d, self.n)} for d in (1, self.n - 1)]
        if rep:
            reps = lax.axis_size("rep")
            here = lax.axis_index("rep")
            peers += [{"rep": lax.rem(here + d, reps)} for d in (rep, reps - rep)]
        for peer in peers:
            pl.semaphore_signal(barrier, inc=1, device_id=peer, device_id_type=MESH)
        if first:
            @pl.when(self.me == 0)
            def _():
                for p in range(1, 2 * self.nx):
                    pl.semaphore_signal(
                        barrier, inc=1, device_id={"seq": self.at(p // 2, 0, p % 2)},
                        device_id_type=MESH,
                    )

            @pl.when((self.z == 0) & (self.me != 0))
            def _():
                pl.semaphore_signal(barrier, inc=1, device_id={"seq": 0}, device_id_type=MESH)

        count = len(peers)
        if first:
            more = jnp.where(self.z == 0, 1, 0)
            count = count + jnp.where(self.me == 0, 2 * self.nx - 1, more)
        pl.semaphore_wait(barrier, count)


class Spread:
    def __init__(self, pl_, src, dst):
        self.p, self.src, self.dst = pl_, src, dst
        p = pl_
        self.rows = src.shape[0] // (2 * p.nx)
        self.piece = p.x * 2 + p.y
        self.a = p.slot(2 * p.nx)
        self.b = p.slot(p.nz)
        self.c = p.slot(2 * p.nx)

    def cut(self, ref, index, rows=None):
        rows = rows or self.rows
        return ref.at[pl.ds(pl.multiple_of(index * rows, rows), rows)]

    def one(self, p):
        first = []
        for i in range(1, 2 * p.nx):
            first.append(
                p.copy(
                    self.src.at[pl.ds(i * self.rows, self.rows)],
                    self.dst.at[pl.ds(i * self.rows, self.rows)],
                    p.at(i // 2, 0, i % 2), self.a + i, self.a,
                )
            )

        @pl.when(p.me == 0)
        def _():
            for made in first:
                made.start()
            self.dst[pl.ds(0, self.rows)] = self.src[pl.ds(0, self.rows)]
        self.first = first

    def two(self, p):
        mine = self.cut(self.dst, self.piece)
        second = [
            p.copy(mine, mine, p.at(p.x, d, p.y), self.b + d, self.b) for d in range(1, p.nz)
        ]

        @pl.when((p.z == 0) & (p.me != 0))
        def _():
            self.first[0].wait_recv()

        @pl.when(p.z == 0)
        def _():
            for made in second:
                made.start()
        self.second = second

    def three(self, p):
        mine = self.cut(self.dst, self.piece)

        @pl.when(p.z != 0)
        def _():
            self.second[0].wait_recv()
        self.third = [
            p.send(mine, mine, p.at(x, p.z, y), self.c + i) for i, x, y in p.plane()
        ]

    def end(self, p):
        for made in self.third:
            made.wait_recv()

        @pl.when(p.me == 0)
        def _():
            for made in self.first:
                made.wait_send()

        @pl.when(p.z == 0)
        def _():
            for made in self.second:
                made.wait_send()


class Collect:
    def __init__(self, p, given, c):
        self.p, self.given = p, given
        self.g1, self.r2, self.g3, self.r3 = c
        self.cut = given.shape[0] // (2 * p.nx)
        self.a = p.slot(2 * p.nx)
        self.c = p.slot(p.nz)

    def part(self, x, y):
        return pl.ds(pl.multiple_of((x * 2 + y) * self.cut, self.cut), self.cut)

    def one(self, p):
        self.first = [
            p.send(
                self.given.at[self.part(x, y)], self.g1.at[p.x * 2 + p.y],
                p.at(x, p.z, y), self.a + i,
            )
            for i, x, y in p.plane()
        ]

    def up(self, d):
        return self.p.copy(self.r2, self.g3.at[d], self.p.at(self.p.x, 0, self.p.y), self.c + d)

    def two(self, p):
        acc = self.given[self.part(p.x, p.y)].astype(F32)
        for made, (_, x, y) in zip(self.first, p.plane(-1)):
            made.wait_recv()
            acc = acc + self.g1[x * 2 + y].astype(F32)
        self.r3[...] = acc
        self.r2[...] = acc.astype(BF16)
        self.third = self.up(p.z)

        @pl.when(p.z != 0)
        def _():
            self.third.start()

    def three(self, p):
        @pl.when(p.z == 0)
        def _():
            tally = self.r3[...]
            for d in range(1, p.nz):
                self.up(d).wait_recv()
                tally = tally + self.g3[d].astype(F32)
            self.r3[...] = tally

        @pl.when(p.z != 0)
        def _():
            self.third.wait_send()


def collect_scratch(nx, nz, rows, kvw):
    cut = rows // nx // 2
    return [
        pltpu.VMEM((2 * nx, cut, kvw), BF16),
        pltpu.VMEM((cut, kvw), BF16),
        pltpu.VMEM((nz, cut, kvw), BF16),
    ]


NT = (((1,), (1,)), ((), ()))
TN = (((0,), (0,)), ((), ()))
NN = (((1,), (0,)), ((), ()))


def mm(a, b, dims):
    return lax.dot_general(a, b, dims, preferred_element_type=F32)


def lanes(g):
    return pl.ds(pl.multiple_of(g * HD, HD), HD)


def gather_kernel(
    n, scale, tok, key, weight_f32, val, wk, tt, kn,
    wl, pbuf, rbuf, send_sem, recv_sem,
):
    p = Place(n, send_sem, recv_sem)
    nx, nz = p.nx, p.nz
    width = tok.shape[1] // nx
    half = nz // 2
    wl[...] = weight_f32[...].astype(BF16)
    p.greet(first=True)

    right = p.at(p.x, p.zs(1), p.y)
    left = p.at(p.x, p.zs(-1), p.y)
    after = lax.rem(p.me + 1, n)
    before = lax.rem(p.me + n - 1, n)

    def shard(dz, k):
        return p.zs(dz) * 2 + (p.y if k == 0 else 1 - p.y)

    rs = [[p.slot() for _ in range(2)] for _ in range(half)]
    ls = [[p.slot() for _ in range(2)] for _ in range(half)]
    hops_r = [[None, None] for _ in range(half)]
    hops_l = [[None, None] for _ in range(half)]

    def relay(s, k):
        src_r = wl if (s == 0 and k == 0) else wk.at[shard(-s, k)]
        src_l = wl if (s == 0 and k == 0) else wk.at[shard(s, k)]
        if s < half - 1 or k == 0:
            hops_r[s][k] = p.send(src_r, wk.at[shard(-s, k)], right, rs[s][k])
        if s < half - 1 or k == 1:
            hops_l[s][k] = p.send(src_l, wk.at[shard(s, k)], left, ls[s][k])

    def arrived(s):
        for k in range(2):
            for hops in (hops_r, hops_l):
                if hops[s][k] is not None:
                    hops[s][k].wait_recv()
            if s + 1 < half:
                relay(s + 1, k)

    keys0 = Spread(p, key, kn.at[2])
    keys0.one(p)
    other = p.send(wl, wk.at[shard(0, 0)], p.at(p.x, p.z, 1 - p.y), p.slot())
    relay(0, 0)
    key_right = p.send(key, kn.at[0], after, p.slot())
    key_left = p.send(key, kn.at[1], before, p.slot())
    cols = [p.slot() for _ in range(nx)]
    moved = []
    for d in range(1, nx):
        to = p.xs(d)
        part = tok.at[:, pl.ds(pl.multiple_of(to * width, width), width)]
        moved.append(p.send(part, tt.at[p.x], p.at(to, p.z, p.y), cols[d]))
    wk[shard(0, 0)] = wl[...]
    tt[p.x] = tok[:, pl.ds(pl.multiple_of(p.x * width, width), width)]
    other.wait_recv()
    relay(0, 1)
    for s in range(half - 1):
        arrived(s)
        if s == max(half - 3, 0):
            keys0.two(p)
    keys0.three(p)
    arrived(half - 1)
    for made in moved:
        made.wait_recv()
    weight = wk[...].reshape(2 * nz * wk.shape[1], wk.shape[2])
    sums = [p.slot() for _ in range(nx)]
    parts = []
    for d in range(1, nx):
        to = p.xs(d)
        part = jnp.dot(tt[to], weight, preferred_element_type=F32) * scale
        pbuf[to] = part.astype(BF16)
        parts.append(p.send(pbuf.at[to], rbuf.at[p.x], p.at(to, p.z, p.y), sums[d]))
    pown = jnp.dot(tt[p.x], weight, preferred_element_type=F32) * scale
    keys0.end(p)
    key_right.wait_recv()
    key_left.wait_recv()
    for d in range(1, nx):
        parts[d - 1].wait_recv()
        pown = pown + rbuf[p.xs(-d)].astype(F32)
    val[...] = pown.astype(BF16)
    p.drain()


def attend_kernel(
    n, q, cot, key, kn, ka, kb, val, va, vb,
    dq, vtot, ktot, dva, dvb, dka, dkb, r3,
    ks, vs, qs, cs, sc, low, gw, delta, dsb,
    vout_l, vout_r, vout_g, vin_l, vin_r, kout_l, kout_r, kout_g, kin_l, kin_r,
    c1, c2, c3, d1, d2, d3, send_sem, recv_sem,
):
    p = Place(n, send_sem, recv_sem)
    nx, nz = p.nx, p.nz
    after = lax.rem(p.me + 1, n)
    before = lax.rem(p.me + n - 1, n)
    p.greet(first=True)
    vals0 = Spread(p, val, vs.at[3])
    vals0.one(p)
    val_right = p.send(val, vs.at[0], after, p.slot())
    val_left = p.send(val, vs.at[2], before, p.slot())
    for s, (kr, vr) in {1: (key, val), 4: (ka, va), 5: (kb, vb)}.items():
        ks[s] = kr[...]
        vs[s] = vr[...]
    ks[0] = kn[0]
    ks[2] = kn[1]
    ks[3] = kn[2]
    for g in range(KV_HEADS):
        for r in range(GROUP):
            at = pl.ds((g * GROUP + r) * HD, HD)
            to = pl.ds(r * BLOCK_TOKENS, BLOCK_TOKENS)
            qs[g, to] = q[:, at]
            cs[g, to] = cot[:, at]
    score = HD ** -0.5
    first_ok = jnp.where(p.me == 0, MASKED, 0.0)
    last_ok = jnp.where(p.me == n - 1, MASKED, 0.0)

    def groups(body, first=0, last=KV_HEADS):
        lax.fori_loop(first, last, body, 0)

    def soften(g, _):
        high = None
        for s in range(6):
            t = mm(ks[s, :, lanes(g)], qs[g], NT) * score
            if s == 0:
                t = t + first_ok
            if s == 2:
                t = t + last_ok
            sc[s] = t
            m = jnp.max(t, axis=0, keepdims=True)
            high = m if high is None else jnp.maximum(high, m)
        total = None
        for s in range(6):
            e = jnp.exp(sc[s] - high)
            sc[s] = e
            m = jnp.sum(e, axis=0, keepdims=True)
            total = m if total is None else total + m
        inv = 1.0 / total
        for s in range(6):
            w = (sc[s] * inv).astype(BF16)
            low[g, s] = w
            if s in (0, 2, 3):
                to = {0: vout_l, 2: vout_r, 3: vout_g}[s]
                to[:, lanes(g)] = mm(w, cs[g], NN).astype(BF16)
        return 0

    def others(g, _):
        vtot[:, lanes(g)] = mm(low[g, 1], cs[g], NN)
        dva[:, lanes(g)] = mm(low[g, 4], cs[g], NN).astype(BF16)
        dvb[:, lanes(g)] = mm(low[g, 5], cs[g], NN).astype(BF16)
        return 0

    delta[...] = jnp.zeros(delta.shape, F32)

    def grade(s):
        def body(g, _):
            t = mm(vs[s, :, lanes(g)], cs[g], NT)
            gw[g, s] = t
            delta[g] = delta[g] + jnp.sum(low[g, s].astype(F32) * t, axis=0, keepdims=True)
            return 0
        groups(body)

    groups(soften, 0, 2)
    vals0.two(p)
    groups(soften, 2)
    sums_v = Collect(p, vout_g, (c1, c2, c3, r3.at[0]))
    sums_v.one(p)
    v_left = p.send(vout_l, vin_r, before, p.slot())
    v_right = p.send(vout_r, vin_l, after, p.slot())
    vals0.three(p)
    grade(1)
    grade(4)
    grade(5)
    val_right.wait_recv()
    grade(0)
    val_left.wait_recv()
    grade(2)
    vals0.end(p)
    grade(3)
    ahead = (3, 0, 2)

    def signal(g, s):
        return (low[g, s].astype(F32) * (gw[g, s] - delta[g]) * score).astype(BF16)

    def group_ahead(slots, g, _):
        for s in slots:
            i = ahead.index(s)
            ds = signal(g, s)
            dsb[g, i] = ds
            to = {0: kout_l, 2: kout_r, 3: kout_g}[s]
            to[:, lanes(g)] = mm(ds, qs[g], NN).astype(BF16)
        return 0

    def group(g, _):
        back = None
        for s in range(6):
            if s in ahead:
                ds = dsb[g, ahead.index(s)]
            else:
                ds = signal(g, s)
                dk = mm(ds, qs[g], NN)
                if s == 1:
                    ktot[:, lanes(g)] = dk
                else:
                    to = {4: dka, 5: dkb}[s]
                    to[:, lanes(g)] = dk.astype(BF16)
            part = mm(ks[s, :, lanes(g)], ds, TN)
            back = part if back is None else back + part
        for r in range(GROUP):
            piece = back[:, r * BLOCK_TOKENS:(r + 1) * BLOCK_TOKENS]
            dq[:, lanes(g * GROUP + r)] = piece.T.astype(BF16)
        return 0

    groups(functools.partial(group_ahead, (3,)))
    sums_k = Collect(p, kout_g, (d1, d2, d3, r3.at[1]))
    sums_k.one(p)
    groups(functools.partial(group_ahead, (0, 2)))
    k_left = p.send(kout_l, kin_r, before, p.slot())
    k_right = p.send(kout_r, kin_l, after, p.slot())
    sums_v.two(p)
    groups(group, 0, 2)
    sums_k.two(p)
    groups(others)
    groups(group, 2)
    for made in (v_left, v_right, k_left, k_right):
        made.wait_recv()
    vtot[...] = vtot[...] + vin_l[...].astype(F32) + vin_r[...].astype(F32)
    ktot[...] = ktot[...] + kin_l[...].astype(F32) + kin_r[...].astype(F32)
    sums_v.three(p)
    sums_k.three(p)
    p.drain()


def update_kernel(
    n, hop, scale, vtot, da, db, ktot, ba, bb, home, homes, tt, wk, weight, ig, nw, kg,
    vsum, ksum, vt, vt4, igs, dsend, drecv, fin, own, ys, yr, us, ur, send_sem, recv_sem,
):
    p = Place(n, send_sem, recv_sem)
    nx, nz = p.nx, p.nz
    width = tt.shape[2]
    deep = width // nz
    vsum[...] = vtot[...] + da[...].astype(F32) + db[...].astype(F32)

    @pl.when(p.me == 0)
    def _():
        cut = home.shape[1]
        for d in range(2 * nx):
            at = pl.ds(d * cut, cut)
            vsum[at] = vsum[at] + (home[0] if d == 0 else homes[d, 0])

    vt[...] = vsum[...].astype(BF16)
    p.greet(near=False, rep=hop, cross=True)
    base = p.slot(nx)
    more = p.slot(nx)
    kvw = vt.shape[1]
    cols = [pl.ds(h * (kvw // 2), kvw // 2) for h in range(2)]
    sent = [
        [
            p.send(
                vt.at[:, cols[h]], vt4.at[p.x, :, cols[h]],
                p.at(p.xs(d), p.z, p.y), (base, more)[h] + d,
            )
            for d in range(1, nx)
        ]
        for h in range(2)
    ]
    vt4[p.x] = vt[...]
    ksum[...] = ktot[...] + ba[...].astype(F32) + bb[...].astype(F32)

    @pl.when(p.me == 0)
    def _():
        cut = home.shape[1]
        for d in range(2 * nx):
            at = pl.ds(d * cut, cut)
            ksum[at] = ksum[at] + (home[1] if d == 0 else homes[d, 1])

    kg[...] = ksum[...].astype(BF16)
    half = nz // 2
    right = p.at(p.x, p.zs(1), p.y)
    left = p.at(p.x, p.zs(-1), p.y)
    rslot, lslot = p.slot(4 * half), p.slot(4 * half)
    fslot, gslot = p.slot(8), p.slot(8)
    hops = {}

    def contribute(block, h):
        rows = tt[:, :, pl.ds(pl.multiple_of(block * deep, deep), deep)]
        rows = rows.reshape(nx * BLOCK_TOKENS, deep)
        grads = vt4[:, :, cols[h]].reshape(nx * BLOCK_TOKENS, kvw // 2)
        whole = (mm(rows, grads, TN) * scale).reshape(2, deep // 2, kvw // 2)
        own[block, :, :, cols[h]] = whole

    def ring(s, h):
        for k in range(2):
            for side, (first, to) in enumerate(((rslot, right), (lslot, left))):
                block = p.zs(half - s) if side == 0 else p.zs(s - half)
                if s == 0 and k != side:
                    continue
                acc = own[block, k, :, cols[h]]
                if (side, s - 1, k, h) in hops:
                    hops[side, s - 1, k, h].wait_recv()
                    acc = acc + drecv[side, s - 1, k, :, cols[h]].astype(F32)
                dsend[side, s, k, :, cols[h]] = acc.astype(BF16)
                piece = dsend.at[side, s, k, :, cols[h]]
                if s == half - 1:
                    done = p.copy(
                        piece, fin.at[side, p.y, :, cols[h]],
                        p.at(p.x, p.zs(1 - 2 * side), k),
                        fslot + 4 * h + 2 * side + k, gslot + 4 * h + 2 * side + p.y,
                    )
                    done.start()
                    p.started.append(done)
                    continue
                hops[side, s, k, h] = p.send(
                    piece, drecv.at[side, s, k, :, cols[h]], to, first + 4 * s + 2 * h + k
                )

    ibase = p.slot(nx)
    here = pl.ds(pl.multiple_of(p.x * width, width), width)
    backs = []

    def back_of(to):
        whole = wk[...].reshape(width, wk.shape[2])
        return (mm(vt4[to], whole, NT) * scale).astype(BF16)

    def send_back(d):
        to = p.xs(d)
        igs[to] = back_of(to)
        backs.append(p.send(igs.at[to], ig.at[:, here], p.at(to, p.z, p.y), ibase + d))

    for h in range(2):
        for made in sent[h]:
            made.wait_recv()
        contribute(p.zs(half), h)
        ring(0, h)
        for d in range(half - 1, 0, -1):
            contribute(p.zs(d), h)
            contribute(p.zs(-d), h)
    waiting = list(range(1, nx))
    for s in range(1, half):
        for h in range(2):
            ring(s, h)
        if s == 1:
            contribute(p.z, 0)
            contribute(p.z, 1)
            ys[...] = own[p.z, 1 - p.y].astype(BF16)
            yc = p.send(ys, yr, p.at(p.x, p.z, 1 - p.y), p.slot())
        elif waiting:
            send_back(waiting.pop())
    while waiting:
        send_back(waiting.pop())
    ig[:, here] = back_of(p.x)
    yc.wait_recv()
    acc = own[p.z, p.y] + yr[...].astype(F32)
    for side in range(2):
        for y in range(2):
            for h in range(2):
                at = gslot + 4 * h + 2 * side + y
                part = fin.at[side, y, :, cols[h]]
                p.copy(part, part, right, at, at).wait_recv()
            acc = acc + fin[side, y].astype(F32)
    updated = weight[...] - LEARN_RATE * acc
    us[...] = updated.astype(BF16)
    reps = lax.axis_size("rep")
    rc = p.send(us, ur, lax.rem(lax.axis_index("rep") + hop, reps), p.slot(), axis="rep")
    rc.wait_recv()
    nw[...] = 0.5 * (updated + ur[...].astype(F32))
    for made in backs:
        made.wait_recv()
    p.drain()


VM = pl.BlockSpec(memory_space=pltpu.VMEM)


def sems(count):
    return [pltpu.SemaphoreType.DMA((count,)), pltpu.SemaphoreType.DMA((count,))]


def params(which, mib=60):
    return pltpu.CompilerParams(
        collective_id=which, has_side_effects=True, vmem_limit_bytes=mib * 2**20
    )


def sds(shape, dtype):
    return jax.ShapeDtypeStruct(shape, dtype)


def swap_kernel(n, c, signs, hop, *refs):
    count = (len(refs) - 4) // 2
    given, home = refs[:count], refs[count]
    taken, homes = refs[count + 1: 2 * count + 1], refs[2 * count + 1]
    send_sem, recv_sem = refs[2 * count + 2:]
    nx, nz = grid_of(n)
    me = lax.axis_index("seq")
    piece = me // (2 * nz) * 2 + lax.rem(me, 2)
    base = lax.rem(me // 2, nz) == 0
    peers = [{"seq": lax.rem(me + d + n, n)} for d in (c, -c, c + 1, -c - 1)]
    targets = []
    for sign in signs:
        targets += [peers[0], peers[3]] if sign > 0 else [peers[1], peers[2]]
    if hop:
        reps = lax.axis_size("rep")
        rep = lax.axis_index("rep")
        peers += [{"rep": lax.rem(rep + d, reps)} for d in (hop, reps - hop)]
        targets.append(peers[4])
    barrier = pltpu.get_barrier_semaphore()
    for peer in peers:
        pl.semaphore_signal(barrier, inc=1, device_id=peer, device_id_type=MESH)

    @pl.when(me == 0)
    def _():
        @pl.loop(1, 2 * nx)
        def _(i):
            to = i // 2 * (2 * nz) + lax.rem(i, 2)
            pl.semaphore_signal(barrier, inc=1, device_id={"seq": to}, device_id_type=MESH)

    @pl.when(base & (me != 0))
    def _():
        pl.semaphore_signal(barrier, inc=1, device_id={"seq": 0}, device_id_type=MESH)

    more = jnp.where(me == 0, 2 * nx - 1, jnp.where(base, 1, 0))
    pl.semaphore_wait(barrier, len(peers) + more)
    made = []
    for i in range(count):
        made.append(
            pltpu.make_async_remote_copy(
                src_ref=given[i], dst_ref=taken[i],
                send_sem=send_sem.at[i], recv_sem=recv_sem.at[i],
                device_id=targets[i], device_id_type=MESH,
            )
        )
        made[-1].start()

    def last(d):
        return pltpu.make_async_remote_copy(
            src_ref=home, dst_ref=homes.at[d],
            send_sem=send_sem.at[count + d], recv_sem=recv_sem.at[count + d],
            device_id={"seq": 0}, device_id_type=MESH,
        )

    @pl.when(base & (me != 0))
    def _():
        last(piece).start()

    for copy in made:
        copy.wait()

    @pl.when(base & (me != 0))
    def _():
        last(piece).wait_send()

    @pl.when(me == 0)
    def _():
        @pl.loop(1, 2 * nx)
        def _(i):
            last(i).wait_recv()


def out_kernel(n, c, signs, *refs):
    count = (len(refs) - 2) // 2
    given, taken = refs[:count], refs[count: 2 * count]
    send_sem, recv_sem = refs[2 * count:]
    me = lax.axis_index("seq")
    peers = [{"seq": lax.rem(me + d + n, n)} for d in (c, -c, c + 1, -c - 1)]
    targets = []
    for sign in signs:
        targets += [peers[0], peers[3]] if sign > 0 else [peers[1], peers[2]]
    barrier = pltpu.get_barrier_semaphore()
    for peer in peers:
        pl.semaphore_signal(barrier, inc=1, device_id=peer, device_id_type=MESH)
    pl.semaphore_wait(barrier, len(peers))
    made = [
        pltpu.make_async_remote_copy(
            src_ref=given[i], dst_ref=taken[i],
            send_sem=send_sem.at[i], recv_sem=recv_sem.at[i],
            device_id=targets[i], device_id_type=MESH,
        )
        for i in range(count)
    ]
    for copy in made:
        copy.start()
    for copy in made:
        copy.wait()


def swap(arrays, signs, shift, n, first_id, hop=0, home=None):
    anywhere = pl.BlockSpec(memory_space=pl.ANY)
    given = list(arrays)
    taken = [sds(a.shape, a.dtype) for a in arrays]
    spare = 0
    if home is not None:
        spare = 2 * grid_of(n)[0]
        given.append(home)
        taken.append(sds((spare, *home.shape), home.dtype))

    def branch(c):
        if home is None:
            body = functools.partial(out_kernel, n, c, signs)
        else:
            body = functools.partial(swap_kernel, n, c, signs, hop)
        return pl.pallas_call(
            body,
            out_shape=tuple(taken),
            in_specs=[anywhere] * len(given),
            out_specs=(anywhere,) * len(taken),
            scratch_shapes=sems(len(arrays) + spare),
            compiler_params=pltpu.CompilerParams(
                collective_id=first_id + c, has_side_effects=True
            ),
            name=f"swap_{c}",
        )

    return lax.switch(shift - 1, [branch(c) for c in range(1, n // 2)], *given)


def shards(inputs, queries, key_heads, cotangent, value_weight, random_blocks):
    n = lax.axis_size("seq")
    nx, nz = grid_of(n)
    tokens, query, key = inputs[0], queries[0], key_heads[0]
    upstream, weight = cotangent[0], value_weight[0]
    rows, model = tokens.shape
    kvw = key.shape[1]
    qw = query.shape[1]
    deep = weight.shape[0]
    scale = model ** -0.5
    offset = lax.rem(n - random_blocks[0, 0], n)
    shift = jnp.minimum(offset, n - 1 - offset)
    block = sds((rows, kvw), BF16)
    total = sds((rows, kvw), F32)
    buffers = [pltpu.VMEM((rows, kvw), BF16)]
    home = sds((2, rows // nx // 2, kvw), F32)

    val, wk, tt, kn = pl.pallas_call(
        functools.partial(gather_kernel, n, scale),
        out_shape=(
            block,
            sds((2 * nz, deep, kvw), BF16),
            sds((nx, rows, model // nx), BF16),
            sds((3, rows, kvw), BF16),
        ),
        in_specs=[VM] * 3,
        out_specs=(VM,) * 4,
        scratch_shapes=[
            pltpu.VMEM((deep, kvw), BF16),
            pltpu.VMEM((nx, rows, kvw), BF16),
            pltpu.VMEM((nx, rows, kvw), BF16),
            *sems(72),
        ],
        compiler_params=params(0),
        name="gather",
    )(tokens, key, weight)

    ka, kb, va, vb = swap((key, key, val, val), (1, 1), shift, n, 3)

    wide = (KV_HEADS, 6, rows, GROUP * rows)
    dq, vtot, ktot, dva, dvb, dka, dkb, r3 = pl.pallas_call(
        functools.partial(attend_kernel, n),
        out_shape=(sds((rows, qw), BF16), total, total, block, block, block, block, home),
        in_specs=[VM] * 9,
        out_specs=(VM,) * 8,
        scratch_shapes=[
            pltpu.VMEM((6, rows, kvw), BF16),
            pltpu.VMEM((6, rows, kvw), BF16),
            pltpu.VMEM((KV_HEADS, GROUP * rows, HD), BF16),
            pltpu.VMEM((KV_HEADS, GROUP * rows, HD), BF16),
            pltpu.VMEM(wide[1:], F32),
            pltpu.VMEM(wide, BF16),
            pltpu.VMEM(wide, F32),
            pltpu.VMEM((KV_HEADS, 1, GROUP * rows), F32),
            pltpu.VMEM((KV_HEADS, 3, rows, GROUP * rows), BF16),
            *buffers * 10,
            *collect_scratch(nx, nz, rows, kvw) * 2,
            *sems(80),
        ],
        compiler_params=params(1),
        name="attend",
    )(query, upstream, key, kn, ka, kb, val, va, vb)

    da, db, ba, bb, homes = swap(
        (dva, dvb, dka, dkb), (-1, -1), shift, n, 3 + n // 2, home=r3
    )
    reps = lax.axis_size("rep")
    hop = 2 ** (STEP % (reps.bit_length() - 1))
    input_grad, new_weight, key_grad = pl.pallas_call(
        functools.partial(update_kernel, n, hop, scale),
        out_shape=(sds((rows, model), BF16), sds((deep, kvw), F32), block),
        in_specs=[VM] * 11,
        out_specs=(VM,) * 3,
        scratch_shapes=[
            pltpu.VMEM((rows, kvw), F32),
            pltpu.VMEM((rows, kvw), F32),
            pltpu.VMEM((rows, kvw), BF16),
            pltpu.VMEM((nx, rows, kvw), BF16),
            pltpu.VMEM((nx, rows, model // nx), BF16),
            pltpu.VMEM((2, nz // 2, 2, deep, kvw), BF16),
            pltpu.VMEM((2, nz // 2, 2, deep, kvw), BF16),
            pltpu.VMEM((2, 2, deep, kvw), BF16),
            pltpu.VMEM((nz, 2, deep, kvw), F32),
            *[pltpu.VMEM((deep, kvw), BF16)] * 4,
            *sems(72),
        ],
        compiler_params=params(2),
        name="update",
    )(vtot, da, db, ktot, ba, bb, r3, homes, tt, wk, weight)
    return input_grad[None], dq[None], key_grad[None], new_weight[None]


def solution(mesh):
    p3 = P("rep", "seq", None)
    return jax.shard_map(
        shards,
        mesh=mesh,
        in_specs=(p3,) * 5 + (P(),),
        out_specs=(p3,) * 4,
        check_vma=False,
    )
```
